32 devices in a mesh: groups: 2 (over y), seq: 8 (over z, x), chan: 2 (over core).
Axes of the slice: x: 2, y: 2, z: 4, core: 2. Of those that a mesh axis runs over, the one named last changes fastest.
Arguments:
- projected: bfloat16 [3, 2048, 1024], P(None, ('groups', 'seq'), 'chan'), parts along dimension 1, may hold values from -6 to 6
- long_filter: float32 [2048, 1024], P(('groups', 'seq'), 'chan'), parts along dimension 0, may hold values from -6 to 6
- short_kernel: float32 [3, 7, 1024], P(None, None, 'chan'), may hold values from -2 to 2
- skip_gain: float32 [1024], P('chan'), may hold values from 0.25 to 1.5
- cotangent: bfloat16 [2048, 1024], P(('groups', 'seq'), 'chan'), parts along dimension 0, may hold values from -6 to 6
Outputs:
- layer_output: bfloat16 [2048, 1024], P(('groups', 'seq'), 'chan'), parts along dimension 0
- stream_grads: bfloat16 [3, 2048, 1024], P(None, ('groups', 'seq'), 'chan'), parts along dimension 1
- filter_grad: float32 [2048, 1024], P(('groups', 'seq'), 'chan'), parts along dimension 0
- kernel_grad: float32 [6, 7, 1024], P('groups', None, 'chan'), parts along dimension 0
- skip_grad: float32 [2048], P(('groups', 'chan')), parts along dimension 0
The draws below stay inside these ranges and needn't reach their ends.
There are 2 independent parts, one for each index of `groups`. The reference program is written for one: setup_inputs(seed, part) draws one part's arguments, and reference() takes and returns one part's arrays. A program takes and returns all parts, laid end to end along the dimension named above; an argument that names none is the same for every part. Nothing has to cross between parts.
All inputs are finite; a program needn't handle non-finite values.
Results may differ from the reference program's by a relative error of at most 0.001.
Values may be sent and summed in bfloat16 or wider, within the bound.
A program may use at most 64 MiB of HBM per device.

```python
import math
import jax
import jax.numpy as jnp

D = 1024
TAPS = 7
TOKENS = 1024


def block_scale(stream_key, dims, pieces, low, high):
    loudness = 1.0
    for position, blocks in pieces:
        heights = jax.random.uniform(jax.random.fold_in(jax.random.fold_in(stream_key, 6), position), (blocks,), jnp.float32, low / len(pieces), high / len(pieces))
        loudness = loudness * jnp.repeat(jnp.exp(heights), dims[position] // blocks).reshape((-1,) + (1,) * (len(dims) - 1 - position))
    return loudness


def gaussian(key, shape, width, limit, shards=(), held_as=jnp.bfloat16):
    values = jax.random.normal(key, shape, jnp.float32) * width
    if len(shards) > 0:
        values = block_scale(key, shape, shards, -0.22, 0.18) * values
    return jnp.clip(values, min=-limit, max=limit).astype(held_as)


def setup_inputs(seed: int = 0, part: int = 0) -> dict:
    keys = jax.random.split(jax.random.key(seed), 6)
    own_keys = jax.random.split(jax.random.fold_in(keys[5], part), 6)
    projected = gaussian(own_keys[0], (3, TOKENS, D), 1.0, 6.0, ((1, 8), (2, 2)))
    long_filter = gaussian(own_keys[1], (TOKENS, D), 1.0, 6.0, ((0, 8), (1, 2)), jnp.float32)
    short_kernel = gaussian(keys[2], (3, TAPS, D), TAPS ** -0.5, 2.0, ((2, 2),), jnp.float32)
    skip_gain = jnp.clip(0.25 + 1.25 * jax.random.uniform(keys[3], (D,), jnp.float32) ** block_scale(keys[3], (D,), ((0, 2),), -0.2, 0.2), 0.25, 1.5)
    cotangent = gaussian(own_keys[4], (TOKENS, D), 1.0, 6.0, ((0, 8), (1, 2)))
    return {"projected": projected, "long_filter": long_filter, "short_kernel": short_kernel, "skip_gain": skip_gain, "cotangent": cotangent}


def circular_taps(streams, short_kernel):
    margin = short_kernel.shape[1] // 2
    summed = jnp.zeros(streams.shape, jnp.float32)
    for offset in range(short_kernel.shape[1]):
        summed = summed + short_kernel[:, offset][:, None, :] * jnp.roll(streams, margin - offset, axis=1)
    return summed

def long_layer(streams, long_filter, short_kernel, skip_gain):
    factor = 1.0 / math.sqrt(TOKENS)
    shorts = circular_taps(streams, short_kernel)
    gated_signal = shorts[1] * shorts[2]
    spectrum = jnp.fft.rfft(gated_signal, axis=0) * jnp.fft.rfft(long_filter * factor, axis=0)
    response = jnp.fft.irfft(spectrum, n=TOKENS, axis=0) + skip_gain * gated_signal
    return response * shorts[0]

def reference(projected, long_filter, short_kernel, skip_gain, cotangent):
    streams = projected.astype(jnp.float32)
    output, pullback = jax.vjp(long_layer, streams, long_filter, short_kernel, skip_gain)
    stream_part, filter_part, kernel_part, skip_part = pullback(cotangent.astype(jnp.float32))
    factor = 1.0 / math.sqrt(TOKENS)
    return (output.astype(jnp.bfloat16), stream_part.astype(jnp.bfloat16), filter_part, kernel_part * factor, skip_part * factor)
```

```python
import functools
import math

import jax
import jax.numpy as jnp
import numpy as np
from jax import lax
from jax.experimental import pallas as pl
from jax.experimental.pallas import tpu as pltpu
from jax.sharding import PartitionSpec as P

HIGHEST = lax.Precision.HIGHEST
LANES = 128
HALF = LANES // 2
RIM = 8
LIMIT = 64 * 1024 * 1024 - 1024 * 1024
BEND = 15.0
SPREAD = 251.0 * math.log(2.0) / math.log(1.0 + BEND)
LOWEST = -125.0 * math.log(2.0)
TINY = 1e-35


def turned(value, step, extent):
    real_part, imaginary = value
    step = step % extent
    if step == 0:
        return value
    if 2 * step == extent:
        return (-real_part, None if imaginary is None else -imaginary)
    if 4 * step == extent:
        return (None if imaginary is None else -imaginary, real_part)
    if 4 * step == 3 * extent:
        return (imaginary, -real_part)
    cosine = math.cos(2.0 * math.pi * step / extent)
    sine = math.sin(2.0 * math.pi * step / extent)
    if imaginary is None:
        return (real_part * cosine, real_part * sine)
    return (real_part * cosine - imaginary * sine, imaginary * cosine + real_part * sine)


def part_sum(left, right, sign):
    if right is None:
        return left
    if left is None:
        return right if sign > 0 else -right
    return left + right if sign > 0 else left - right


def real_spectrum(values):
    extent = len(values)
    if extent == 2:
        return [(values[0] + values[1], None), (values[0] - values[1], None)]
    even, odd = real_spectrum(values[0::2]), real_spectrum(values[1::2])
    half = extent // 2

    def entry(spectrum, index):
        index = index % half
        if 2 * index <= half:
            return spectrum[index]
        real_part, imaginary = spectrum[half - index]
        return (real_part, None if imaginary is None else -imaginary)

    found = []
    for index in range(half + 1):
        left, right = entry(even, index), turned(entry(odd, index), -index, extent)
        found.append((part_sum(left[0], right[0], 1), part_sum(left[1], right[1], 1)))
    return found


def real_values(spectrum):
    extent = 2 * (len(spectrum) - 1)
    if extent == 2:
        first, last = spectrum[0][0], spectrum[1][0]
        return [first + last, first - last]
    half = extent // 2
    even, odd = [], []
    for index in range(half // 2 + 1):
        real_part, imaginary = spectrum[index]
        if 2 * index == half:
            even.append((2.0 * real_part, None))
            odd.append((-2.0 * imaginary, None))
            continue
        other_real, other_imag = spectrum[half - index]
        even.append(
            (real_part + other_real, part_sum(imaginary, other_imag, -1))
        )
        odd.append(
            turned(
                (real_part - other_real, part_sum(imaginary, other_imag, 1)), index, extent
            )
        )
    found = [None] * extent
    found[0::2] = real_values(even)
    found[1::2] = real_values(odd)
    return found


def fine_tables(slabs, width):
    extent = slabs * width
    coarse = np.arange(slabs // 2 + 1)[:, None, None]
    fine = np.arange(width)[None, :, None]
    place = np.arange(width)[None, None, :]
    angles = ((coarse + slabs * fine) * place % extent) * (2.0 * np.pi / extent)
    cosine, sine = np.cos(angles), np.sin(angles)
    table = np.concatenate(
        [np.concatenate([cosine, sine], 2), np.concatenate([-sine, cosine], 2)], 1
    )
    inverse = np.swapaxes(table, 1, 2) / (extent * math.sqrt(extent))
    return table.astype(np.float32), inverse.astype(np.float32)


def low_lanes(shape):
    return lax.broadcasted_iota(jnp.int32, shape, len(shape) - 1) < HALF


def swap(value):
    return pltpu.roll(value, HALF, 1)


def wide(value):
    return value.astype(jnp.float32)


def join(first, second, parity):
    low = low_lanes(first.shape)
    if parity == 0:
        return jnp.where(low, first, swap(second))
    return jnp.where(low, swap(first), second)


def split(first, second):
    return join(first, second, 0), join(first, second, 1)


def bend_of(top):
    return jnp.where(top > TINY, BEND / jnp.maximum(top, TINY), 0.0)


def encode(value, bend):
    size = jnp.exp(SPREAD * jnp.log(1.0 + jnp.abs(value) * bend) + LOWEST)
    return jnp.where(value < 0.0, -size, size)


def decode(code, top):
    size = (jnp.exp((jnp.log(jnp.abs(code)) - LOWEST) * (1.0 / SPREAD)) - 1.0) * (top / BEND)
    return jnp.where(code < 0.0, -size, size)


def layer_kernel(
    devices,
    projected_in,
    cotangent_in,
    filter_in,
    taps_in,
    gain_in,
    forward_in,
    inverse_in,
    recv_conv,
    recv_back,
    recv_sums,
    kept_out,
    projected_ref,
    cotangent_ref,
    filter_ref,
    taps_ref,
    gain_ref,
    forward_ref,
    inverse_ref,
    send_first,
    recv_first,
    send_second,
    recv_second,
    send_filter,
    recv_filter,
    send_top,
    recv_top,
    send_rim,
    recv_rim,
    send_conv,
    send_back,
    send_sums,
    around,
    kept,
    first_rim,
    second_rim,
    first_short,
    signal,
    upstream,
    response,
    back,
    signal_spectra,
    product_spectra,
    load_sem,
    keep_sem,
    send_sem,
    recv_sem,
):
    hops = [(devices // 2 + (-1) ** i * ((i + 1) // 2)) for i in range(devices - 1)]
    arguments = (projected_in, cotangent_in, filter_in, taps_in, gain_in, forward_in, inverse_in)
    held = (
        projected_ref,
        cotangent_ref,
        filter_ref,
        taps_ref,
        gain_ref,
        forward_ref,
        inverse_ref,
    )
    loads = [
        pltpu.make_async_copy(source, target, load_sem.at[index])
        for index, (source, target) in enumerate(zip(arguments, held))
    ]
    for load in loads:
        load.start()
    rows, channels = cotangent_ref.shape
    tiles = channels // LANES
    span = taps_ref.shape[1]
    margin = span // 2
    width = rows // 2
    slabs = 2 * devices
    extent = rows * devices
    factor = 1.0 / math.sqrt(extent)
    me = lax.axis_index("seq")
    odd = lax.rem(me, 2) == 1

    def copy_to(kind, hop, source, target, peer):
        return pltpu.make_async_remote_copy(
            src_ref=source,
            dst_ref=target,
            send_sem=send_sem.at[kind, hop],
            recv_sem=recv_sem.at[kind, hop],
            device_id={"seq": peer},
            device_id_type=pl.DeviceIdType.MESH,
        )

    def peer_at(hop):
        return lax.rem(me + hop, devices)

    def source_at(hop):
        return lax.rem(me + devices - hop, devices)

    barrier = pltpu.get_barrier_semaphore()
    for hop in hops:
        pl.semaphore_signal(
            barrier, inc=1, device_id={"seq": peer_at(hop)}, device_id_type=pl.DeviceIdType.MESH
        )

    loads[0].wait()
    loads[1].wait()

    def lanes_of(peer):
        return pl.ds(pl.multiple_of((peer // 2) * LANES, LANES), LANES)

    def join_for(peer, first, second):
        flip = lax.rem(peer, 2) == 1
        return jnp.where(
            low_lanes(first.shape),
            jnp.where(flip, swap(first), first),
            jnp.where(flip, second, swap(second)),
        ).astype(jnp.bfloat16)

    def pack_first(peer, target):
        lanes = lanes_of(peer)
        target[...] = join_for(
            peer, wide(projected_ref[1, :, lanes]), wide(projected_ref[2, :, lanes])
        )

    def pack_second(peer, target):
        lanes = lanes_of(peer)
        target[...] = join_for(
            peer, wide(projected_ref[0, :, lanes]), wide(cotangent_ref[:, lanes])
        )

    for side, start in enumerate((0, rows - 2 * RIM)):
        part = slice(0, RIM) if side == 0 else slice(RIM, 2 * RIM)
        ends = [wide(projected_ref[s, start : start + 2 * RIM])[part] for s in range(3)]
        ends.append(wide(cotangent_ref[start : start + 2 * RIM])[part])
        for pair in range(2):
            send_rim[side, pair] = jnp.concatenate(ends[2 * pair : 2 * pair + 2], axis=0).astype(
                jnp.bfloat16
            )
    rim_copies = [
        copy_to(7, hop, send_rim.at[side], recv_rim.at[side], peer_at(hop))
        for side, hop in enumerate((devices - 1, 1))
    ]
    for place, hop in enumerate(hops):
        peer = peer_at(hop)
        pack_first(peer, send_first.at[peer])
        if place == 0:
            pl.semaphore_wait(barrier, devices - 1)
            for copy in rim_copies:
                copy.start()
        copy_to(0, hop, send_first.at[peer], recv_first.at[me], peer).start()

    loads[2].wait()
    for tile in range(tiles):
        lanes = slice(tile * LANES, (tile + 1) * LANES)
        whole = filter_ref[:, lanes]
        top = jnp.max(jnp.abs(whole), axis=0, keepdims=True)
        coded = encode(whole, bend_of(top))
        for half in range(2):
            send_filter[2 * tile + half] = join(coded[:width], coded[width:], half).astype(
                jnp.bfloat16
            )
            send_top[2 * tile + half] = join(top, top, half)
    for hop in hops:
        peer = peer_at(hop)
        copy_to(2, hop, send_filter.at[peer], recv_filter.at[me], peer).start()
        copy_to(3, hop, send_top.at[peer], recv_top.at[me], peer).start()
    for hop in hops:
        peer = peer_at(hop)
        pack_second(peer, send_second.at[peer])
        copy_to(1, hop, send_second.at[peer], recv_second.at[me], peer).start()
    pack_first(me, recv_first.at[me])
    pack_second(me, recv_second.at[me])
    recv_filter[me] = send_filter[me]
    recv_top[me] = send_top[me]

    for load in loads[3:5]:
        load.wait()
    own = pl.ds(pl.multiple_of((me // 2) * LANES, LANES), LANES)

    def own_pair(first, second):
        return jnp.where(odd, join(first, second, 1), join(first, second, 0))

    gate_taps, left_taps, right_taps = [taps_ref[s, :, own] for s in range(3)]
    first_taps = own_pair(left_taps, right_taps)
    centre = wide(lax.broadcasted_iota(jnp.int32, (span, LANES), 0) == margin)
    second_taps = jnp.where(low_lanes((span, LANES)), own_pair(gate_taps, gate_taps), centre)
    own_gain = gain_ref[:, own]
    gain = own_pair(own_gain, own_gain)

    for copy in rim_copies:
        copy.wait()
    for stream in range(4):
        around[stream, 0:RIM] = jnp.zeros((RIM, channels), jnp.float32)
        around[stream, rows + 3 * RIM :] = jnp.zeros((RIM, channels), jnp.float32)
        half = slice((stream % 2) * RIM, (stream % 2 + 1) * RIM)
        before, after = wide(recv_rim[1, stream // 2])[half], wide(recv_rim[0, stream // 2])[half]
        around[stream, RIM : 2 * RIM] = before
        around[stream, rows + 2 * RIM : rows + 3 * RIM] = after
        source = cotangent_ref[...] if stream == 3 else projected_ref[stream]
        around[stream, 2 * RIM : 2 * RIM + rows] = wide(source)
    kept[3] = around[3, RIM : rows + 3 * RIM]

    def own_short(step, carry):
        stream, tile = step // tiles, lax.rem(step, tiles)
        lanes = pl.ds(pl.multiple_of(tile * LANES, LANES), LANES)
        taps = taps_ref[stream, :, lanes]
        for part in range(2):
            count = width + RIM
            total = jnp.zeros((count, LANES), jnp.float32)
            for tap in range(span):
                low = part * count + RIM + tap - margin
                total = total + taps[tap : tap + 1] * around[stream, low : low + count, lanes]
            kept[stream, part * count : (part + 1) * count, lanes] = total
        return carry

    lax.fori_loop(0, 3 * tiles, own_short, 0)
    keeping = pltpu.make_async_copy(kept, kept_out, keep_sem.at[3])
    keeping.start()

    def wait_from(kind, source, target):
        for hop in hops:
            copy_to(
                kind, hop, source.at[peer_at(hop)], target.at[source_at(hop)], peer_at(hop)
            ).wait()

    def close_rim(rim):
        rim[0:RIM] = rim[extent : extent + RIM]
        rim[extent + RIM : extent + 2 * RIM] = rim[RIM : 2 * RIM]

    def open_rim(rim, received):
        for block in range(devices):
            rim[RIM + block * rows : RIM + (block + 1) * rows] = wide(received[block])
        close_rim(rim)

    def filtered(rim, taps, start):
        near = rim[pl.ds(start, width + 2 * RIM)]
        total = jnp.zeros((width, LANES), jnp.float32)
        for tap in range(span):
            low = RIM + tap - margin
            total = total + taps[tap : tap + 1] * near[low : low + width]
        return total

    wait_from(0, send_first, recv_first)
    open_rim(first_rim, recv_first)

    def shorten_first(slab, carry):
        start = pl.multiple_of(slab * width, width)
        total = filtered(first_rim, first_taps, start)
        first_short[pl.ds(start, width)] = total
        signal[pl.ds(start, width)] = total * swap(total)
        return carry

    lax.fori_loop(0, slabs, shorten_first, 0)
    for load in loads[5:]:
        load.wait()
    wait_from(2, send_filter, recv_filter)
    wait_from(3, send_top, recv_top)

    def put_spectrum(spectra, found, start, count):
        for index, (real_part, imaginary) in enumerate(found):
            if imaginary is None:
                imaginary = jnp.zeros_like(real_part)
            spectra[index, pl.ds(start, count)] = real_part
            spectra[index, pl.ds(width + start, count)] = imaginary

    def get_spectrum(spectra, start, count):
        found = []
        for index in range(slabs // 2 + 1):
            imaginary = None
            if 0 < index < slabs // 2:
                imaginary = spectra[index, pl.ds(width + start, count)]
            found.append((spectra[index, pl.ds(start, count)], imaginary))
        return found

    def first_spectrum(step, carry):
        start = pl.multiple_of(step * 16, 16)
        low = low_lanes((16, LANES))
        values = []
        for block in range(devices):
            found = decode(wide(recv_filter[block, pl.ds(start, 16)]), recv_top[block])
            for half in range(2):
                here = signal[pl.ds(block * rows + half * width + start, 16)]
                values.append(jnp.where(low, here, swap(found) if half == 0 else found))
        put_spectrum(signal_spectra, real_spectrum(values), start, 16)
        return carry

    lax.fori_loop(0, width // 16, first_spectrum, 0)

    for index in range(slabs // 2 + 1):
        found = jnp.dot(forward_ref[index], signal_spectra[index], precision=HIGHEST)
        signal_spectra[index] = found
        real_part, imaginary = found[:width], found[width:]
        other_real, other_imag = swap(real_part), swap(imaginary)
        product = jnp.concatenate(
            [
                real_part * other_real - imaginary * other_imag,
                real_part * other_imag + imaginary * other_real,
            ],
            axis=0,
        )
        product_spectra[index] = jnp.dot(inverse_ref[index], product, precision=HIGHEST)

    def first_back(step, top):
        start = pl.multiple_of(step * 8, 8)
        for slab, value in enumerate(real_values(get_spectrum(product_spectra, start, 8))):
            place = pl.ds(slab * width + start, 8)
            whole = value + gain * signal[place]
            response[place] = whole
            top = jnp.maximum(top, jnp.abs(whole))
        return top

    nothing = jnp.zeros((8, LANES), jnp.float32)
    top = lax.fori_loop(0, width // 8, first_back, nothing)
    response_top = jnp.max(top, axis=0, keepdims=True)
    response_bend = bend_of(response_top)

    def step_hop(step):
        return devices // 2 + (step + 1) // 2 * (1 - 2 * lax.rem(step, 2))

    def pack_conv(peer):
        start = pl.multiple_of(peer * rows, rows)
        folded = jnp.where(
            low_lanes((width, LANES)),
            response[pl.ds(start, width)],
            response[pl.ds(start + width, width)],
        )
        send_conv[peer] = encode(folded, response_bend).astype(jnp.bfloat16)

    def step_conv(step, carry):
        hop = step_hop(step)
        peer = peer_at(hop)
        pack_conv(peer)
        copy_to(4, hop, send_conv.at[peer], recv_conv.at[me], peer).start()
        return carry

    lax.fori_loop(0, devices - 1, step_conv, 0)
    pack_conv(me)
    keeps = [
        pltpu.make_async_copy(source, target.at[me], keep_sem.at[index])
        for index, (source, target) in enumerate(
            (
                (send_conv.at[me], recv_conv),
                (send_back.at[me], recv_back),
                (send_sums, recv_sums),
            )
        )
    ]
    keeps[0].start()

    wait_from(1, send_second, recv_second)
    open_rim(second_rim, recv_second)

    def shorten_second(slab, carry):
        start = pl.multiple_of(slab * width, width)
        total = filtered(second_rim, second_taps, start)
        total = total * swap(total)
        upstream[pl.ds(start, width)] = total
        return carry + jnp.sum(
            (total * signal[pl.ds(start, width)]).reshape(-1, 8, LANES), axis=0
        )

    gain_sum = lax.fori_loop(0, slabs, shorten_second, nothing)

    def second_spectrum(step, carry):
        start = pl.multiple_of(step * 8, 8)
        values = [upstream[pl.ds(slab * width + start, 8)] for slab in range(slabs)]
        put_spectrum(product_spectra, real_spectrum(values), start, 8)
        return carry

    lax.fori_loop(0, width // 8, second_spectrum, 0)

    for index in range(slabs // 2 + 1):
        found = jnp.dot(forward_ref[index], product_spectra[index], precision=HIGHEST)
        real_part, imaginary = found[:width], found[width:]
        other_real = swap(signal_spectra[index, :width])
        other_imag = swap(signal_spectra[index, width:])
        product = jnp.concatenate(
            [
                real_part * other_real + imaginary * other_imag,
                imaginary * other_real - real_part * other_imag,
            ],
            axis=0,
        )
        product_spectra[index] = jnp.dot(inverse_ref[index], product, precision=HIGHEST)

    low_gain = jnp.where(low_lanes((1, LANES)), gain, 0.0)

    def second_back(step, top):
        start = pl.multiple_of(step * 8, 8)
        for slab, value in enumerate(real_values(get_spectrum(product_spectra, start, 8))):
            place = pl.ds(slab * width + start, 8)
            whole = value + low_gain * upstream[place]
            back[place] = whole
            top = jnp.maximum(top, jnp.abs(whole))
        return top

    top = lax.fori_loop(0, width // 8, second_back, nothing)
    back_top = jnp.max(top, axis=0, keepdims=True)
    back_bend = bend_of(back_top)
    rim_bend = jnp.where(low_lanes((1, LANES)), back_bend, response_bend)

    def pack_back(peer):
        start = pl.multiple_of(peer * rows, rows)
        send_back[peer, 0:rows] = encode(back[pl.ds(start, rows)], back_bend).astype(jnp.bfloat16)
        places = (
            lax.rem(start + extent - RIM, extent),
            lax.rem(start + rows, extent),
        )
        ends = []
        for place in places:
            here = pl.ds(pl.multiple_of(place, RIM), RIM)
            ends.append(jnp.where(low_lanes((RIM, LANES)), back[here], response[here]))
        send_back[peer, rows : rows + 2 * RIM] = encode(
            jnp.concatenate(ends, axis=0), rim_bend
        ).astype(jnp.bfloat16)

    def step_back(step, carry):
        hop = step_hop(step)
        peer = peer_at(hop)
        pack_back(peer)
        copy_to(5, hop, send_back.at[peer], recv_back.at[me], peer).start()
        return carry

    lax.fori_loop(0, devices - 1, step_back, 0)
    pack_back(me)
    keeps[1].start()

    def add_sums(slab, sums):
        sums = list(sums)
        start = pl.multiple_of(slab * width, width)
        here = pl.ds(start, width)
        low = low_lanes((width, LANES))
        grad = back[here]
        grad = jnp.where(low, grad, swap(grad)) * swap(first_short[here])
        near_first = first_rim[pl.ds(start, width + 2 * RIM)]
        near_second = second_rim[pl.ds(start, width + 2 * RIM)]
        other = response[here] * swap(near_second[RIM : RIM + width])
        for tap in range(span):
            inner = slice(RIM + tap - margin, RIM + tap - margin + width)
            for which, (grads, near) in enumerate(((grad, near_first), (other, near_second))):
                sums[which * span + tap] = sums[which * span + tap] + jnp.sum(
                    (grads * near[inner]).reshape(-1, 8, LANES), axis=0
                )
        return tuple(sums)

    sums = lax.fori_loop(0, slabs, add_sums, (nothing,) * (2 * span))
    sums = [factor * jnp.sum(value, axis=0, keepdims=True) for value in sums + (gain_sum,)]
    middle = (span + 1) // 2
    for index in range(span):
        send_sums[index : index + 1] = sums[index]
    for index in range(span, span + middle):
        send_sums[index : index + 1] = join(sums[index], sums[index + middle], 0)
    send_sums[span + middle : span + middle + 1] = response_top
    send_sums[span + middle + 1 : span + middle + 2] = back_top
    for hop in hops:
        copy_to(6, hop, send_sums, recv_sums.at[me], peer_at(hop)).start()
    keeps[2].start()
    keeping.wait()
    for keep in keeps:
        keep.wait()
    wait_from(4, send_conv, recv_conv)
    wait_from(5, send_back, recv_back)
    for hop in hops:
        copy_to(6, hop, send_sums, recv_sums.at[source_at(hop)], peer_at(hop)).wait()


def unpack_kernel(*refs):
    packed, results, held, refs = refs[:5], refs[5:10], refs[10:15], refs[15:]
    output_ref, streams_ref, filter_grad_ref, taps_grad_ref, gain_grad_ref = refs[:5]
    recv_conv, recv_back, recv_sums, kept, taps_ref = held
    grads, load_sem, store_sem = refs[5:]
    loads = [pltpu.make_async_copy(packed[i], held[i], load_sem.at[i]) for i in range(5)]
    stores = [pltpu.make_async_copy(refs[i], results[i], store_sem.at[i]) for i in range(5)]
    for load in loads:
        load.start()
    tiles = recv_conv.shape[0] // 2
    rows = output_ref.shape[0]
    span = taps_grad_ref.shape[1]
    margin = span // 2
    middle = (span + 1) // 2
    for load in loads:
        load.wait()
    for tile in range(tiles):
        lanes = slice(tile * LANES, (tile + 1) * LANES)
        tops = [recv_sums[2 * tile + half] for half in range(2)]
        low_part, high_part = split(tops[0], tops[1])
        taps_grad_ref[1, :, lanes] = low_part[0:span]
        taps_grad_ref[2, :, lanes] = high_part[0:span]
        taps_grad_ref[0, :middle, lanes] = low_part[span : span + middle]
        taps_grad_ref[0, middle:, lanes] = high_part[span : 2 * span - middle]
        gain_grad_ref[:, lanes] = high_part[2 * span - middle : 2 * span - middle + 1]
        response_top, back_top = [
            [top[span + middle + i : span + middle + i + 1] for top in tops] for i in range(2)
        ]
        pieces = split(
            *(decode(wide(recv_conv[2 * tile + i]), response_top[i]) for i in range(2))
        )
        found = [
            decode(wide(recv_back[2 * tile + i, 0:rows]), back_top[i]) for i in range(2)
        ]
        grad, filter_grad = split(*found)
        filter_grad_ref[:, lanes] = filter_grad
        low = low_lanes((1, LANES))
        rims = [
            decode(
                wide(recv_back[2 * tile + i, rows : rows + 2 * RIM]),
                jnp.where(low, back_top[i], response_top[i]),
            )
            for i in range(2)
        ]
        grad_rim, response_rim = split(*rims)
        response = jnp.concatenate(
            [response_rim[:RIM], pieces[0], pieces[1], response_rim[RIM:]], axis=0
        )
        grad = jnp.concatenate([grad_rim[:RIM], grad, grad_rim[RIM:]], axis=0)
        output_ref[:, lanes] = (
            response[RIM : RIM + rows] * kept[0, RIM : RIM + rows, lanes]
        ).astype(jnp.bfloat16)
        grads[0] = response * kept[3, :, lanes]
        grads[1] = grad * kept[2, :, lanes]
        grads[2] = grad * kept[1, :, lanes]
        for stream in range(3):
            taps = taps_ref[stream, :, lanes]
            total = jnp.zeros((rows, LANES), jnp.float32)
            for tap in range(span):
                first = RIM + margin - tap
                total = total + taps[tap : tap + 1] * grads[stream, first : first + rows]
            streams_ref[stream, :, lanes] = total.astype(jnp.bfloat16)
    for store in stores:
        store.start()
    for store in stores:
        store.wait()


def packed_body(devices, projected, long_filter, short_kernel, skip_gain, cotangent):
    rows, channels = long_filter.shape
    span = short_kernel.shape[1]
    extent = rows * devices
    slabs = 2 * devices
    width = rows // 2
    tables = fine_tables(slabs, width)
    sums_rows = span + (span + 1) // 2 + 2
    block = (devices, rows, LANES)
    half_block = (devices, width, LANES)
    longer = (devices, rows + 2 * RIM, LANES)
    narrow, full = jnp.bfloat16, jnp.float32
    arguments = (projected, cotangent, long_filter, short_kernel, skip_gain[None], *tables)
    in_hbm = pl.BlockSpec(memory_space=pltpu.HBM)
    packed_shapes = (
        jax.ShapeDtypeStruct(half_block, narrow),
        jax.ShapeDtypeStruct(longer, narrow),
        jax.ShapeDtypeStruct((devices, sums_rows, LANES), full),
        jax.ShapeDtypeStruct((4, rows + 2 * RIM, channels), full),
    )
    out_shapes = (
        jax.ShapeDtypeStruct((rows, channels), narrow),
        jax.ShapeDtypeStruct((3, rows, channels), narrow),
        jax.ShapeDtypeStruct((rows, channels), full),
        jax.ShapeDtypeStruct(short_kernel.shape, full),
        jax.ShapeDtypeStruct((1, channels), full),
    )
    packed = pl.pallas_call(
        functools.partial(layer_kernel, devices),
        out_shape=packed_shapes,
        in_specs=[in_hbm] * 7,
        out_specs=(in_hbm,) * 4,
        scratch_shapes=[
            *(pltpu.VMEM(value.shape, value.dtype) for value in arguments),
            pltpu.VMEM(block, narrow),
            pltpu.VMEM(block, narrow),
            pltpu.VMEM(block, narrow),
            pltpu.VMEM(block, narrow),
            pltpu.VMEM(half_block, narrow),
            pltpu.VMEM(half_block, narrow),
            pltpu.VMEM((devices, 1, LANES), full),
            pltpu.VMEM((devices, 1, LANES), full),
            pltpu.VMEM((2, 2, 2 * RIM, channels), narrow),
            pltpu.VMEM((2, 2, 2 * RIM, channels), narrow),
            pltpu.VMEM(half_block, narrow),
            pltpu.VMEM(longer, narrow),
            pltpu.VMEM((sums_rows, LANES), full),
            pltpu.VMEM((4, rows + 4 * RIM, channels), full),
            pltpu.VMEM((4, rows + 2 * RIM, channels), full),
            pltpu.VMEM((extent + 2 * RIM, LANES), full),
            pltpu.VMEM((extent + 2 * RIM, LANES), full),
            *[pltpu.VMEM((extent, LANES), full)] * 5,
            *[pltpu.VMEM((slabs // 2 + 1, rows, LANES), full)] * 2,
            pltpu.SemaphoreType.DMA((len(arguments),)),
            pltpu.SemaphoreType.DMA((4,)),
            pltpu.SemaphoreType.DMA((8, devices)),
            pltpu.SemaphoreType.DMA((8, devices)),
        ],
        compiler_params=pltpu.CompilerParams(
            collective_id=0, has_side_effects=True, vmem_limit_bytes=LIMIT
        ),
    )(*arguments)
    found = pl.pallas_call(
        unpack_kernel,
        out_shape=out_shapes,
        in_specs=[in_hbm] * 5,
        out_specs=(in_hbm,) * 5,
        scratch_shapes=[
            *(pltpu.VMEM(value.shape, value.dtype) for value in packed_shapes),
            pltpu.VMEM(short_kernel.shape, full),
            *(pltpu.VMEM(value.shape, value.dtype) for value in out_shapes),
            pltpu.VMEM((3, rows + 2 * RIM, LANES), full),
            pltpu.SemaphoreType.DMA((5,)),
            pltpu.SemaphoreType.DMA((5,)),
        ],
        compiler_params=pltpu.CompilerParams(vmem_limit_bytes=LIMIT),
    )(*packed, short_kernel)
    return (*found[:4], found[4][0])


def with_halo(block, sides, width):
    for axis, dim in sides:
        count = lax.axis_size(axis)
        forward = [(i, i + 1) for i in range(count - 1)]
        forward.append((count - 1, 0))
        backward = [(target, source) for source, target in forward]
        low = lax.ppermute(
            lax.slice_in_dim(block, block.shape[dim] - width, None, axis=dim), axis, forward
        )
        high = lax.ppermute(lax.slice_in_dim(block, 0, width, axis=dim), axis, backward)
        block = jnp.concatenate([low, block, high], axis=dim)
    return block


def dft_tables(extent):
    indices = jnp.arange(extent, dtype=jnp.int32)
    angles = (indices[:, None] * indices[None, :] % extent).astype(jnp.float32) * (
        2.0 * math.pi / extent
    )
    return (jnp.cos(angles), jnp.sin(angles))


def apply_along(matrix, signal, axis_dim):
    letters = "wxyz"
    target = letters[:axis_dim] + "k" + letters[axis_dim + 1 :]
    return jnp.einsum(
        "k" + letters[axis_dim] + "," + letters + "->" + target, matrix, signal, precision=HIGHEST
    )


def forward_section(real_part, imaginary, axis_dim):
    cosine, sine_table = dft_tables(real_part.shape[axis_dim])
    out_real = apply_along(cosine, real_part, axis_dim)
    out_imag = -apply_along(sine_table, real_part, axis_dim)
    if imaginary is not None:
        out_real = out_real + apply_along(sine_table, imaginary, axis_dim)
        out_imag = out_imag + apply_along(cosine, imaginary, axis_dim)
    return (out_real, out_imag)


def inverse_section(real_part, imaginary, axis_dim, keep_imag):
    cosine, sine_table = dft_tables(real_part.shape[axis_dim])
    out_real = apply_along(cosine, real_part, axis_dim) - apply_along(
        sine_table, imaginary, axis_dim
    )
    if keep_imag:
        return (
            out_real,
            apply_along(sine_table, real_part, axis_dim) + apply_along(cosine, imaginary, axis_dim),
        )
    return (out_real, None)


def twist(real_part, imaginary, angles, sign_factor):
    cosine = jnp.cos(angles)
    sine_table = jnp.sin(angles)
    return (
        real_part * cosine + sign_factor * imaginary * sine_table,
        imaginary * cosine - sign_factor * real_part * sine_table,
    )


def twiddle(low_index, high_index, extent):
    return (low_index * high_index % extent).astype(jnp.float32) * (2.0 * math.pi / extent)


def block_angles(devices, portion, extent):
    low_index = jnp.arange(devices, dtype=jnp.int32)[None, :, None, None]
    high_index = (lax.axis_index("seq") * portion + jnp.arange(portion, dtype=jnp.int32))[
        None, None, :, None
    ]
    return twiddle(low_index, high_index, extent)


def sequence_forward(signals, extent):
    devices = lax.axis_size("seq")
    portion = signals.shape[1] // devices
    columns = lax.all_to_all(signals[:, None], "seq", split_axis=2, concat_axis=1, tiled=True)
    real_part, imaginary = forward_section(columns, None, 1)
    real_part, imaginary = twist(real_part, imaginary, block_angles(devices, portion, extent), 1.0)
    spread = (
        lax.all_to_all(real_part, "seq", split_axis=1, concat_axis=2, tiled=True),
        lax.all_to_all(imaginary, "seq", split_axis=1, concat_axis=2, tiled=True),
    )
    return forward_section(spread[0], spread[1], 2)


def sequence_inverse(real_part, imaginary, extent):
    devices = lax.axis_size("seq")
    portion = real_part.shape[2] // devices
    real_part, imaginary = inverse_section(real_part, imaginary, 2, True)
    gathered = (
        lax.all_to_all(real_part, "seq", split_axis=2, concat_axis=1, tiled=True),
        lax.all_to_all(imaginary, "seq", split_axis=2, concat_axis=1, tiled=True),
    )
    real_part, imaginary = twist(
        gathered[0], gathered[1], block_angles(devices, portion, extent), -1.0
    )
    pieces = inverse_section(real_part, imaginary, 1, False)[0] * (1.0 / extent)
    blocks = lax.all_to_all(pieces, "seq", split_axis=1, concat_axis=2, tiled=True)
    return blocks[:, 0]


def body(projected, long_filter, short_kernel, skip_gain, cotangent):
    rows_here = projected.shape[1]
    extent = rows_here * lax.axis_size("seq")
    factor = 1.0 / math.sqrt(extent)
    kernel_span = short_kernel.shape[1]
    margin = kernel_span // 2
    padded = with_halo(projected, (("seq", 1),), margin)
    shorts = jnp.zeros(projected.shape, jnp.float32)
    for offset in range(kernel_span):
        shorts = shorts + short_kernel[:, offset][:, None, :] * padded[
            :, offset : offset + rows_here
        ].astype(jnp.float32)
    gated_signal = shorts[1] * shorts[2]
    transform, restore = (sequence_forward, sequence_inverse)
    upstream = cotangent.astype(jnp.float32)
    grad_response = upstream * shorts[0]
    spec_real, spec_imag = transform(jnp.stack([gated_signal, long_filter]), extent)
    gated_real, gated_imag = (spec_real[0], spec_imag[0])
    filter_real, filter_imag = (spec_real[1] * factor, spec_imag[1] * factor)
    product_real = filter_real * gated_real - filter_imag * gated_imag
    product_imag = filter_real * gated_imag + filter_imag * gated_real
    convolved = restore(product_real[None], product_imag[None], extent)[0]
    upstream_real, upstream_imag = transform(grad_response[None], extent)
    upstream_real, upstream_imag = (upstream_real[0], upstream_imag[0])
    back_real = jnp.stack(
        [
            filter_real * upstream_real + filter_imag * upstream_imag,
            gated_real * upstream_real + gated_imag * upstream_imag,
        ]
    )
    back_imag = jnp.stack(
        [
            filter_real * upstream_imag - filter_imag * upstream_real,
            gated_real * upstream_imag - gated_imag * upstream_real,
        ]
    )
    restored = restore(back_real, back_imag, extent)
    grad_gated = restored[0] + skip_gain * grad_response
    filter_grad = restored[1] * factor
    response = convolved + skip_gain * gated_signal
    layer_output = (response * shorts[0]).astype(jnp.bfloat16)
    grad_shorts = jnp.stack([upstream * response, grad_gated * shorts[2], grad_gated * shorts[1]])
    rimmed = with_halo(grad_shorts, (("seq", 1),), margin)
    stream_sum = jnp.zeros(grad_shorts.shape, jnp.float32)
    kernel_terms = []
    for offset in range(kernel_span):
        start_row = 2 * margin - offset
        stream_sum = (
            stream_sum
            + short_kernel[:, offset][:, None, :] * rimmed[:, start_row : start_row + rows_here]
        )
        kernel_terms.append(
            jnp.sum(
                grad_shorts * padded[:, offset : offset + rows_here].astype(jnp.float32), axis=1
            )
        )
    kernel_part = jnp.stack(kernel_terms, axis=1)
    skip_part = jnp.sum(grad_response * gated_signal, axis=0)
    kernel_total, skip_total = lax.psum((kernel_part, skip_part), "seq")
    return (
        layer_output,
        stream_sum.astype(jnp.bfloat16),
        filter_grad,
        kernel_total * factor,
        skip_total * factor,
    )


def solution(mesh):
    placed = (
        P(None, ("groups", "seq"), "chan"),
        P(("groups", "seq"), "chan"),
        P(None, None, "chan"),
        P("chan"),
        P(("groups", "seq"), "chan"),
    )
    devices = mesh.shape["seq"]

    def run(projected, *others):
        rows, channels = projected.shape[1:]
        if channels == HALF * devices and rows == LANES and devices & (devices - 1) == 0:
            return packed_body(devices, projected, *others)
        return body(projected, *others)

    return jax.shard_map(
        run,
        mesh=mesh,
        in_specs=placed,
        out_specs=(
            P(("groups", "seq"), "chan"),
            P(None, ("groups", "seq"), "chan"),
            P(("groups", "seq"), "chan"),
            P("groups", None, "chan"),
            P(("groups", "chan")),
        ),
        check_vma=False,
    )
```

```python
import functools
import math

import jax
import jax.numpy as jnp
import ml_dtypes
import numpy as np
from jax import lax
from jax.experimental import pallas as pl
from jax.experimental.pallas import tpu as pltpu
from jax.sharding import PartitionSpec as P

HIGHEST = lax.Precision.HIGHEST
LANES = 128
HALF = LANES // 2
RIM = 8
LIMIT = 20 * 1024 * 1024
BEND = 15.0
SPREAD = 251.0 * math.log(2.0) / math.log(1.0 + BEND)
LOWEST = -125.0 * math.log(2.0)
TINY = 1e-35


def turned(value, step, extent):
    real_part, imaginary = value
    step = step % extent
    if step == 0:
        return value
    if 2 * step == extent:
        return (-real_part, None if imaginary is None else -imaginary)
    if 4 * step == extent:
        return (None if imaginary is None else -imaginary, real_part)
    if 4 * step == 3 * extent:
        return (imaginary, -real_part)
    cosine = math.cos(2.0 * math.pi * step / extent)
    sine = math.sin(2.0 * math.pi * step / extent)
    if imaginary is None:
        return (real_part * cosine, real_part * sine)
    return (real_part * cosine - imaginary * sine, imaginary * cosine + real_part * sine)


def part_sum(left, right, sign):
    if right is None:
        return left
    if left is None:
        return right if sign > 0 else -right
    return left + right if sign > 0 else left - right


def real_spectrum(values):
    extent = len(values)
    if extent == 2:
        return [(values[0] + values[1], None), (values[0] - values[1], None)]
    even, odd = real_spectrum(values[0::2]), real_spectrum(values[1::2])
    half = extent // 2

    def entry(spectrum, index):
        index = index % half
        if 2 * index <= half:
            return spectrum[index]
        real_part, imaginary = spectrum[half - index]
        return (real_part, None if imaginary is None else -imaginary)

    found = []
    for index in range(half + 1):
        left, right = entry(even, index), turned(entry(odd, index), -index, extent)
        found.append((part_sum(left[0], right[0], 1), part_sum(left[1], right[1], 1)))
    return found


def real_values(spectrum):
    extent = 2 * (len(spectrum) - 1)
    if extent == 2:
        first, last = spectrum[0][0], spectrum[1][0]
        return [first + last, first - last]
    half = extent // 2
    even, odd = [], []
    for index in range(half // 2 + 1):
        real_part, imaginary = spectrum[index]
        if 2 * index == half:
            even.append((2.0 * real_part, None))
            odd.append((-2.0 * imaginary, None))
            continue
        other_real, other_imag = spectrum[half - index]
        even.append(
            (real_part + other_real, part_sum(imaginary, other_imag, -1))
        )
        odd.append(
            turned(
                (real_part - other_real, part_sum(imaginary, other_imag, 1)), index, extent
            )
        )
    found = [None] * extent
    found[0::2] = real_values(even)
    found[1::2] = real_values(odd)
    return found


def fine_tables(slabs, width):
    extent = slabs * width
    coarse = np.arange(slabs // 2 + 1)[:, None, None]
    fine = np.arange(width)[None, :, None]
    place = np.arange(width)[None, None, :]
    angles = ((coarse + slabs * fine) * place % extent) * (2.0 * np.pi / extent)
    cosine, sine = np.cos(angles), np.sin(angles)
    table = np.concatenate(
        [np.concatenate([cosine, sine], 2), np.concatenate([-sine, cosine], 2)], 1
    )
    inverse = np.swapaxes(table, 1, 2) / (extent * math.sqrt(extent))
    return table.astype(np.float32), inverse.astype(np.float32)


def low_lanes(shape):
    return lax.broadcasted_iota(jnp.int32, shape, len(shape) - 1) < HALF


def swap(value):
    return pltpu.roll(value, HALF, 1)


def wide(value):
    return value.astype(jnp.float32)


def join(first, second, parity):
    low = low_lanes(first.shape)
    if parity == 0:
        return jnp.where(low, first, swap(second))
    return jnp.where(low, swap(first), second)


def split(first, second):
    return join(first, second, 0), join(first, second, 1)


def bend_of(top):
    return jnp.where(top > TINY, BEND / jnp.maximum(top, TINY), 0.0)


def encode(value, bend):
    size = jnp.exp(SPREAD * jnp.log(1.0 + jnp.abs(value) * bend) + LOWEST)
    return jnp.where(value < 0.0, -size, size)


def decode(code, top):
    size = (jnp.exp((jnp.log(jnp.abs(code)) - LOWEST) * (1.0 / SPREAD)) - 1.0) * (top / BEND)
    return jnp.where(code < 0.0, -size, size)


def halves(value):
    coarse = value.astype(jnp.bfloat16)
    return coarse, (value - wide(coarse)).astype(jnp.bfloat16)


def apply_table(table, index, value):
    coarse, rest = halves(value)
    depth = coarse.shape[0]
    return jnp.dot(
        table[index],
        jnp.concatenate([coarse, coarse], axis=0),
        preferred_element_type=jnp.float32,
    ) + jnp.dot(table[index, :, :depth], rest, preferred_element_type=jnp.float32)


def layer_kernel(
    devices,
    projected_in,
    cotangent_in,
    filter_in,
    taps_in,
    gain_in,
    forward_in,
    inverse_in,
    recv_conv,
    recv_back,
    recv_sums,
    kept_out,
    taps_out,
    projected_ref,
    cotangent_ref,
    filter_ref,
    taps_ref,
    gain_ref,
    forward_ref,
    inverse_ref,
    send_first,
    recv_first,
    send_second,
    recv_second,
    send_filter,
    recv_filter,
    send_top,
    recv_top,
    send_rim,
    recv_rim,
    send_conv,
    send_back,
    send_sums,
    around,
    kept,
    first_rim,
    second_rim,
    first_short,
    signal,
    upstream,
    response,
    back,
    signal_spectra,
    product_spectra,
    load_sem,
    keep_sem,
    send_sem,
    recv_sem,
):
    hops = [(devices // 2 + (-1) ** i * ((i + 1) // 2)) for i in range(devices - 1)]
    arguments = (projected_in, cotangent_in, filter_in, taps_in, gain_in, forward_in, inverse_in)
    held = (
        projected_ref,
        cotangent_ref,
        filter_ref,
        taps_ref,
        gain_ref,
        forward_ref,
        inverse_ref,
    )
    loads = [
        pltpu.make_async_copy(source, target, load_sem.at[index])
        for index, (source, target) in enumerate(zip(arguments, held))
    ]
    for load in loads:
        load.start()
    rows, channels = cotangent_ref.shape
    tiles = channels // LANES
    span = taps_ref.shape[1]
    margin = span // 2
    width = rows // 2
    slabs = 2 * devices
    extent = rows * devices
    factor = 1.0 / math.sqrt(extent)
    me = lax.axis_index("seq")
    odd = lax.rem(me, 2) == 1

    def copy_to(kind, hop, source, target, peer):
        return pltpu.make_async_remote_copy(
            src_ref=source,
            dst_ref=target,
            send_sem=send_sem.at[kind, hop],
            recv_sem=recv_sem.at[kind, hop],
            device_id={"seq": peer},
            device_id_type=pl.DeviceIdType.MESH,
        )

    def peer_at(hop):
        return lax.rem(me + hop, devices)

    def source_at(hop):
        return lax.rem(me + devices - hop, devices)

    barrier = pltpu.get_barrier_semaphore()
    for hop in hops:
        pl.semaphore_signal(
            barrier, inc=1, device_id={"seq": peer_at(hop)}, device_id_type=pl.DeviceIdType.MESH
        )

    loads[0].wait()
    loads[1].wait()

    def lanes_of(peer):
        return pl.ds(pl.multiple_of((peer // 2) * LANES, LANES), LANES)

    def join_for(peer, first, second):
        flip = lax.rem(peer, 2) == 1
        return jnp.where(
            low_lanes(first.shape),
            jnp.where(flip, swap(first), first),
            jnp.where(flip, second, swap(second)),
        ).astype(jnp.bfloat16)

    def pack_first(peer, target):
        lanes = lanes_of(peer)
        target[...] = join_for(
            peer, wide(projected_ref[1, :, lanes]), wide(projected_ref[2, :, lanes])
        )

    def pack_second(peer, target):
        lanes = lanes_of(peer)
        target[...] = join_for(
            peer, wide(projected_ref[0, :, lanes]), wide(cotangent_ref[:, lanes])
        )

    for side, start in enumerate((0, rows - 2 * RIM)):
        part = slice(0, RIM) if side == 0 else slice(RIM, 2 * RIM)
        ends = [wide(projected_ref[s, start : start + 2 * RIM])[part] for s in range(3)]
        ends.append(wide(cotangent_ref[start : start + 2 * RIM])[part])
        for pair in range(2):
            send_rim[side, pair] = jnp.concatenate(ends[2 * pair : 2 * pair + 2], axis=0).astype(
                jnp.bfloat16
            )
    rim_copies = [
        copy_to(7, hop, send_rim.at[side], recv_rim.at[side], peer_at(hop))
        for side, hop in enumerate((devices - 1, 1))
    ]
    for place, hop in enumerate(hops):
        peer = peer_at(hop)
        pack_first(peer, send_first.at[peer])
        if place == 0:
            pl.semaphore_wait(barrier, devices - 1)
        copy_to(0, hop, send_first.at[peer], recv_first.at[me], peer).start()

    loads[2].wait()
    for tile in range(tiles):
        lanes = slice(tile * LANES, (tile + 1) * LANES)
        whole = filter_ref[:, lanes]
        top = jnp.max(jnp.abs(whole), axis=0, keepdims=True)
        coded = encode(whole, bend_of(top))
        for half in range(2):
            send_filter[2 * tile + half] = join(coded[:width], coded[width:], half).astype(
                jnp.bfloat16
            )
            send_top[2 * tile + half] = join(top, top, half)
    for hop in hops:
        peer = peer_at(hop)
        copy_to(2, hop, send_filter.at[peer], recv_filter.at[me], peer).start()
        copy_to(3, hop, send_top.at[peer], recv_top.at[me], peer).start()
    for hop in hops:
        peer = peer_at(hop)
        pack_second(peer, send_second.at[peer])
        copy_to(1, hop, send_second.at[peer], recv_second.at[me], peer).start()
    for copy in rim_copies:
        copy.start()
    pack_first(me, recv_first.at[me])
    pack_second(me, recv_second.at[me])
    recv_filter[me] = send_filter[me]
    recv_top[me] = send_top[me]

    for load in loads[3:5]:
        load.wait()
    own = pl.ds(pl.multiple_of((me // 2) * LANES, LANES), LANES)

    def own_pair(first, second):
        return jnp.where(odd, join(first, second, 1), join(first, second, 0))

    gate_taps, left_taps, right_taps = [taps_ref[s, :, own] for s in range(3)]
    first_taps = own_pair(left_taps, right_taps)
    centre = wide(lax.broadcasted_iota(jnp.int32, (span, LANES), 0) == margin)
    second_taps = jnp.where(low_lanes((span, LANES)), own_pair(gate_taps, gate_taps), centre)
    own_gain = gain_ref[:, own]
    gain = own_pair(own_gain, own_gain)

    def wait_from(kind, source, target):
        for hop in hops:
            copy_to(
                kind, hop, source.at[peer_at(hop)], target.at[source_at(hop)], peer_at(hop)
            ).wait()

    def close_rim(rim):
        rim[0:RIM] = rim[extent : extent + RIM]
        rim[extent + RIM : extent + 2 * RIM] = rim[RIM : 2 * RIM]

    def open_rim(rim, received):
        for block in range(devices):
            rim[RIM + block * rows : RIM + (block + 1) * rows] = wide(received[block])
        close_rim(rim)

    def filtered(rim, taps, start):
        near = rim[pl.ds(start, width + 2 * RIM)]
        total = jnp.zeros((width, LANES), jnp.float32)
        for tap in range(span):
            low = RIM + tap - margin
            total = total + taps[tap : tap + 1] * near[low : low + width]
        return total

    wait_from(0, send_first, recv_first)
    open_rim(first_rim, recv_first)

    def shorten_first(slab, carry):
        start = pl.multiple_of(slab * width, width)
        total = filtered(first_rim, first_taps, start)
        first_short[pl.ds(start, width)] = total
        signal[pl.ds(start, width)] = total * swap(total)
        return carry

    lax.fori_loop(0, slabs, shorten_first, 0)
    for load in loads[5:]:
        load.wait()
    wait_from(2, send_filter, recv_filter)
    wait_from(3, send_top, recv_top)

    def put_spectrum(spectra, found, start, count):
        for index, (real_part, imaginary) in enumerate(found):
            if imaginary is None:
                imaginary = jnp.zeros_like(real_part)
            spectra[index, pl.ds(start, count)] = real_part
            spectra[index, pl.ds(width + start, count)] = imaginary

    def get_spectrum(spectra, start, count):
        found = []
        for index in range(slabs // 2 + 1):
            imaginary = None
            if 0 < index < slabs // 2:
                imaginary = spectra[index, pl.ds(width + start, count)]
            found.append((spectra[index, pl.ds(start, count)], imaginary))
        return found

    def first_spectrum(step, carry):
        start = pl.multiple_of(step * 16, 16)
        low = low_lanes((16, LANES))
        values = []
        for block in range(devices):
            found = decode(wide(recv_filter[block, pl.ds(start, 16)]), recv_top[block])
            for half in range(2):
                here = signal[pl.ds(block * rows + half * width + start, 16)]
                values.append(jnp.where(low, here, swap(found) if half == 0 else found))
        put_spectrum(signal_spectra, real_spectrum(values), start, 16)
        return carry

    lax.fori_loop(0, width // 16, first_spectrum, 0)

    for index in range(slabs // 2 + 1):
        found = apply_table(forward_ref, index, signal_spectra[index])
        signal_spectra[index] = found
        real_part, imaginary = found[:width], found[width:]
        other_real, other_imag = swap(real_part), swap(imaginary)
        product = jnp.concatenate(
            [
                real_part * other_real - imaginary * other_imag,
                real_part * other_imag + imaginary * other_real,
            ],
            axis=0,
        )
        product_spectra[index] = apply_table(inverse_ref, index, product)

    def first_back(step, top):
        start = pl.multiple_of(step * 8, 8)
        for slab, value in enumerate(real_values(get_spectrum(product_spectra, start, 8))):
            place = pl.ds(slab * width + start, 8)
            whole = value + gain * signal[place]
            response[place] = whole
            top = jnp.maximum(top, jnp.abs(whole))
        return top

    nothing = jnp.zeros((8, LANES), jnp.float32)
    top = lax.fori_loop(0, width // 8, first_back, nothing)
    response_top = jnp.max(top, axis=0, keepdims=True)
    response_bend = bend_of(response_top)

    def step_hop(step):
        return devices // 2 + (step + 1) // 2 * (1 - 2 * lax.rem(step, 2))

    def pack_conv(peer):
        start = pl.multiple_of(peer * rows, rows)
        folded = jnp.where(
            low_lanes((width, LANES)),
            response[pl.ds(start, width)],
            response[pl.ds(start + width, width)],
        )
        send_conv[peer] = encode(folded, response_bend).astype(jnp.bfloat16)

    def step_conv(step, carry):
        hop = step_hop(step)
        peer = peer_at(hop)
        pack_conv(peer)
        copy_to(4, hop, send_conv.at[peer], recv_conv.at[me], peer).start()
        return carry

    lax.fori_loop(0, devices - 1, step_conv, 0)
    pack_conv(me)
    keeps = [
        pltpu.make_async_copy(source, target.at[me], keep_sem.at[index])
        for index, (source, target) in enumerate(
            (
                (send_conv.at[me], recv_conv),
                (send_back.at[me], recv_back),
                (send_sums, recv_sums),
            )
        )
    ]
    keeps[0].start()

    wait_from(1, send_second, recv_second)
    open_rim(second_rim, recv_second)

    def shorten_second(slab, carry):
        start = pl.multiple_of(slab * width, width)
        total = filtered(second_rim, second_taps, start)
        total = total * swap(total)
        upstream[pl.ds(start, width)] = total
        return carry + jnp.sum(
            (total * signal[pl.ds(start, width)]).reshape(-1, 8, LANES), axis=0
        )

    gain_sum = lax.fori_loop(0, slabs, shorten_second, nothing)

    def second_spectrum(step, carry):
        start = pl.multiple_of(step * 8, 8)
        values = [upstream[pl.ds(slab * width + start, 8)] for slab in range(slabs)]
        put_spectrum(product_spectra, real_spectrum(values), start, 8)
        return carry

    lax.fori_loop(0, width // 8, second_spectrum, 0)

    for index in range(slabs // 2 + 1):
        found = apply_table(forward_ref, index, product_spectra[index])
        real_part, imaginary = found[:width], found[width:]
        other_real = swap(signal_spectra[index, :width])
        other_imag = swap(signal_spectra[index, width:])
        product = jnp.concatenate(
            [
                real_part * other_real + imaginary * other_imag,
                imaginary * other_real - real_part * other_imag,
            ],
            axis=0,
        )
        product_spectra[index] = apply_table(inverse_ref, index, product)

    low_gain = jnp.where(low_lanes((1, LANES)), gain, 0.0)

    def second_back(step, top):
        start = pl.multiple_of(step * 8, 8)
        for slab, value in enumerate(real_values(get_spectrum(product_spectra, start, 8))):
            place = pl.ds(slab * width + start, 8)
            whole = value + low_gain * upstream[place]
            back[place] = whole
            top = jnp.maximum(top, jnp.abs(whole))
        return top

    top = lax.fori_loop(0, width // 8, second_back, nothing)
    back_top = jnp.max(top, axis=0, keepdims=True)
    back_bend = bend_of(back_top)
    rim_bend = jnp.where(low_lanes((1, LANES)), back_bend, response_bend)

    def pack_back(peer):
        start = pl.multiple_of(peer * rows, rows)
        send_back[peer, 0:rows] = encode(back[pl.ds(start, rows)], back_bend).astype(jnp.bfloat16)
        places = (
            lax.rem(start + extent - RIM, extent),
            lax.rem(start + rows, extent),
        )
        ends = []
        for place in places:
            here = pl.ds(pl.multiple_of(place, RIM), RIM)
            ends.append(jnp.where(low_lanes((RIM, LANES)), back[here], response[here]))
        send_back[peer, rows : rows + 2 * RIM] = encode(
            jnp.concatenate(ends, axis=0), rim_bend
        ).astype(jnp.bfloat16)

    def step_back(step, carry):
        hop = step_hop(step)
        peer = peer_at(hop)
        pack_back(peer)
        copy_to(5, hop, send_back.at[peer], recv_back.at[me], peer).start()
        return carry

    lax.fori_loop(0, devices - 1, step_back, 0)
    pack_back(me)
    keeps[1].start()

    def add_sums(slab, sums):
        sums = list(sums)
        start = pl.multiple_of(slab * width, width)
        here = pl.ds(start, width)
        low = low_lanes((width, LANES))
        grad = back[here]
        grad = jnp.where(low, grad, swap(grad)) * swap(first_short[here])
        near_first = first_rim[pl.ds(start, width + 2 * RIM)]
        near_second = second_rim[pl.ds(start, width + 2 * RIM)]
        other = response[here] * swap(near_second[RIM : RIM + width])
        for tap in range(span):
            inner = slice(RIM + tap - margin, RIM + tap - margin + width)
            for which, (grads, near) in enumerate(((grad, near_first), (other, near_second))):
                sums[which * span + tap] = sums[which * span + tap] + jnp.sum(
                    (grads * near[inner]).reshape(-1, 8, LANES), axis=0
                )
        return tuple(sums)

    sums = lax.fori_loop(0, slabs, add_sums, (nothing,) * (2 * span))
    sums = [factor * jnp.sum(value, axis=0, keepdims=True) for value in sums + (gain_sum,)]
    middle = (span + 1) // 2
    for index in range(span):
        send_sums[index : index + 1] = sums[index]
    for index in range(span, span + middle):
        send_sums[index : index + 1] = join(sums[index], sums[index + middle], 0)
    send_sums[span + middle : span + middle + 1] = response_top
    send_sums[span + middle + 1 : span + middle + 2] = back_top
    for hop in hops:
        copy_to(6, hop, send_sums, recv_sums.at[me], peer_at(hop)).start()
    keeps[2].start()

    for copy in rim_copies:
        copy.wait()
    for stream in range(4):
        around[stream, 0:RIM] = jnp.zeros((RIM, channels), jnp.float32)
        around[stream, rows + 3 * RIM :] = jnp.zeros((RIM, channels), jnp.float32)
        half = slice((stream % 2) * RIM, (stream % 2 + 1) * RIM)
        before, after = wide(recv_rim[1, stream // 2])[half], wide(recv_rim[0, stream // 2])[half]
        around[stream, RIM : 2 * RIM] = before
        around[stream, rows + 2 * RIM : rows + 3 * RIM] = after
        source = cotangent_ref[...] if stream == 3 else projected_ref[stream]
        around[stream, 2 * RIM : 2 * RIM + rows] = wide(source)
    kept[3] = around[3, RIM : rows + 3 * RIM]

    def own_short(step, carry):
        stream, tile = step // tiles, lax.rem(step, tiles)
        lanes = pl.ds(pl.multiple_of(tile * LANES, LANES), LANES)
        taps = taps_ref[stream, :, lanes]
        for part in range(2):
            count = width + RIM
            total = jnp.zeros((count, LANES), jnp.float32)
            for tap in range(span):
                low = part * count + RIM + tap - margin
                total = total + taps[tap : tap + 1] * around[stream, low : low + count, lanes]
            kept[stream, part * count : (part + 1) * count, lanes] = total
        return carry

    lax.fori_loop(0, 3 * tiles, own_short, 0)
    keeping = pltpu.make_async_copy(kept, kept_out, keep_sem.at[3])
    keeping.start()
    passing = pltpu.make_async_copy(taps_ref, taps_out, keep_sem.at[4])
    passing.start()

    keeping.wait()
    passing.wait()
    for keep in keeps:
        keep.wait()
    wait_from(4, send_conv, recv_conv)
    wait_from(5, send_back, recv_back)
    for hop in hops:
        copy_to(6, hop, send_sums, recv_sums.at[source_at(hop)], peer_at(hop)).wait()


def unpack_kernel(*refs):
    packed, results, held, refs = refs[:5], refs[5:10], refs[10:15], refs[15:]
    output_ref, streams_ref, filter_grad_ref, taps_grad_ref, gain_grad_ref = refs[:5]
    recv_conv, recv_back, recv_sums, kept, taps_ref = held
    grads, load_sem, store_sem = refs[5:]
    loads = [pltpu.make_async_copy(packed[i], held[i], load_sem.at[i]) for i in range(5)]
    stores = [pltpu.make_async_copy(refs[i], results[i], store_sem.at[i]) for i in range(5)]
    for load in loads:
        load.start()
    tiles = recv_conv.shape[0] // 2
    rows = output_ref.shape[0]
    span = taps_grad_ref.shape[1]
    margin = span // 2
    middle = (span + 1) // 2
    for load in loads:
        load.wait()
    for tile in range(tiles):
        lanes = slice(tile * LANES, (tile + 1) * LANES)
        tops = [recv_sums[2 * tile + half] for half in range(2)]
        low_part, high_part = split(tops[0], tops[1])
        taps_grad_ref[1, :, lanes] = low_part[0:span]
        taps_grad_ref[2, :, lanes] = high_part[0:span]
        taps_grad_ref[0, :middle, lanes] = low_part[span : span + middle]
        taps_grad_ref[0, middle:, lanes] = high_part[span : 2 * span - middle]
        gain_grad_ref[:, lanes] = high_part[2 * span - middle : 2 * span - middle + 1]
        response_top, back_top = [
            [top[span + middle + i : span + middle + i + 1] for top in tops] for i in range(2)
        ]
        pieces = split(
            *(decode(wide(recv_conv[2 * tile + i]), response_top[i]) for i in range(2))
        )
        found = [
            decode(wide(recv_back[2 * tile + i, 0:rows]), back_top[i]) for i in range(2)
        ]
        grad, filter_grad = split(*found)
        filter_grad_ref[:, lanes] = filter_grad
        if tile == tiles - 1:
            for index in (2, 3, 4):
                stores[index].start()
        low = low_lanes((1, LANES))
        rims = [
            decode(
                wide(recv_back[2 * tile + i, rows : rows + 2 * RIM]),
                jnp.where(low, back_top[i], response_top[i]),
            )
            for i in range(2)
        ]
        grad_rim, response_rim = split(*rims)
        response = jnp.concatenate(
            [response_rim[:RIM], pieces[0], pieces[1], response_rim[RIM:]], axis=0
        )
        grad = jnp.concatenate([grad_rim[:RIM], grad, grad_rim[RIM:]], axis=0)
        output_ref[:, lanes] = (
            response[RIM : RIM + rows] * kept[0, RIM : RIM + rows, lanes]
        ).astype(jnp.bfloat16)
        if tile == tiles - 1:
            stores[0].start()
        grads[0] = response * kept[3, :, lanes]
        grads[1] = grad * kept[2, :, lanes]
        grads[2] = grad * kept[1, :, lanes]
        for stream in range(3):
            taps = taps_ref[stream, :, lanes]
            total = jnp.zeros((rows, LANES), jnp.float32)
            for tap in range(span):
                first = RIM + margin - tap
                total = total + taps[tap : tap + 1] * grads[stream, first : first + rows]
            streams_ref[stream, :, lanes] = total.astype(jnp.bfloat16)
    stores[1].start()
    for store in stores:
        store.wait()


def halved(table):
    coarse = table.astype(ml_dtypes.bfloat16)
    rest = (table - coarse.astype(np.float32)).astype(ml_dtypes.bfloat16)
    return np.concatenate([coarse, rest], axis=2)


def packed_body(devices, projected, long_filter, short_kernel, skip_gain, cotangent):
    rows, channels = long_filter.shape
    span = short_kernel.shape[1]
    extent = rows * devices
    slabs = 2 * devices
    width = rows // 2
    tables = [halved(table) for table in fine_tables(slabs, width)]
    sums_rows = span + (span + 1) // 2 + 2
    block = (devices, rows, LANES)
    half_block = (devices, width, LANES)
    longer = (devices, rows + 2 * RIM, LANES)
    narrow, full = jnp.bfloat16, jnp.float32
    arguments = (projected, cotangent, long_filter, short_kernel, skip_gain[None], *tables)
    in_hbm = pl.BlockSpec(memory_space=pltpu.HBM)
    anywhere = pl.BlockSpec(memory_space=pl.ANY)
    arguments = [pltpu.with_memory_space_constraint(value, pltpu.HBM) for value in arguments]
    packed_shapes = (
        jax.ShapeDtypeStruct(half_block, narrow),
        jax.ShapeDtypeStruct(longer, narrow),
        jax.ShapeDtypeStruct((devices, sums_rows, LANES), full),
        jax.ShapeDtypeStruct((4, rows + 2 * RIM, channels), full),
        jax.ShapeDtypeStruct(short_kernel.shape, full),
    )
    out_shapes = (
        jax.ShapeDtypeStruct((rows, channels), narrow),
        jax.ShapeDtypeStruct((3, rows, channels), narrow),
        jax.ShapeDtypeStruct((rows, channels), full),
        jax.ShapeDtypeStruct(short_kernel.shape, full),
        jax.ShapeDtypeStruct((1, channels), full),
    )
    packed = pl.pallas_call(
        functools.partial(layer_kernel, devices),
        out_shape=packed_shapes,
        in_specs=[in_hbm] * 7,
        out_specs=(anywhere,) * 5,
        scratch_shapes=[
            *(pltpu.VMEM(value.shape, value.dtype) for value in arguments),
            pltpu.VMEM(block, narrow),
            pltpu.VMEM(block, narrow),
            pltpu.VMEM(block, narrow),
            pltpu.VMEM(block, narrow),
            pltpu.VMEM(half_block, narrow),
            pltpu.VMEM(half_block, narrow),
            pltpu.VMEM((devices, 1, LANES), full),
            pltpu.VMEM((devices, 1, LANES), full),
            pltpu.VMEM((2, 2, 2 * RIM, channels), narrow),
            pltpu.VMEM((2, 2, 2 * RIM, channels), narrow),
            pltpu.VMEM(half_block, narrow),
            pltpu.VMEM(longer, narrow),
            pltpu.VMEM((sums_rows, LANES), full),
            pltpu.VMEM((4, rows + 4 * RIM, channels), full),
            pltpu.VMEM((4, rows + 2 * RIM, channels), full),
            pltpu.VMEM((extent + 2 * RIM, LANES), full),
            pltpu.VMEM((extent + 2 * RIM, LANES), full),
            *[pltpu.VMEM((extent, LANES), full)] * 5,
            *[pltpu.VMEM((slabs // 2 + 1, rows, LANES), full)] * 2,
            pltpu.SemaphoreType.DMA((len(arguments),)),
            pltpu.SemaphoreType.DMA((5,)),
            pltpu.SemaphoreType.DMA((8, devices)),
            pltpu.SemaphoreType.DMA((8, devices)),
        ],
        compiler_params=pltpu.CompilerParams(
            collective_id=0, has_side_effects=True, vmem_limit_bytes=LIMIT
        ),
    )(*arguments)
    found = pl.pallas_call(
        unpack_kernel,
        out_shape=out_shapes,
        in_specs=[anywhere] * 5,
        out_specs=(in_hbm,) * 5,
        scratch_shapes=[
            *(pltpu.VMEM(value.shape, value.dtype) for value in packed_shapes),
            *(pltpu.VMEM(value.shape, value.dtype) for value in out_shapes),
            pltpu.VMEM((3, rows + 2 * RIM, LANES), full),
            pltpu.SemaphoreType.DMA((5,)),
            pltpu.SemaphoreType.DMA((5,)),
        ],
        compiler_params=pltpu.CompilerParams(vmem_limit_bytes=LIMIT),
    )(*packed)
    return (*found[:4], found[4][0])


def with_halo(block, sides, width):
    for axis, dim in sides:
        count = lax.axis_size(axis)
        forward = [(i, i + 1) for i in range(count - 1)]
        forward.append((count - 1, 0))
        backward = [(target, source) for source, target in forward]
        low = lax.ppermute(
            lax.slice_in_dim(block, block.shape[dim] - width, None, axis=dim), axis, forward
        )
        high = lax.ppermute(lax.slice_in_dim(block, 0, width, axis=dim), axis, backward)
        block = jnp.concatenate([low, block, high], axis=dim)
    return block


def dft_tables(extent):
    indices = jnp.arange(extent, dtype=jnp.int32)
    angles = (indices[:, None] * indices[None, :] % extent).astype(jnp.float32) * (
        2.0 * math.pi / extent
    )
    return (jnp.cos(angles), jnp.sin(angles))


def apply_along(matrix, signal, axis_dim):
    letters = "wxyz"
    target = letters[:axis_dim] + "k" + letters[axis_dim + 1 :]
    return jnp.einsum(
        "k" + letters[axis_dim] + "," + letters + "->" + target, matrix, signal, precision=HIGHEST
    )


def forward_section(real_part, imaginary, axis_dim):
    cosine, sine_table = dft_tables(real_part.shape[axis_dim])
    out_real = apply_along(cosine, real_part, axis_dim)
    out_imag = -apply_along(sine_table, real_part, axis_dim)
    if imaginary is not None:
        out_real = out_real + apply_along(sine_table, imaginary, axis_dim)
        out_imag = out_imag + apply_along(cosine, imaginary, axis_dim)
    return (out_real, out_imag)


def inverse_section(real_part, imaginary, axis_dim, keep_imag):
    cosine, sine_table = dft_tables(real_part.shape[axis_dim])
    out_real = apply_along(cosine, real_part, axis_dim) - apply_along(
        sine_table, imaginary, axis_dim
    )
    if keep_imag:
        return (
            out_real,
            apply_along(sine_table, real_part, axis_dim) + apply_along(cosine, imaginary, axis_dim),
        )
    return (out_real, None)


def twist(real_part, imaginary, angles, sign_factor):
    cosine = jnp.cos(angles)
    sine_table = jnp.sin(angles)
    return (
        real_part * cosine + sign_factor * imaginary * sine_table,
        imaginary * cosine - sign_factor * real_part * sine_table,
    )


def twiddle(low_index, high_index, extent):
    return (low_index * high_index % extent).astype(jnp.float32) * (2.0 * math.pi / extent)


def block_angles(devices, portion, extent):
    low_index = jnp.arange(devices, dtype=jnp.int32)[None, :, None, None]
    high_index = (lax.axis_index("seq") * portion + jnp.arange(portion, dtype=jnp.int32))[
        None, None, :, None
    ]
    return twiddle(low_index, high_index, extent)


def sequence_forward(signals, extent):
    devices = lax.axis_size("seq")
    portion = signals.shape[1] // devices
    columns = lax.all_to_all(signals[:, None], "seq", split_axis=2, concat_axis=1, tiled=True)
    real_part, imaginary = forward_section(columns, None, 1)
    real_part, imaginary = twist(real_part, imaginary, block_angles(devices, portion, extent), 1.0)
    spread = (
        lax.all_to_all(real_part, "seq", split_axis=1, concat_axis=2, tiled=True),
        lax.all_to_all(imaginary, "seq", split_axis=1, concat_axis=2, tiled=True),
    )
    return forward_section(spread[0], spread[1], 2)


def sequence_inverse(real_part, imaginary, extent):
    devices = lax.axis_size("seq")
    portion = real_part.shape[2] // devices
    real_part, imaginary = inverse_section(real_part, imaginary, 2, True)
    gathered = (
        lax.all_to_all(real_part, "seq", split_axis=2, concat_axis=1, tiled=True),
        lax.all_to_all(imaginary, "seq", split_axis=2, concat_axis=1, tiled=True),
    )
    real_part, imaginary = twist(
        gathered[0], gathered[1], block_angles(devices, portion, extent), -1.0
    )
    pieces = inverse_section(real_part, imaginary, 1, False)[0] * (1.0 / extent)
    blocks = lax.all_to_all(pieces, "seq", split_axis=1, concat_axis=2, tiled=True)
    return blocks[:, 0]


def body(projected, long_filter, short_kernel, skip_gain, cotangent):
    rows_here = projected.shape[1]
    extent = rows_here * lax.axis_size("seq")
    factor = 1.0 / math.sqrt(extent)
    kernel_span = short_kernel.shape[1]
    margin = kernel_span // 2
    padded = with_halo(projected, (("seq", 1),), margin)
    shorts = jnp.zeros(projected.shape, jnp.float32)
    for offset in range(kernel_span):
        shorts = shorts + short_kernel[:, offset][:, None, :] * padded[
            :, offset : offset + rows_here
        ].astype(jnp.float32)
    gated_signal = shorts[1] * shorts[2]
    transform, restore = (sequence_forward, sequence_inverse)
    upstream = cotangent.astype(jnp.float32)
    grad_response = upstream * shorts[0]
    spec_real, spec_imag = transform(jnp.stack([gated_signal, long_filter]), extent)
    gated_real, gated_imag = (spec_real[0], spec_imag[0])
    filter_real, filter_imag = (spec_real[1] * factor, spec_imag[1] * factor)
    product_real = filter_real * gated_real - filter_imag * gated_imag
    product_imag = filter_real * gated_imag + filter_imag * gated_real
    convolved = restore(product_real[None], product_imag[None], extent)[0]
    upstream_real, upstream_imag = transform(grad_response[None], extent)
    upstream_real, upstream_imag = (upstream_real[0], upstream_imag[0])
    back_real = jnp.stack(
        [
            filter_real * upstream_real + filter_imag * upstream_imag,
            gated_real * upstream_real + gated_imag * upstream_imag,
        ]
    )
    back_imag = jnp.stack(
        [
            filter_real * upstream_imag - filter_imag * upstream_real,
            gated_real * upstream_imag - gated_imag * upstream_real,
        ]
    )
    restored = restore(back_real, back_imag, extent)
    grad_gated = restored[0] + skip_gain * grad_response
    filter_grad = restored[1] * factor
    response = convolved + skip_gain * gated_signal
    layer_output = (response * shorts[0]).astype(jnp.bfloat16)
    grad_shorts = jnp.stack([upstream * response, grad_gated * shorts[2], grad_gated * shorts[1]])
    rimmed = with_halo(grad_shorts, (("seq", 1),), margin)
    stream_sum = jnp.zeros(grad_shorts.shape, jnp.float32)
    kernel_terms = []
    for offset in range(kernel_span):
        start_row = 2 * margin - offset
        stream_sum = (
            stream_sum
            + short_kernel[:, offset][:, None, :] * rimmed[:, start_row : start_row + rows_here]
        )
        kernel_terms.append(
            jnp.sum(
                grad_shorts * padded[:, offset : offset + rows_here].astype(jnp.float32), axis=1
            )
        )
    kernel_part = jnp.stack(kernel_terms, axis=1)
    skip_part = jnp.sum(grad_response * gated_signal, axis=0)
    kernel_total, skip_total = lax.psum((kernel_part, skip_part), "seq")
    return (
        layer_output,
        stream_sum.astype(jnp.bfloat16),
        filter_grad,
        kernel_total * factor,
        skip_total * factor,
    )


def solution(mesh):
    placed = (
        P(None, ("groups", "seq"), "chan"),
        P(("groups", "seq"), "chan"),
        P(None, None, "chan"),
        P("chan"),
        P(("groups", "seq"), "chan"),
    )
    devices = mesh.shape["seq"]

    def run(projected, *others):
        rows, channels = projected.shape[1:]
        if channels == HALF * devices and rows == LANES and devices & (devices - 1) == 0:
            return packed_body(devices, projected, *others)
        return body(projected, *others)

    return jax.shard_map(
        run,
        mesh=mesh,
        in_specs=placed,
        out_specs=(
            P(("groups", "seq"), "chan"),
            P(None, ("groups", "seq"), "chan"),
            P(("groups", "seq"), "chan"),
            P("groups", None, "chan"),
            P(("groups", "chan")),
        ),
        check_vma=False,
    )
```

```python
import functools
import math

import jax
import jax.numpy as jnp
import ml_dtypes
import numpy as np
from jax import lax
from jax.experimental import pallas as pl
from jax.experimental.pallas import tpu as pltpu
from jax.sharding import PartitionSpec as P

HIGHEST = lax.Precision.HIGHEST
LANES = 128
HALF = LANES // 2
RIM = 8
LIMIT = 20 * 1024 * 1024
BEND = 15.0
SPREAD = 251.0 * math.log(2.0) / math.log(1.0 + BEND)
LOWEST = -125.0 * math.log(2.0)
TINY = 1e-35


def turned(value, step, extent):
    real_part, imaginary = value
    step = step % extent
    if step == 0:
        return value
    if 2 * step == extent:
        return (-real_part, None if imaginary is None else -imaginary)
    if 4 * step == extent:
        return (None if imaginary is None else -imaginary, real_part)
    if 4 * step == 3 * extent:
        return (imaginary, -real_part)
    cosine = math.cos(2.0 * math.pi * step / extent)
    sine = math.sin(2.0 * math.pi * step / extent)
    if imaginary is None:
        return (real_part * cosine, real_part * sine)
    return (real_part * cosine - imaginary * sine, imaginary * cosine + real_part * sine)


def part_sum(left, right, sign):
    if right is None:
        return left
    if left is None:
        return right if sign > 0 else -right
    return left + right if sign > 0 else left - right


def real_spectrum(values):
    extent = len(values)
    if extent == 2:
        return [(values[0] + values[1], None), (values[0] - values[1], None)]
    even, odd = real_spectrum(values[0::2]), real_spectrum(values[1::2])
    half = extent // 2

    def entry(spectrum, index):
        index = index % half
        if 2 * index <= half:
            return spectrum[index]
        real_part, imaginary = spectrum[half - index]
        return (real_part, None if imaginary is None else -imaginary)

    found = []
    for index in range(half + 1):
        left, right = entry(even, index), turned(entry(odd, index), -index, extent)
        found.append((part_sum(left[0], right[0], 1), part_sum(left[1], right[1], 1)))
    return found


def real_values(spectrum):
    extent = 2 * (len(spectrum) - 1)
    if extent == 2:
        first, last = spectrum[0][0], spectrum[1][0]
        return [first + last, first - last]
    half = extent // 2
    even, odd = [], []
    for index in range(half // 2 + 1):
        real_part, imaginary = spectrum[index]
        if 2 * index == half:
            even.append((2.0 * real_part, None))
            odd.append((-2.0 * imaginary, None))
            continue
        other_real, other_imag = spectrum[half - index]
        even.append(
            (real_part + other_real, part_sum(imaginary, other_imag, -1))
        )
        odd.append(
            turned(
                (real_part - other_real, part_sum(imaginary, other_imag, 1)), index, extent
            )
        )
    found = [None] * extent
    found[0::2] = real_values(even)
    found[1::2] = real_values(odd)
    return found


def fine_tables(slabs, width):
    extent = slabs * width
    coarse = np.arange(slabs // 2 + 1)[:, None, None]
    fine = np.arange(width)[None, :, None]
    place = np.arange(width)[None, None, :]
    angles = ((coarse + slabs * fine) * place % extent) * (2.0 * np.pi / extent)
    cosine, sine = np.cos(angles), np.sin(angles)
    table = np.concatenate(
        [np.concatenate([cosine, sine], 2), np.concatenate([-sine, cosine], 2)], 1
    )
    inverse = np.swapaxes(table, 1, 2) / (extent * math.sqrt(extent))
    return table.astype(np.float32), inverse.astype(np.float32)


def low_lanes(shape):
    return lax.broadcasted_iota(jnp.int32, shape, len(shape) - 1) < HALF


def swap(value):
    return pltpu.roll(value, HALF, 1)


def wide(value):
    return value.astype(jnp.float32)


def join(first, second, parity):
    low = low_lanes(first.shape)
    if parity == 0:
        return jnp.where(low, first, swap(second))
    return jnp.where(low, swap(first), second)


def split(first, second):
    return join(first, second, 0), join(first, second, 1)


def bend_of(top):
    return jnp.where(top > TINY, BEND / jnp.maximum(top, TINY), 0.0)


def encode(value, bend):
    size = jnp.exp(SPREAD * jnp.log(1.0 + jnp.abs(value) * bend) + LOWEST)
    return jnp.where(value < 0.0, -size, size)


def decode(code, top):
    size = (jnp.exp((jnp.log(jnp.abs(code)) - LOWEST) * (1.0 / SPREAD)) - 1.0) * (top / BEND)
    return jnp.where(code < 0.0, -size, size)


def halves(value):
    coarse = value.astype(jnp.bfloat16)
    return coarse, (value - wide(coarse)).astype(jnp.bfloat16)


def apply_table(table, index, value):
    coarse, rest = halves(value)
    depth = coarse.shape[0]
    return jnp.dot(
        table[index],
        jnp.concatenate([coarse, coarse], axis=0),
        preferred_element_type=jnp.float32,
    ) + jnp.dot(table[index, :, :depth], rest, preferred_element_type=jnp.float32)


def layer_kernel(
    devices,
    projected_in,
    cotangent_in,
    filter_in,
    taps_in,
    gain_in,
    forward_in,
    inverse_in,
    recv_conv,
    recv_back,
    recv_sums,
    kept_out,
    taps_out,
    projected_ref,
    cotangent_ref,
    filter_ref,
    taps_ref,
    gain_ref,
    forward_ref,
    inverse_ref,
    send_first,
    recv_first,
    send_second,
    recv_second,
    send_filter,
    recv_filter,
    send_top,
    recv_top,
    send_rim,
    recv_rim,
    send_conv,
    send_back,
    send_sums,
    around,
    kept,
    first_rim,
    second_rim,
    first_short,
    signal,
    upstream,
    response,
    back,
    signal_spectra,
    product_spectra,
    load_sem,
    keep_sem,
    send_sem,
    recv_sem,
):
    hops = [(devices // 2 + (-1) ** i * ((i + 1) // 2)) for i in range(devices - 1)]
    arguments = (projected_in, cotangent_in, filter_in, taps_in, gain_in, forward_in, inverse_in)
    held = (
        projected_ref,
        cotangent_ref,
        filter_ref,
        taps_ref,
        gain_ref,
        forward_ref,
        inverse_ref,
    )
    loads = [
        pltpu.make_async_copy(source, target, load_sem.at[index])
        for index, (source, target) in enumerate(zip(arguments, held))
    ]
    for load in loads:
        load.start()
    rows, channels = cotangent_ref.shape
    tiles = channels // LANES
    span = taps_ref.shape[1]
    margin = span // 2
    width = rows // 2
    slabs = 2 * devices
    extent = rows * devices
    factor = 1.0 / math.sqrt(extent)
    me = lax.axis_index("seq")
    odd = lax.rem(me, 2) == 1

    def copy_to(kind, hop, source, target, peer):
        return pltpu.make_async_remote_copy(
            src_ref=source,
            dst_ref=target,
            send_sem=send_sem.at[kind, hop],
            recv_sem=recv_sem.at[kind, hop],
            device_id={"seq": peer},
            device_id_type=pl.DeviceIdType.MESH,
        )

    def peer_at(hop):
        return lax.rem(me + hop, devices)

    def source_at(hop):
        return lax.rem(me + devices - hop, devices)

    barrier = pltpu.get_barrier_semaphore()
    for hop in hops:
        pl.semaphore_signal(
            barrier, inc=1, device_id={"seq": peer_at(hop)}, device_id_type=pl.DeviceIdType.MESH
        )

    loads[0].wait()
    loads[1].wait()

    def lanes_of(peer):
        return pl.ds(pl.multiple_of((peer // 2) * LANES, LANES), LANES)

    def join_for(peer, first, second):
        flip = lax.rem(peer, 2) == 1
        return jnp.where(
            low_lanes(first.shape),
            jnp.where(flip, swap(first), first),
            jnp.where(flip, second, swap(second)),
        ).astype(jnp.bfloat16)

    def pack_first(peer, target):
        lanes = lanes_of(peer)
        target[...] = join_for(
            peer, wide(projected_ref[1, :, lanes]), wide(projected_ref[2, :, lanes])
        )

    def pack_second(peer, target):
        lanes = lanes_of(peer)
        target[...] = join_for(
            peer, wide(projected_ref[0, :, lanes]), wide(cotangent_ref[:, lanes])
        )

    for side, start in enumerate((0, rows - 2 * RIM)):
        part = slice(0, RIM) if side == 0 else slice(RIM, 2 * RIM)
        ends = [wide(projected_ref[s, start : start + 2 * RIM])[part] for s in range(3)]
        ends.append(wide(cotangent_ref[start : start + 2 * RIM])[part])
        for pair in range(2):
            send_rim[side, pair] = jnp.concatenate(ends[2 * pair : 2 * pair + 2], axis=0).astype(
                jnp.bfloat16
            )
    rim_copies = [
        copy_to(7, hop, send_rim.at[side], recv_rim.at[side], peer_at(hop))
        for side, hop in enumerate((devices - 1, 1))
    ]
    for place, hop in enumerate(hops):
        peer = peer_at(hop)
        pack_first(peer, send_first.at[peer])
        if place == 0:
            pl.semaphore_wait(barrier, devices - 1)
        copy_to(0, hop, send_first.at[peer], recv_first.at[me], peer).start()

    loads[2].wait()
    for tile in range(tiles):
        lanes = slice(tile * LANES, (tile + 1) * LANES)
        whole = filter_ref[:, lanes]
        top = jnp.max(jnp.abs(whole), axis=0, keepdims=True)
        coded = encode(whole, bend_of(top))
        for half in range(2):
            send_filter[2 * tile + half] = join(coded[:width], coded[width:], half).astype(
                jnp.bfloat16
            )
            send_top[2 * tile + half] = join(top, top, half)
    for hop in hops:
        peer = peer_at(hop)
        copy_to(2, hop, send_filter.at[peer], recv_filter.at[me], peer).start()
        copy_to(3, hop, send_top.at[peer], recv_top.at[me], peer).start()
    for hop in hops:
        peer = peer_at(hop)
        pack_second(peer, send_second.at[peer])
        copy_to(1, hop, send_second.at[peer], recv_second.at[me], peer).start()
    for copy in rim_copies:
        copy.start()
    pack_first(me, recv_first.at[me])
    pack_second(me, recv_second.at[me])
    recv_filter[me] = send_filter[me]
    recv_top[me] = send_top[me]

    for load in loads[3:5]:
        load.wait()
    own = pl.ds(pl.multiple_of((me // 2) * LANES, LANES), LANES)

    def own_pair(first, second):
        return jnp.where(odd, join(first, second, 1), join(first, second, 0))

    gate_taps, left_taps, right_taps = [taps_ref[s, :, own] for s in range(3)]
    first_taps = own_pair(left_taps, right_taps)
    centre = wide(lax.broadcasted_iota(jnp.int32, (span, LANES), 0) == margin)
    second_taps = jnp.where(low_lanes((span, LANES)), own_pair(gate_taps, gate_taps), centre)
    own_gain = gain_ref[:, own]
    gain = own_pair(own_gain, own_gain)

    def wait_from(kind, source, target):
        for hop in hops:
            copy_to(
                kind, hop, source.at[peer_at(hop)], target.at[source_at(hop)], peer_at(hop)
            ).wait()

    def close_rim(rim):
        rim[0:RIM] = rim[extent : extent + RIM]
        rim[extent + RIM : extent + 2 * RIM] = rim[RIM : 2 * RIM]

    def open_rim(rim, received):
        for block in range(devices):
            rim[RIM + block * rows : RIM + (block + 1) * rows] = wide(received[block])
        close_rim(rim)

    def filtered(rim, taps, start):
        near = rim[pl.ds(start, width + 2 * RIM)]
        total = jnp.zeros((width, LANES), jnp.float32)
        for tap in range(span):
            low = RIM + tap - margin
            total = total + taps[tap : tap + 1] * near[low : low + width]
        return total

    wait_from(0, send_first, recv_first)
    open_rim(first_rim, recv_first)

    def shorten_first(slab, carry):
        start = pl.multiple_of(slab * width, width)
        total = filtered(first_rim, first_taps, start)
        first_short[pl.ds(start, width)] = total
        signal[pl.ds(start, width)] = total * swap(total)
        return carry

    lax.fori_loop(0, slabs, shorten_first, 0)
    for load in loads[5:]:
        load.wait()
    wait_from(2, send_filter, recv_filter)
    wait_from(3, send_top, recv_top)

    def put_spectrum(spectra, found, start, count):
        for index, (real_part, imaginary) in enumerate(found):
            if imaginary is None:
                imaginary = jnp.zeros_like(real_part)
            spectra[index, pl.ds(start, count)] = real_part
            spectra[index, pl.ds(width + start, count)] = imaginary

    def get_spectrum(spectra, start, count):
        found = []
        for index in range(slabs // 2 + 1):
            imaginary = None
            if 0 < index < slabs // 2:
                imaginary = spectra[index, pl.ds(width + start, count)]
            found.append((spectra[index, pl.ds(start, count)], imaginary))
        return found

    def first_spectrum(step, carry):
        start = pl.multiple_of(step * 16, 16)
        low = low_lanes((16, LANES))
        values = []
        for block in range(devices):
            found = decode(wide(recv_filter[block, pl.ds(start, 16)]), recv_top[block])
            for half in range(2):
                here = signal[pl.ds(block * rows + half * width + start, 16)]
                values.append(jnp.where(low, here, swap(found) if half == 0 else found))
        put_spectrum(signal_spectra, real_spectrum(values), start, 16)
        return carry

    lax.fori_loop(0, width // 16, first_spectrum, 0)

    for index in range(slabs // 2 + 1):
        found = apply_table(forward_ref, index, signal_spectra[index])
        signal_spectra[index] = found
        real_part, imaginary = found[:width], found[width:]
        other_real, other_imag = swap(real_part), swap(imaginary)
        product = jnp.concatenate(
            [
                real_part * other_real - imaginary * other_imag,
                real_part * other_imag + imaginary * other_real,
            ],
            axis=0,
        )
        product_spectra[index] = apply_table(inverse_ref, index, product)

    def first_back(step, top):
        start = pl.multiple_of(step * 8, 8)
        for slab, value in enumerate(real_values(get_spectrum(product_spectra, start, 8))):
            place = pl.ds(slab * width + start, 8)
            whole = value + gain * signal[place]
            response[place] = whole
            top = jnp.maximum(top, jnp.abs(whole))
        return top

    nothing = jnp.zeros((8, LANES), jnp.float32)
    top = lax.fori_loop(0, width // 8, first_back, nothing)
    response_top = jnp.max(top, axis=0, keepdims=True)
    response_bend = bend_of(response_top)

    def step_hop(step):
        return devices // 2 + (step + 1) // 2 * (1 - 2 * lax.rem(step, 2))

    def pack_conv(peer):
        start = pl.multiple_of(peer * rows, rows)
        folded = jnp.where(
            low_lanes((width, LANES)),
            response[pl.ds(start, width)],
            response[pl.ds(start + width, width)],
        )
        send_conv[peer] = encode(folded, response_bend).astype(jnp.bfloat16)

    def step_conv(step, carry):
        hop = step_hop(step)
        peer = peer_at(hop)
        pack_conv(peer)
        copy_to(4, hop, send_conv.at[peer], recv_conv.at[me], peer).start()
        return carry

    lax.fori_loop(0, devices - 1, step_conv, 0)
    pack_conv(me)
    keeps = [
        pltpu.make_async_copy(source, target.at[me], keep_sem.at[index])
        for index, (source, target) in enumerate(
            (
                (send_conv.at[me], recv_conv),
                (send_back.at[me], recv_back),
                (send_sums, recv_sums),
            )
        )
    ]
    keeps[0].start()

    wait_from(1, send_second, recv_second)
    open_rim(second_rim, recv_second)

    def shorten_second(slab, carry):
        start = pl.multiple_of(slab * width, width)
        total = filtered(second_rim, second_taps, start)
        total = total * swap(total)
        upstream[pl.ds(start, width)] = total
        return carry + jnp.sum(
            (total * signal[pl.ds(start, width)]).reshape(-1, 8, LANES), axis=0
        )

    gain_sum = lax.fori_loop(0, slabs, shorten_second, nothing)

    def second_spectrum(step, carry):
        start = pl.multiple_of(step * 8, 8)
        values = [upstream[pl.ds(slab * width + start, 8)] for slab in range(slabs)]
        put_spectrum(product_spectra, real_spectrum(values), start, 8)
        return carry

    lax.fori_loop(0, width // 8, second_spectrum, 0)

    for index in range(slabs // 2 + 1):
        found = apply_table(forward_ref, index, product_spectra[index])
        real_part, imaginary = found[:width], found[width:]
        other_real = swap(signal_spectra[index, :width])
        other_imag = swap(signal_spectra[index, width:])
        product = jnp.concatenate(
            [
                real_part * other_real + imaginary * other_imag,
                imaginary * other_real - real_part * other_imag,
            ],
            axis=0,
        )
        product_spectra[index] = apply_table(inverse_ref, index, product)

    low_gain = jnp.where(low_lanes((1, LANES)), gain, 0.0)

    def second_back(step, top):
        start = pl.multiple_of(step * 8, 8)
        for slab, value in enumerate(real_values(get_spectrum(product_spectra, start, 8))):
            place = pl.ds(slab * width + start, 8)
            whole = value + low_gain * upstream[place]
            back[place] = whole
            top = jnp.maximum(top, jnp.abs(whole))
        return top

    top = lax.fori_loop(0, width // 8, second_back, nothing)
    back_top = jnp.max(top, axis=0, keepdims=True)
    back_bend = bend_of(back_top)
    rim_bend = jnp.where(low_lanes((1, LANES)), back_bend, response_bend)

    def pack_back(peer):
        start = pl.multiple_of(peer * rows, rows)
        send_back[peer, 0:rows] = encode(back[pl.ds(start, rows)], back_bend).astype(jnp.bfloat16)
        places = (
            lax.rem(start + extent - RIM, extent),
            lax.rem(start + rows, extent),
        )
        ends = []
        for place in places:
            here = pl.ds(pl.multiple_of(place, RIM), RIM)
            ends.append(jnp.where(low_lanes((RIM, LANES)), back[here], response[here]))
        send_back[peer, rows : rows + 2 * RIM] = encode(
            jnp.concatenate(ends, axis=0), rim_bend
        ).astype(jnp.bfloat16)

    def step_back(step, carry):
        hop = step_hop(step)
        peer = peer_at(hop)
        pack_back(peer)
        copy_to(5, hop, send_back.at[peer], recv_back.at[me], peer).start()
        return carry

    lax.fori_loop(0, devices - 1, step_back, 0)
    pack_back(me)
    keeps[1].start()

    def add_sums(slab, sums):
        sums = list(sums)
        start = pl.multiple_of(slab * width, width)
        here = pl.ds(start, width)
        low = low_lanes((width, LANES))
        grad = back[here]
        grad = jnp.where(low, grad, swap(grad)) * swap(first_short[here])
        near_first = first_rim[pl.ds(start, width + 2 * RIM)]
        near_second = second_rim[pl.ds(start, width + 2 * RIM)]
        other = response[here] * swap(near_second[RIM : RIM + width])
        for tap in range(span):
            inner = slice(RIM + tap - margin, RIM + tap - margin + width)
            for which, (grads, near) in enumerate(((grad, near_first), (other, near_second))):
                sums[which * span + tap] = sums[which * span + tap] + jnp.sum(
                    (grads * near[inner]).reshape(-1, 8, LANES), axis=0
                )
        return tuple(sums)

    sums = lax.fori_loop(0, slabs, add_sums, (nothing,) * (2 * span))
    sums = [factor * jnp.sum(value, axis=0, keepdims=True) for value in sums + (gain_sum,)]
    middle = (span + 1) // 2
    for index in range(span):
        send_sums[index : index + 1] = sums[index]
    for index in range(span, span + middle):
        send_sums[index : index + 1] = join(sums[index], sums[index + middle], 0)
    send_sums[span + middle : span + middle + 1] = response_top
    send_sums[span + middle + 1 : span + middle + 2] = back_top
    for hop in hops:
        copy_to(6, hop, send_sums, recv_sums.at[me], peer_at(hop)).start()
    keeps[2].start()

    for copy in rim_copies:
        copy.wait()
    for stream in range(4):
        around[stream, 0:RIM] = jnp.zeros((RIM, channels), jnp.float32)
        around[stream, rows + 3 * RIM :] = jnp.zeros((RIM, channels), jnp.float32)
        half = slice((stream % 2) * RIM, (stream % 2 + 1) * RIM)
        before, after = wide(recv_rim[1, stream // 2])[half], wide(recv_rim[0, stream // 2])[half]
        around[stream, RIM : 2 * RIM] = before
        around[stream, rows + 2 * RIM : rows + 3 * RIM] = after
        source = cotangent_ref[...] if stream == 3 else projected_ref[stream]
        around[stream, 2 * RIM : 2 * RIM + rows] = wide(source)
    kept[3] = around[3, RIM : rows + 3 * RIM]

    def own_short(step, carry):
        stream, tile = step // tiles, lax.rem(step, tiles)
        lanes = pl.ds(pl.multiple_of(tile * LANES, LANES), LANES)
        taps = taps_ref[stream, :, lanes]
        for part in range(2):
            count = width + RIM
            total = jnp.zeros((count, LANES), jnp.float32)
            for tap in range(span):
                low = part * count + RIM + tap - margin
                total = total + taps[tap : tap + 1] * around[stream, low : low + count, lanes]
            kept[stream, part * count : (part + 1) * count, lanes] = total
        return carry

    lax.fori_loop(0, 3 * tiles, own_short, 0)
    keeping = pltpu.make_async_copy(kept, kept_out, keep_sem.at[3])
    keeping.start()
    passing = pltpu.make_async_copy(taps_ref, taps_out, keep_sem.at[4])
    passing.start()

    keeping.wait()
    passing.wait()
    for keep in keeps:
        keep.wait()
    wait_from(4, send_conv, recv_conv)
    wait_from(5, send_back, recv_back)
    for hop in hops:
        copy_to(6, hop, send_sums, recv_sums.at[source_at(hop)], peer_at(hop)).wait()


def unpack_kernel(*refs):
    held, results, refs = refs[:5], refs[5:10], refs[10:]
    output_ref, streams_ref, filter_grad_ref, taps_grad_ref, gain_grad_ref = refs[:5]
    recv_conv, recv_back, recv_sums, kept, taps_ref = held
    response, grad, grads, store_sem = refs[5:]
    tiles = recv_conv.shape[0] // 2
    rows = output_ref.shape[0]
    span = taps_grad_ref.shape[1]
    margin = span // 2
    middle = (span + 1) // 2
    stores = [
        pltpu.make_async_copy(refs[i], results[i], store_sem.at[i]) for i in (0, 2, 3, 4)
    ]
    streams = [
        pltpu.make_async_copy(streams_ref.at[i], results[1].at[i], store_sem.at[5 + i])
        for i in range(3)
    ]
    main = slice(RIM, RIM + rows)
    ends = (slice(0, RIM), slice(RIM + rows, rows + 2 * RIM))
    for tile in range(tiles):
        lanes = slice(tile * LANES, (tile + 1) * LANES)
        low = low_lanes((1, LANES))
        tops = [recv_sums[2 * tile + half] for half in range(2)]
        response_top, back_top = [
            [top[span + middle + i : span + middle + i + 1] for top in tops] for i in range(2)
        ]
        found = [decode(wide(recv_back[2 * tile + i, 0:rows]), back_top[i]) for i in range(2)]
        grad[main, lanes], filter_grad_ref[:, lanes] = split(*found)
        rims = [
            decode(
                wide(recv_back[2 * tile + i, rows : rows + 2 * RIM]),
                jnp.where(low, back_top[i], response_top[i]),
            )
            for i in range(2)
        ]
        for target, rim in zip((grad, response), split(*rims)):
            for index, place in enumerate(ends):
                target[place, lanes] = rim[index * RIM : (index + 1) * RIM]
    stores[1].start()
    for tile in range(tiles):
        lanes = slice(tile * LANES, (tile + 1) * LANES)
        tops = [recv_sums[2 * tile + half] for half in range(2)]
        low_part, high_part = split(tops[0], tops[1])
        taps_grad_ref[1, :, lanes] = low_part[0:span]
        taps_grad_ref[2, :, lanes] = high_part[0:span]
        taps_grad_ref[0, :middle, lanes] = low_part[span : span + middle]
        taps_grad_ref[0, middle:, lanes] = high_part[span : 2 * span - middle]
        gain_grad_ref[:, lanes] = high_part[2 * span - middle : 2 * span - middle + 1]
        pieces = split(
            *(
                decode(
                    wide(recv_conv[2 * tile + i]), tops[i][span + middle : span + middle + 1]
                )
                for i in range(2)
            )
        )
        whole = jnp.concatenate(pieces, axis=0)
        response[main, lanes] = whole
        output_ref[:, lanes] = (whole * kept[0, main, lanes]).astype(jnp.bfloat16)
    for index in (0, 2, 3):
        stores[index].start()
    for stream, (value, other) in enumerate(((response, 3), (grad, 2), (grad, 1))):
        for tile in range(tiles):
            lanes = slice(tile * LANES, (tile + 1) * LANES)
            grads[stream, tile] = value[:, lanes] * kept[other, :, lanes]
            taps = taps_ref[stream, :, lanes]
            total = jnp.zeros((rows, LANES), jnp.float32)
            for tap in range(span):
                first = RIM + margin - tap
                total = total + taps[tap : tap + 1] * grads[stream, tile, first : first + rows]
            streams_ref[stream, :, lanes] = total.astype(jnp.bfloat16)
        streams[stream].start()
    for store in stores + streams:
        store.wait()


def halved(table):
    coarse = table.astype(ml_dtypes.bfloat16)
    rest = (table - coarse.astype(np.float32)).astype(ml_dtypes.bfloat16)
    return np.concatenate([coarse, rest], axis=2)


def packed_body(devices, projected, long_filter, short_kernel, skip_gain, cotangent):
    rows, channels = long_filter.shape
    span = short_kernel.shape[1]
    extent = rows * devices
    slabs = 2 * devices
    width = rows // 2
    tables = [halved(table) for table in fine_tables(slabs, width)]
    sums_rows = span + (span + 1) // 2 + 2
    block = (devices, rows, LANES)
    half_block = (devices, width, LANES)
    longer = (devices, rows + 2 * RIM, LANES)
    narrow, full = jnp.bfloat16, jnp.float32
    arguments = (projected, cotangent, long_filter, short_kernel, skip_gain[None], *tables)
    in_hbm = pl.BlockSpec(memory_space=pltpu.HBM)
    anywhere = pl.BlockSpec(memory_space=pl.ANY)
    arguments = [pltpu.with_memory_space_constraint(value, pltpu.HBM) for value in arguments]
    packed_shapes = (
        jax.ShapeDtypeStruct(half_block, narrow),
        jax.ShapeDtypeStruct(longer, narrow),
        jax.ShapeDtypeStruct((devices, sums_rows, LANES), full),
        jax.ShapeDtypeStruct((4, rows + 2 * RIM, channels), full),
        jax.ShapeDtypeStruct(short_kernel.shape, full),
    )
    out_shapes = (
        jax.ShapeDtypeStruct((rows, channels), narrow),
        jax.ShapeDtypeStruct((3, rows, channels), narrow),
        jax.ShapeDtypeStruct((rows, channels), full),
        jax.ShapeDtypeStruct(short_kernel.shape, full),
        jax.ShapeDtypeStruct((1, channels), full),
    )
    packed = pl.pallas_call(
        functools.partial(layer_kernel, devices),
        out_shape=packed_shapes,
        in_specs=[in_hbm] * 7,
        out_specs=(anywhere,) * 5,
        scratch_shapes=[
            *(pltpu.VMEM(value.shape, value.dtype) for value in arguments),
            pltpu.VMEM(block, narrow),
            pltpu.VMEM(block, narrow),
            pltpu.VMEM(block, narrow),
            pltpu.VMEM(block, narrow),
            pltpu.VMEM(half_block, narrow),
            pltpu.VMEM(half_block, narrow),
            pltpu.VMEM((devices, 1, LANES), full),
            pltpu.VMEM((devices, 1, LANES), full),
            pltpu.VMEM((2, 2, 2 * RIM, channels), narrow),
            pltpu.VMEM((2, 2, 2 * RIM, channels), narrow),
            pltpu.VMEM(half_block, narrow),
            pltpu.VMEM(longer, narrow),
            pltpu.VMEM((sums_rows, LANES), full),
            pltpu.VMEM((4, rows + 4 * RIM, channels), full),
            pltpu.VMEM((4, rows + 2 * RIM, channels), full),
            pltpu.VMEM((extent + 2 * RIM, LANES), full),
            pltpu.VMEM((extent + 2 * RIM, LANES), full),
            *[pltpu.VMEM((extent, LANES), full)] * 5,
            *[pltpu.VMEM((slabs // 2 + 1, rows, LANES), full)] * 2,
            pltpu.SemaphoreType.DMA((len(arguments),)),
            pltpu.SemaphoreType.DMA((5,)),
            pltpu.SemaphoreType.DMA((8, devices)),
            pltpu.SemaphoreType.DMA((8, devices)),
        ],
        compiler_params=pltpu.CompilerParams(
            collective_id=0, has_side_effects=True, vmem_limit_bytes=LIMIT
        ),
    )(*arguments)
    found = pl.pallas_call(
        unpack_kernel,
        out_shape=out_shapes,
        in_specs=[pl.BlockSpec(memory_space=pltpu.VMEM)] * 5,
        out_specs=(in_hbm,) * 5,
        scratch_shapes=[
            *(pltpu.VMEM(value.shape, value.dtype) for value in out_shapes),
            *[pltpu.VMEM((rows + 2 * RIM, channels), full)] * 2,
            pltpu.VMEM((3, channels // LANES, rows + 2 * RIM, LANES), full),
            pltpu.SemaphoreType.DMA((8,)),
        ],
        compiler_params=pltpu.CompilerParams(vmem_limit_bytes=LIMIT),
    )(*packed)
    return (*found[:4], found[4][0])


def with_halo(block, sides, width):
    for axis, dim in sides:
        count = lax.axis_size(axis)
        forward = [(i, i + 1) for i in range(count - 1)]
        forward.append((count - 1, 0))
        backward = [(target, source) for source, target in forward]
        low = lax.ppermute(
            lax.slice_in_dim(block, block.shape[dim] - width, None, axis=dim), axis, forward
        )
        high = lax.ppermute(lax.slice_in_dim(block, 0, width, axis=dim), axis, backward)
        block = jnp.concatenate([low, block, high], axis=dim)
    return block


def dft_tables(extent):
    indices = jnp.arange(extent, dtype=jnp.int32)
    angles = (indices[:, None] * indices[None, :] % extent).astype(jnp.float32) * (
        2.0 * math.pi / extent
    )
    return (jnp.cos(angles), jnp.sin(angles))


def apply_along(matrix, signal, axis_dim):
    letters = "wxyz"
    target = letters[:axis_dim] + "k" + letters[axis_dim + 1 :]
    return jnp.einsum(
        "k" + letters[axis_dim] + "," + letters + "->" + target, matrix, signal, precision=HIGHEST
    )


def forward_section(real_part, imaginary, axis_dim):
    cosine, sine_table = dft_tables(real_part.shape[axis_dim])
    out_real = apply_along(cosine, real_part, axis_dim)
    out_imag = -apply_along(sine_table, real_part, axis_dim)
    if imaginary is not None:
        out_real = out_real + apply_along(sine_table, imaginary, axis_dim)
        out_imag = out_imag + apply_along(cosine, imaginary, axis_dim)
    return (out_real, out_imag)


def inverse_section(real_part, imaginary, axis_dim, keep_imag):
    cosine, sine_table = dft_tables(real_part.shape[axis_dim])
    out_real = apply_along(cosine, real_part, axis_dim) - apply_along(
        sine_table, imaginary, axis_dim
    )
    if keep_imag:
        return (
            out_real,
            apply_along(sine_table, real_part, axis_dim) + apply_along(cosine, imaginary, axis_dim),
        )
    return (out_real, None)


def twist(real_part, imaginary, angles, sign_factor):
    cosine = jnp.cos(angles)
    sine_table = jnp.sin(angles)
    return (
        real_part * cosine + sign_factor * imaginary * sine_table,
        imaginary * cosine - sign_factor * real_part * sine_table,
    )


def twiddle(low_index, high_index, extent):
    return (low_index * high_index % extent).astype(jnp.float32) * (2.0 * math.pi / extent)


def block_angles(devices, portion, extent):
    low_index = jnp.arange(devices, dtype=jnp.int32)[None, :, None, None]
    high_index = (lax.axis_index("seq") * portion + jnp.arange(portion, dtype=jnp.int32))[
        None, None, :, None
    ]
    return twiddle(low_index, high_index, extent)


def sequence_forward(signals, extent):
    devices = lax.axis_size("seq")
    portion = signals.shape[1] // devices
    columns = lax.all_to_all(signals[:, None], "seq", split_axis=2, concat_axis=1, tiled=True)
    real_part, imaginary = forward_section(columns, None, 1)
    real_part, imaginary = twist(real_part, imaginary, block_angles(devices, portion, extent), 1.0)
    spread = (
        lax.all_to_all(real_part, "seq", split_axis=1, concat_axis=2, tiled=True),
        lax.all_to_all(imaginary, "seq", split_axis=1, concat_axis=2, tiled=True),
    )
    return forward_section(spread[0], spread[1], 2)


def sequence_inverse(real_part, imaginary, extent):
    devices = lax.axis_size("seq")
    portion = real_part.shape[2] // devices
    real_part, imaginary = inverse_section(real_part, imaginary, 2, True)
    gathered = (
        lax.all_to_all(real_part, "seq", split_axis=2, concat_axis=1, tiled=True),
        lax.all_to_all(imaginary, "seq", split_axis=2, concat_axis=1, tiled=True),
    )
    real_part, imaginary = twist(
        gathered[0], gathered[1], block_angles(devices, portion, extent), -1.0
    )
    pieces = inverse_section(real_part, imaginary, 1, False)[0] * (1.0 / extent)
    blocks = lax.all_to_all(pieces, "seq", split_axis=1, concat_axis=2, tiled=True)
    return blocks[:, 0]


def body(projected, long_filter, short_kernel, skip_gain, cotangent):
    rows_here = projected.shape[1]
    extent = rows_here * lax.axis_size("seq")
    factor = 1.0 / math.sqrt(extent)
    kernel_span = short_kernel.shape[1]
    margin = kernel_span // 2
    padded = with_halo(projected, (("seq", 1),), margin)
    shorts = jnp.zeros(projected.shape, jnp.float32)
    for offset in range(kernel_span):
        shorts = shorts + short_kernel[:, offset][:, None, :] * padded[
            :, offset : offset + rows_here
        ].astype(jnp.float32)
    gated_signal = shorts[1] * shorts[2]
    transform, restore = (sequence_forward, sequence_inverse)
    upstream = cotangent.astype(jnp.float32)
    grad_response = upstream * shorts[0]
    spec_real, spec_imag = transform(jnp.stack([gated_signal, long_filter]), extent)
    gated_real, gated_imag = (spec_real[0], spec_imag[0])
    filter_real, filter_imag = (spec_real[1] * factor, spec_imag[1] * factor)
    product_real = filter_real * gated_real - filter_imag * gated_imag
    product_imag = filter_real * gated_imag + filter_imag * gated_real
    convolved = restore(product_real[None], product_imag[None], extent)[0]
    upstream_real, upstream_imag = transform(grad_response[None], extent)
    upstream_real, upstream_imag = (upstream_real[0], upstream_imag[0])
    back_real = jnp.stack(
        [
            filter_real * upstream_real + filter_imag * upstream_imag,
            gated_real * upstream_real + gated_imag * upstream_imag,
        ]
    )
    back_imag = jnp.stack(
        [
            filter_real * upstream_imag - filter_imag * upstream_real,
            gated_real * upstream_imag - gated_imag * upstream_real,
        ]
    )
    restored = restore(back_real, back_imag, extent)
    grad_gated = restored[0] + skip_gain * grad_response
    filter_grad = restored[1] * factor
    response = convolved + skip_gain * gated_signal
    layer_output = (response * shorts[0]).astype(jnp.bfloat16)
    grad_shorts = jnp.stack([upstream * response, grad_gated * shorts[2], grad_gated * shorts[1]])
    rimmed = with_halo(grad_shorts, (("seq", 1),), margin)
    stream_sum = jnp.zeros(grad_shorts.shape, jnp.float32)
    kernel_terms = []
    for offset in range(kernel_span):
        start_row = 2 * margin - offset
        stream_sum = (
            stream_sum
            + short_kernel[:, offset][:, None, :] * rimmed[:, start_row : start_row + rows_here]
        )
        kernel_terms.append(
            jnp.sum(
                grad_shorts * padded[:, offset : offset + rows_here].astype(jnp.float32), axis=1
            )
        )
    kernel_part = jnp.stack(kernel_terms, axis=1)
    skip_part = jnp.sum(grad_response * gated_signal, axis=0)
    kernel_total, skip_total = lax.psum((kernel_part, skip_part), "seq")
    return (
        layer_output,
        stream_sum.astype(jnp.bfloat16),
        filter_grad,
        kernel_total * factor,
        skip_total * factor,
    )


def solution(mesh):
    placed = (
        P(None, ("groups", "seq"), "chan"),
        P(("groups", "seq"), "chan"),
        P(None, None, "chan"),
        P("chan"),
        P(("groups", "seq"), "chan"),
    )
    devices = mesh.shape["seq"]

    def run(projected, *others):
        rows, channels = projected.shape[1:]
        if channels == HALF * devices and rows == LANES and devices & (devices - 1) == 0:
            return packed_body(devices, projected, *others)
        return body(projected, *others)

    return jax.shard_map(
        run,
        mesh=mesh,
        in_specs=placed,
        out_specs=(
            P(("groups", "seq"), "chan"),
            P(None, ("groups", "seq"), "chan"),
            P(("groups", "seq"), "chan"),
            P("groups", None, "chan"),
            P(("groups", "chan")),
        ),
        check_vma=False,
    )
```

```python
import functools
import math

import jax
import jax.numpy as jnp
import ml_dtypes
import numpy as np
from jax import lax
from jax.experimental import pallas as pl
from jax.experimental.pallas import tpu as pltpu
from jax.sharding import PartitionSpec as P

HIGHEST = lax.Precision.HIGHEST
LANES = 128
HALF = LANES // 2
RIM = 8
LIMIT = 20 * 1024 * 1024
BEND = 15.0
SPREAD = 251.0 * math.log(2.0) / math.log(1.0 + BEND)
LOWEST = -125.0 * math.log(2.0)
TINY = 1e-35


def turned(value, step, extent):
    real_part, imaginary = value
    step = step % extent
    if step == 0:
        return value
    if 2 * step == extent:
        return (-real_part, None if imaginary is None else -imaginary)
    if 4 * step == extent:
        return (None if imaginary is None else -imaginary, real_part)
    if 4 * step == 3 * extent:
        return (imaginary, -real_part)
    cosine = math.cos(2.0 * math.pi * step / extent)
    sine = math.sin(2.0 * math.pi * step / extent)
    if imaginary is None:
        return (real_part * cosine, real_part * sine)
    return (real_part * cosine - imaginary * sine, imaginary * cosine + real_part * sine)


def part_sum(left, right, sign):
    if right is None:
        return left
    if left is None:
        return right if sign > 0 else -right
    return left + right if sign > 0 else left - right


def real_spectrum(values):
    extent = len(values)
    if extent == 2:
        return [(values[0] + values[1], None), (values[0] - values[1], None)]
    even, odd = real_spectrum(values[0::2]), real_spectrum(values[1::2])
    half = extent // 2

    def entry(spectrum, index):
        index = index % half
        if 2 * index <= half:
            return spectrum[index]
        real_part, imaginary = spectrum[half - index]
        return (real_part, None if imaginary is None else -imaginary)

    found = []
    for index in range(half + 1):
        left, right = entry(even, index), turned(entry(odd, index), -index, extent)
        found.append((part_sum(left[0], right[0], 1), part_sum(left[1], right[1], 1)))
    return found


def real_values(spectrum):
    extent = 2 * (len(spectrum) - 1)
    if extent == 2:
        first, last = spectrum[0][0], spectrum[1][0]
        return [first + last, first - last]
    half = extent // 2
    even, odd = [], []
    for index in range(half // 2 + 1):
        real_part, imaginary = spectrum[index]
        if 2 * index == half:
            even.append((2.0 * real_part, None))
            odd.append((-2.0 * imaginary, None))
            continue
        other_real, other_imag = spectrum[half - index]
        even.append(
            (real_part + other_real, part_sum(imaginary, other_imag, -1))
        )
        odd.append(
            turned(
                (real_part - other_real, part_sum(imaginary, other_imag, 1)), index, extent
            )
        )
    found = [None] * extent
    found[0::2] = real_values(even)
    found[1::2] = real_values(odd)
    return found


def fine_tables(slabs, width):
    extent = slabs * width
    coarse = np.arange(slabs // 2 + 1)[:, None, None]
    fine = np.arange(width)[None, :, None]
    place = np.arange(width)[None, None, :]
    angles = ((coarse + slabs * fine) * place % extent) * (2.0 * np.pi / extent)
    cosine, sine = np.cos(angles), np.sin(angles)
    table = np.concatenate(
        [np.concatenate([cosine, sine], 2), np.concatenate([-sine, cosine], 2)], 1
    )
    inverse = np.swapaxes(table, 1, 2) / (extent * math.sqrt(extent))
    return table.astype(np.float32), inverse.astype(np.float32)


def low_lanes(shape):
    return lax.broadcasted_iota(jnp.int32, shape, len(shape) - 1) < HALF


def swap(value):
    return pltpu.roll(value, HALF, 1)


def wide(value):
    return value.astype(jnp.float32)


def join(first, second, parity):
    low = low_lanes(first.shape)
    if parity == 0:
        return jnp.where(low, first, swap(second))
    return jnp.where(low, swap(first), second)


def split(first, second):
    return join(first, second, 0), join(first, second, 1)


def bend_of(top):
    return jnp.where(top > TINY, BEND / jnp.maximum(top, TINY), 0.0)


def rounded_top(value):
    top = jnp.max(jnp.abs(value), axis=0, keepdims=True)
    return wide((top * (1.0 + 2.0**-7)).astype(jnp.bfloat16))


def sums_tops(tops, span, middle):
    low = low_lanes((1, LANES))
    last = jnp.where(low, tops[1], tops[2])
    return jnp.concatenate([tops[0]] * span + [tops[1]] * (middle - 1) + [last], axis=0)


def encode(value, bend):
    size = jnp.exp(SPREAD * jnp.log(1.0 + jnp.abs(value) * bend) + LOWEST)
    return jnp.where(value < 0.0, -size, size)


def decode(code, top):
    size = (jnp.exp((jnp.log(jnp.abs(code)) - LOWEST) * (1.0 / SPREAD)) - 1.0) * (top / BEND)
    return jnp.where(code < 0.0, -size, size)


def halves(value):
    coarse = value.astype(jnp.bfloat16)
    return coarse, (value - wide(coarse)).astype(jnp.bfloat16)


def apply_table(table, index, value):
    coarse, rest = halves(value)
    depth = coarse.shape[0]
    return jnp.dot(
        table[index],
        jnp.concatenate([coarse, coarse], axis=0),
        preferred_element_type=jnp.float32,
    ) + jnp.dot(table[index, :, :depth], rest, preferred_element_type=jnp.float32)


def layer_kernel(
    devices,
    projected_in,
    cotangent_in,
    filter_in,
    taps_in,
    gain_in,
    forward_in,
    inverse_in,
    recv_conv,
    recv_back,
    recv_sums,
    kept_out,
    taps_out,
    projected_ref,
    cotangent_ref,
    filter_ref,
    taps_ref,
    gain_ref,
    forward_ref,
    inverse_ref,
    send_first,
    recv_first,
    send_second,
    recv_second,
    send_filter,
    recv_filter,
    send_top,
    recv_top,
    send_rim,
    recv_rim,
    send_conv,
    send_back,
    send_sums,
    around,
    kept,
    first_rim,
    second_rim,
    first_short,
    signal,
    upstream,
    response,
    back,
    signal_spectra,
    product_spectra,
    load_sem,
    keep_sem,
    send_sem,
    recv_sem,
):
    hops = [(devices // 2 + (-1) ** i * ((i + 1) // 2)) for i in range(devices - 1)]
    arguments = (projected_in, cotangent_in, filter_in, taps_in, gain_in, forward_in, inverse_in)
    held = (
        projected_ref,
        cotangent_ref,
        filter_ref,
        taps_ref,
        gain_ref,
        forward_ref,
        inverse_ref,
    )
    loads = [
        pltpu.make_async_copy(source, target, load_sem.at[index])
        for index, (source, target) in enumerate(zip(arguments, held))
    ]
    for load in loads:
        load.start()
    rows, channels = cotangent_ref.shape
    tiles = channels // LANES
    span = taps_ref.shape[1]
    margin = span // 2
    width = rows // 2
    slabs = 2 * devices
    extent = rows * devices
    factor = 1.0 / math.sqrt(extent)
    me = lax.axis_index("seq")
    odd = lax.rem(me, 2) == 1

    def copy_to(kind, hop, source, target, peer):
        return pltpu.make_async_remote_copy(
            src_ref=source,
            dst_ref=target,
            send_sem=send_sem.at[kind, hop],
            recv_sem=recv_sem.at[kind, hop],
            device_id={"seq": peer},
            device_id_type=pl.DeviceIdType.MESH,
        )

    def peer_at(hop):
        return lax.rem(me + hop, devices)

    def source_at(hop):
        return lax.rem(me + devices - hop, devices)

    barrier = pltpu.get_barrier_semaphore()
    for hop in hops:
        pl.semaphore_signal(
            barrier, inc=1, device_id={"seq": peer_at(hop)}, device_id_type=pl.DeviceIdType.MESH
        )

    loads[0].wait()
    loads[1].wait()

    def lanes_of(peer):
        return pl.ds(pl.multiple_of((peer // 2) * LANES, LANES), LANES)

    def join_for(peer, first, second):
        flip = lax.rem(peer, 2) == 1
        return jnp.where(
            low_lanes(first.shape),
            jnp.where(flip, swap(first), first),
            jnp.where(flip, second, swap(second)),
        ).astype(jnp.bfloat16)

    def pack_first(peer, target):
        lanes = lanes_of(peer)
        target[...] = join_for(
            peer, wide(projected_ref[1, :, lanes]), wide(projected_ref[2, :, lanes])
        )

    def pack_second(peer, target):
        lanes = lanes_of(peer)
        target[...] = join_for(
            peer, wide(projected_ref[0, :, lanes]), wide(cotangent_ref[:, lanes])
        )

    for side, start in enumerate((0, rows - 2 * RIM)):
        part = slice(0, RIM) if side == 0 else slice(RIM, 2 * RIM)
        ends = [wide(projected_ref[s, start : start + 2 * RIM])[part] for s in range(3)]
        ends.append(wide(cotangent_ref[start : start + 2 * RIM])[part])
        for pair in range(2):
            send_rim[side, pair] = jnp.concatenate(ends[2 * pair : 2 * pair + 2], axis=0).astype(
                jnp.bfloat16
            )
    rim_copies = [
        copy_to(7, hop, send_rim.at[side], recv_rim.at[side], peer_at(hop))
        for side, hop in enumerate((devices - 1, 1))
    ]
    for place, hop in enumerate(hops):
        peer = peer_at(hop)
        pack_first(peer, send_first.at[peer])
        if place == 0:
            pl.semaphore_wait(barrier, devices - 1)
        copy_to(0, hop, send_first.at[peer], recv_first.at[me], peer).start()

    loads[2].wait()
    for tile in range(tiles):
        lanes = slice(tile * LANES, (tile + 1) * LANES)
        whole = filter_ref[:, lanes]
        top = jnp.max(jnp.abs(whole), axis=0, keepdims=True)
        coded = encode(whole, bend_of(top))
        for half in range(2):
            send_filter[2 * tile + half] = join(coded[:width], coded[width:], half).astype(
                jnp.bfloat16
            )
            send_top[2 * tile + half] = join(top, top, half)
    for hop in hops:
        peer = peer_at(hop)
        copy_to(2, hop, send_filter.at[peer], recv_filter.at[me], peer).start()
        copy_to(3, hop, send_top.at[peer], recv_top.at[me], peer).start()
    for hop in hops:
        peer = peer_at(hop)
        pack_second(peer, send_second.at[peer])
        copy_to(1, hop, send_second.at[peer], recv_second.at[me], peer).start()
    for copy in rim_copies:
        copy.start()
    pack_first(me, recv_first.at[me])
    pack_second(me, recv_second.at[me])
    recv_filter[me] = send_filter[me]
    recv_top[me] = send_top[me]

    for load in loads[3:5]:
        load.wait()
    own = pl.ds(pl.multiple_of((me // 2) * LANES, LANES), LANES)

    def own_pair(first, second):
        return jnp.where(odd, join(first, second, 1), join(first, second, 0))

    gate_taps, left_taps, right_taps = [taps_ref[s, :, own] for s in range(3)]
    first_taps = own_pair(left_taps, right_taps)
    centre = wide(lax.broadcasted_iota(jnp.int32, (span, LANES), 0) == margin)
    second_taps = jnp.where(low_lanes((span, LANES)), own_pair(gate_taps, gate_taps), centre)
    own_gain = gain_ref[:, own]
    gain = own_pair(own_gain, own_gain)

    def wait_from(kind, source, target):
        for hop in hops:
            copy_to(
                kind, hop, source.at[peer_at(hop)], target.at[source_at(hop)], peer_at(hop)
            ).wait()

    def close_rim(rim):
        rim[0:RIM] = rim[extent : extent + RIM]
        rim[extent + RIM : extent + 2 * RIM] = rim[RIM : 2 * RIM]

    def open_rim(rim, received):
        for block in range(devices):
            rim[RIM + block * rows : RIM + (block + 1) * rows] = wide(received[block])
        close_rim(rim)

    def filtered(rim, taps, start):
        near = rim[pl.ds(start, width + 2 * RIM)]
        total = jnp.zeros((width, LANES), jnp.float32)
        for tap in range(span):
            low = RIM + tap - margin
            total = total + taps[tap : tap + 1] * near[low : low + width]
        return total

    wait_from(0, send_first, recv_first)
    open_rim(first_rim, recv_first)

    def shorten_first(slab, carry):
        start = pl.multiple_of(slab * width, width)
        total = filtered(first_rim, first_taps, start)
        first_short[pl.ds(start, width)] = total
        signal[pl.ds(start, width)] = total * swap(total)
        return carry

    lax.fori_loop(0, slabs, shorten_first, 0)
    for load in loads[5:]:
        load.wait()
    wait_from(2, send_filter, recv_filter)
    wait_from(3, send_top, recv_top)

    def put_spectrum(spectra, found, start, count):
        for index, (real_part, imaginary) in enumerate(found):
            if imaginary is None:
                imaginary = jnp.zeros_like(real_part)
            spectra[index, pl.ds(start, count)] = real_part
            spectra[index, pl.ds(width + start, count)] = imaginary

    def get_spectrum(spectra, start, count):
        found = []
        for index in range(slabs // 2 + 1):
            imaginary = None
            if 0 < index < slabs // 2:
                imaginary = spectra[index, pl.ds(width + start, count)]
            found.append((spectra[index, pl.ds(start, count)], imaginary))
        return found

    def first_spectrum(step, carry):
        start = pl.multiple_of(step * 16, 16)
        low = low_lanes((16, LANES))
        values = []
        for block in range(devices):
            found = decode(wide(recv_filter[block, pl.ds(start, 16)]), recv_top[block])
            for half in range(2):
                here = signal[pl.ds(block * rows + half * width + start, 16)]
                values.append(jnp.where(low, here, swap(found) if half == 0 else found))
        put_spectrum(signal_spectra, real_spectrum(values), start, 16)
        return carry

    lax.fori_loop(0, width // 16, first_spectrum, 0)

    for index in range(slabs // 2 + 1):
        found = apply_table(forward_ref, index, signal_spectra[index])
        signal_spectra[index] = found
        real_part, imaginary = found[:width], found[width:]
        other_real, other_imag = swap(real_part), swap(imaginary)
        product = jnp.concatenate(
            [
                real_part * other_real - imaginary * other_imag,
                real_part * other_imag + imaginary * other_real,
            ],
            axis=0,
        )
        product_spectra[index] = apply_table(inverse_ref, index, product)

    def first_back(step, top):
        start = pl.multiple_of(step * 8, 8)
        for slab, value in enumerate(real_values(get_spectrum(product_spectra, start, 8))):
            place = pl.ds(slab * width + start, 8)
            whole = value + gain * signal[place]
            response[place] = whole
            top = jnp.maximum(top, jnp.abs(whole))
        return top

    nothing = jnp.zeros((8, LANES), jnp.float32)
    top = lax.fori_loop(0, width // 8, first_back, nothing)
    response_top = rounded_top(top)
    response_bend = bend_of(response_top)

    def step_hop(step):
        return devices // 2 + (step + 1) // 2 * (1 - 2 * lax.rem(step, 2))

    def pack_conv(peer):
        start = pl.multiple_of(peer * rows, rows)
        folded = jnp.where(
            low_lanes((width, LANES)),
            response[pl.ds(start, width)],
            response[pl.ds(start + width, width)],
        )
        send_conv[peer] = encode(folded, response_bend).astype(jnp.bfloat16)

    def step_conv(step, carry):
        hop = step_hop(step)
        peer = peer_at(hop)
        pack_conv(peer)
        copy_to(4, hop, send_conv.at[peer], recv_conv.at[me], peer).start()
        return carry

    lax.fori_loop(0, devices - 1, step_conv, 0)
    pack_conv(me)
    keeps = [
        pltpu.make_async_copy(source, target.at[me], keep_sem.at[index])
        for index, (source, target) in enumerate(
            (
                (send_conv.at[me], recv_conv),
                (send_back.at[me], recv_back),
                (send_sums, recv_sums),
            )
        )
    ]
    keeps[0].start()

    wait_from(1, send_second, recv_second)
    open_rim(second_rim, recv_second)

    def shorten_second(slab, carry):
        start = pl.multiple_of(slab * width, width)
        total = filtered(second_rim, second_taps, start)
        total = total * swap(total)
        upstream[pl.ds(start, width)] = total
        return carry + jnp.sum(
            (total * signal[pl.ds(start, width)]).reshape(-1, 8, LANES), axis=0
        )

    gain_sum = lax.fori_loop(0, slabs, shorten_second, nothing)

    def second_spectrum(step, carry):
        start = pl.multiple_of(step * 8, 8)
        values = [upstream[pl.ds(slab * width + start, 8)] for slab in range(slabs)]
        put_spectrum(product_spectra, real_spectrum(values), start, 8)
        return carry

    lax.fori_loop(0, width // 8, second_spectrum, 0)

    for index in range(slabs // 2 + 1):
        found = apply_table(forward_ref, index, product_spectra[index])
        real_part, imaginary = found[:width], found[width:]
        other_real = swap(signal_spectra[index, :width])
        other_imag = swap(signal_spectra[index, width:])
        product = jnp.concatenate(
            [
                real_part * other_real + imaginary * other_imag,
                imaginary * other_real - real_part * other_imag,
            ],
            axis=0,
        )
        product_spectra[index] = apply_table(inverse_ref, index, product)

    low_gain = jnp.where(low_lanes((1, LANES)), gain, 0.0)

    def second_back(step, top):
        start = pl.multiple_of(step * 8, 8)
        for slab, value in enumerate(real_values(get_spectrum(product_spectra, start, 8))):
            place = pl.ds(slab * width + start, 8)
            whole = value + low_gain * upstream[place]
            back[place] = whole
            top = jnp.maximum(top, jnp.abs(whole))
        return top

    top = lax.fori_loop(0, width // 8, second_back, nothing)
    back_top = rounded_top(top)
    back_bend = bend_of(back_top)
    rim_bend = jnp.where(low_lanes((1, LANES)), back_bend, response_bend)

    def pack_back(peer):
        start = pl.multiple_of(peer * rows, rows)
        send_back[peer, 0:rows] = encode(back[pl.ds(start, rows)], back_bend).astype(jnp.bfloat16)
        places = (
            lax.rem(start + extent - RIM, extent),
            lax.rem(start + rows, extent),
        )
        ends = []
        for place in places:
            here = pl.ds(pl.multiple_of(place, RIM), RIM)
            ends.append(jnp.where(low_lanes((RIM, LANES)), back[here], response[here]))
        send_back[peer, rows : rows + 2 * RIM] = encode(
            jnp.concatenate(ends, axis=0), rim_bend
        ).astype(jnp.bfloat16)

    def step_back(step, carry):
        hop = step_hop(step)
        peer = peer_at(hop)
        pack_back(peer)
        copy_to(5, hop, send_back.at[peer], recv_back.at[me], peer).start()
        return carry

    lax.fori_loop(0, devices - 1, step_back, 0)
    pack_back(me)
    keeps[1].start()

    def add_sums(slab, sums):
        sums = list(sums)
        start = pl.multiple_of(slab * width, width)
        here = pl.ds(start, width)
        low = low_lanes((width, LANES))
        grad = back[here]
        grad = jnp.where(low, grad, swap(grad)) * swap(first_short[here])
        near_first = first_rim[pl.ds(start, width + 2 * RIM)]
        near_second = second_rim[pl.ds(start, width + 2 * RIM)]
        other = response[here] * swap(near_second[RIM : RIM + width])
        for tap in range(span):
            inner = slice(RIM + tap - margin, RIM + tap - margin + width)
            for which, (grads, near) in enumerate(((grad, near_first), (other, near_second))):
                sums[which * span + tap] = sums[which * span + tap] + jnp.sum(
                    (grads * near[inner]).reshape(-1, 8, LANES), axis=0
                )
        return tuple(sums)

    sums = lax.fori_loop(0, slabs, add_sums, (nothing,) * (2 * span))
    sums = [factor * jnp.sum(value, axis=0, keepdims=True) for value in sums + (gain_sum,)]
    middle = (span + 1) // 2
    low = low_lanes((1, LANES))
    parts = sums[:span] + [join(sums[i], sums[i + middle], 0) for i in range(span, span + middle)]
    last = parts[-1]
    tops = [
        rounded_top(jnp.concatenate(parts[:span], axis=0)),
        rounded_top(jnp.concatenate(parts[span:-1] + [jnp.where(low, last, 0.0)], axis=0)),
        rounded_top(last),
    ]
    coded = encode(jnp.concatenate(parts, axis=0), bend_of(sums_tops(tops, span, middle)))
    send_sums[...] = jnp.concatenate([coded, *tops, response_top, back_top], axis=0).astype(
        jnp.bfloat16
    )
    for hop in hops:
        copy_to(6, hop, send_sums, recv_sums.at[me], peer_at(hop)).start()
    keeps[2].start()

    for copy in rim_copies:
        copy.wait()
    for stream in range(4):
        around[stream, 0:RIM] = jnp.zeros((RIM, channels), jnp.float32)
        around[stream, rows + 3 * RIM :] = jnp.zeros((RIM, channels), jnp.float32)
        half = slice((stream % 2) * RIM, (stream % 2 + 1) * RIM)
        before, after = wide(recv_rim[1, stream // 2])[half], wide(recv_rim[0, stream // 2])[half]
        around[stream, RIM : 2 * RIM] = before
        around[stream, rows + 2 * RIM : rows + 3 * RIM] = after
        source = cotangent_ref[...] if stream == 3 else projected_ref[stream]
        around[stream, 2 * RIM : 2 * RIM + rows] = wide(source)
    kept[3] = around[3, RIM : rows + 3 * RIM]

    def own_short(step, carry):
        stream, tile = step // tiles, lax.rem(step, tiles)
        lanes = pl.ds(pl.multiple_of(tile * LANES, LANES), LANES)
        taps = taps_ref[stream, :, lanes]
        for part in range(2):
            count = width + RIM
            total = jnp.zeros((count, LANES), jnp.float32)
            for tap in range(span):
                low = part * count + RIM + tap - margin
                total = total + taps[tap : tap + 1] * around[stream, low : low + count, lanes]
            kept[stream, part * count : (part + 1) * count, lanes] = total
        return carry

    lax.fori_loop(0, 3 * tiles, own_short, 0)
    keeping = pltpu.make_async_copy(kept, kept_out, keep_sem.at[3])
    keeping.start()
    passing = pltpu.make_async_copy(taps_ref, taps_out, keep_sem.at[4])
    passing.start()

    keeping.wait()
    passing.wait()
    for keep in keeps:
        keep.wait()
    wait_from(4, send_conv, recv_conv)
    wait_from(5, send_back, recv_back)
    for hop in hops:
        copy_to(6, hop, send_sums, recv_sums.at[source_at(hop)], peer_at(hop)).wait()


def unpack_kernel(*refs):
    held, results, refs = refs[:5], refs[5:10], refs[10:]
    output_ref, streams_ref, filter_grad_ref, taps_grad_ref, gain_grad_ref = refs[:5]
    recv_conv, recv_back, recv_sums, kept, taps_ref = held
    response, grad, grads, store_sem = refs[5:]
    tiles = recv_conv.shape[0] // 2
    rows = output_ref.shape[0]
    span = taps_grad_ref.shape[1]
    margin = span // 2
    middle = (span + 1) // 2
    stores = [
        pltpu.make_async_copy(refs[i], results[i], store_sem.at[i]) for i in (0, 2, 3, 4)
    ]
    streams = [
        pltpu.make_async_copy(streams_ref.at[i], results[1].at[i], store_sem.at[5 + i])
        for i in range(3)
    ]
    main = slice(RIM, RIM + rows)
    ends = (slice(0, RIM), slice(RIM + rows, rows + 2 * RIM))
    for tile in range(tiles):
        lanes = slice(tile * LANES, (tile + 1) * LANES)
        low = low_lanes((1, LANES))
        tops = [wide(recv_sums[2 * tile + half]) for half in range(2)]
        response_top, back_top = [
            [top[span + middle + i : span + middle + i + 1] for top in tops] for i in (3, 4)
        ]
        found = [decode(wide(recv_back[2 * tile + i, 0:rows]), back_top[i]) for i in range(2)]
        grad[main, lanes], filter_grad_ref[:, lanes] = split(*found)
        rims = [
            decode(
                wide(recv_back[2 * tile + i, rows : rows + 2 * RIM]),
                jnp.where(low, back_top[i], response_top[i]),
            )
            for i in range(2)
        ]
        for target, rim in zip((grad, response), split(*rims)):
            for index, place in enumerate(ends):
                target[place, lanes] = rim[index * RIM : (index + 1) * RIM]
    stores[1].start()
    for tile in range(tiles):
        lanes = slice(tile * LANES, (tile + 1) * LANES)
        tops = [wide(recv_sums[2 * tile + half]) for half in range(2)]
        count = span + middle
        low_part, high_part = split(
            *(
                decode(
                    top[:count],
                    sums_tops([top[count + i : count + i + 1] for i in range(3)], span, middle),
                )
                for top in tops
            )
        )
        taps_grad_ref[1, :, lanes] = low_part[0:span]
        taps_grad_ref[2, :, lanes] = high_part[0:span]
        taps_grad_ref[0, :middle, lanes] = low_part[span : span + middle]
        taps_grad_ref[0, middle:, lanes] = high_part[span : 2 * span - middle]
        gain_grad_ref[:, lanes] = high_part[2 * span - middle : 2 * span - middle + 1]
        pieces = split(
            *(
                decode(
                    wide(recv_conv[2 * tile + i]), tops[i][count + 3 : count + 4]
                )
                for i in range(2)
            )
        )
        whole = jnp.concatenate(pieces, axis=0)
        response[main, lanes] = whole
        output_ref[:, lanes] = (whole * kept[0, main, lanes]).astype(jnp.bfloat16)
    for index in (0, 2, 3):
        stores[index].start()
    for stream, (value, other) in enumerate(((response, 3), (grad, 2), (grad, 1))):
        for tile in range(tiles):
            lanes = slice(tile * LANES, (tile + 1) * LANES)
            grads[stream, tile] = value[:, lanes] * kept[other, :, lanes]
            taps = taps_ref[stream, :, lanes]
            total = jnp.zeros((rows, LANES), jnp.float32)
            for tap in range(span):
                first = RIM + margin - tap
                total = total + taps[tap : tap + 1] * grads[stream, tile, first : first + rows]
            streams_ref[stream, :, lanes] = total.astype(jnp.bfloat16)
        streams[stream].start()
    for store in stores + streams:
        store.wait()


def halved(table):
    coarse = table.astype(ml_dtypes.bfloat16)
    rest = (table - coarse.astype(np.float32)).astype(ml_dtypes.bfloat16)
    return np.concatenate([coarse, rest], axis=2)


def packed_body(devices, projected, long_filter, short_kernel, skip_gain, cotangent):
    rows, channels = long_filter.shape
    span = short_kernel.shape[1]
    extent = rows * devices
    slabs = 2 * devices
    width = rows // 2
    tables = [halved(table) for table in fine_tables(slabs, width)]
    sums_rows = span + (span + 1) // 2 + 5
    block = (devices, rows, LANES)
    half_block = (devices, width, LANES)
    longer = (devices, rows + 2 * RIM, LANES)
    narrow, full = jnp.bfloat16, jnp.float32
    arguments = (projected, cotangent, long_filter, short_kernel, skip_gain[None], *tables)
    in_hbm = pl.BlockSpec(memory_space=pltpu.HBM)
    anywhere = pl.BlockSpec(memory_space=pl.ANY)
    arguments = [pltpu.with_memory_space_constraint(value, pltpu.HBM) for value in arguments]
    packed_shapes = (
        jax.ShapeDtypeStruct(half_block, narrow),
        jax.ShapeDtypeStruct(longer, narrow),
        jax.ShapeDtypeStruct((devices, sums_rows, LANES), narrow),
        jax.ShapeDtypeStruct((4, rows + 2 * RIM, channels), full),
        jax.ShapeDtypeStruct(short_kernel.shape, full),
    )
    out_shapes = (
        jax.ShapeDtypeStruct((rows, channels), narrow),
        jax.ShapeDtypeStruct((3, rows, channels), narrow),
        jax.ShapeDtypeStruct((rows, channels), full),
        jax.ShapeDtypeStruct(short_kernel.shape, full),
        jax.ShapeDtypeStruct((1, channels), full),
    )
    packed = pl.pallas_call(
        functools.partial(layer_kernel, devices),
        out_shape=packed_shapes,
        in_specs=[in_hbm] * 7,
        out_specs=(anywhere,) * 5,
        scratch_shapes=[
            *(pltpu.VMEM(value.shape, value.dtype) for value in arguments),
            pltpu.VMEM(block, narrow),
            pltpu.VMEM(block, narrow),
            pltpu.VMEM(block, narrow),
            pltpu.VMEM(block, narrow),
            pltpu.VMEM(half_block, narrow),
            pltpu.VMEM(half_block, narrow),
            pltpu.VMEM((devices, 1, LANES), full),
            pltpu.VMEM((devices, 1, LANES), full),
            pltpu.VMEM((2, 2, 2 * RIM, channels), narrow),
            pltpu.VMEM((2, 2, 2 * RIM, channels), narrow),
            pltpu.VMEM(half_block, narrow),
            pltpu.VMEM(longer, narrow),
            pltpu.VMEM((sums_rows, LANES), narrow),
            pltpu.VMEM((4, rows + 4 * RIM, channels), full),
            pltpu.VMEM((4, rows + 2 * RIM, channels), full),
            pltpu.VMEM((extent + 2 * RIM, LANES), full),
            pltpu.VMEM((extent + 2 * RIM, LANES), full),
            *[pltpu.VMEM((extent, LANES), full)] * 5,
            *[pltpu.VMEM((slabs // 2 + 1, rows, LANES), full)] * 2,
            pltpu.SemaphoreType.DMA((len(arguments),)),
            pltpu.SemaphoreType.DMA((5,)),
            pltpu.SemaphoreType.DMA((8, devices)),
            pltpu.SemaphoreType.DMA((8, devices)),
        ],
        compiler_params=pltpu.CompilerParams(
            collective_id=0, has_side_effects=True, vmem_limit_bytes=LIMIT
        ),
    )(*arguments)
    found = pl.pallas_call(
        unpack_kernel,
        out_shape=out_shapes,
        in_specs=[pl.BlockSpec(memory_space=pltpu.VMEM)] * 5,
        out_specs=(in_hbm,) * 5,
        scratch_shapes=[
            *(pltpu.VMEM(value.shape, value.dtype) for value in out_shapes),
            *[pltpu.VMEM((rows + 2 * RIM, channels), full)] * 2,
            pltpu.VMEM((3, channels // LANES, rows + 2 * RIM, LANES), full),
            pltpu.SemaphoreType.DMA((8,)),
        ],
        compiler_params=pltpu.CompilerParams(vmem_limit_bytes=LIMIT),
    )(*packed)
    return (*found[:4], found[4][0])


def with_halo(block, sides, width):
    for axis, dim in sides:
        count = lax.axis_size(axis)
        forward = [(i, i + 1) for i in range(count - 1)]
        forward.append((count - 1, 0))
        backward = [(target, source) for source, target in forward]
        low = lax.ppermute(
            lax.slice_in_dim(block, block.shape[dim] - width, None, axis=dim), axis, forward
        )
        high = lax.ppermute(lax.slice_in_dim(block, 0, width, axis=dim), axis, backward)
        block = jnp.concatenate([low, block, high], axis=dim)
    return block


def dft_tables(extent):
    indices = jnp.arange(extent, dtype=jnp.int32)
    angles = (indices[:, None] * indices[None, :] % extent).astype(jnp.float32) * (
        2.0 * math.pi / extent
    )
    return (jnp.cos(angles), jnp.sin(angles))


def apply_along(matrix, signal, axis_dim):
    letters = "wxyz"
    target = letters[:axis_dim] + "k" + letters[axis_dim + 1 :]
    return jnp.einsum(
        "k" + letters[axis_dim] + "," + letters + "->" + target, matrix, signal, precision=HIGHEST
    )


def forward_section(real_part, imaginary, axis_dim):
    cosine, sine_table = dft_tables(real_part.shape[axis_dim])
    out_real = apply_along(cosine, real_part, axis_dim)
    out_imag = -apply_along(sine_table, real_part, axis_dim)
    if imaginary is not None:
        out_real = out_real + apply_along(sine_table, imaginary, axis_dim)
        out_imag = out_imag + apply_along(cosine, imaginary, axis_dim)
    return (out_real, out_imag)


def inverse_section(real_part, imaginary, axis_dim, keep_imag):
    cosine, sine_table = dft_tables(real_part.shape[axis_dim])
    out_real = apply_along(cosine, real_part, axis_dim) - apply_along(
        sine_table, imaginary, axis_dim
    )
    if keep_imag:
        return (
            out_real,
            apply_along(sine_table, real_part, axis_dim) + apply_along(cosine, imaginary, axis_dim),
        )
    return (out_real, None)


def twist(real_part, imaginary, angles, sign_factor):
    cosine = jnp.cos(angles)
    sine_table = jnp.sin(angles)
    return (
        real_part * cosine + sign_factor * imaginary * sine_table,
        imaginary * cosine - sign_factor * real_part * sine_table,
    )


def twiddle(low_index, high_index, extent):
    return (low_index * high_index % extent).astype(jnp.float32) * (2.0 * math.pi / extent)


def block_angles(devices, portion, extent):
    low_index = jnp.arange(devices, dtype=jnp.int32)[None, :, None, None]
    high_index = (lax.axis_index("seq") * portion + jnp.arange(portion, dtype=jnp.int32))[
        None, None, :, None
    ]
    return twiddle(low_index, high_index, extent)


def sequence_forward(signals, extent):
    devices = lax.axis_size("seq")
    portion = signals.shape[1] // devices
    columns = lax.all_to_all(signals[:, None], "seq", split_axis=2, concat_axis=1, tiled=True)
    real_part, imaginary = forward_section(columns, None, 1)
    real_part, imaginary = twist(real_part, imaginary, block_angles(devices, portion, extent), 1.0)
    spread = (
        lax.all_to_all(real_part, "seq", split_axis=1, concat_axis=2, tiled=True),
        lax.all_to_all(imaginary, "seq", split_axis=1, concat_axis=2, tiled=True),
    )
    return forward_section(spread[0], spread[1], 2)


def sequence_inverse(real_part, imaginary, extent):
    devices = lax.axis_size("seq")
    portion = real_part.shape[2] // devices
    real_part, imaginary = inverse_section(real_part, imaginary, 2, True)
    gathered = (
        lax.all_to_all(real_part, "seq", split_axis=2, concat_axis=1, tiled=True),
        lax.all_to_all(imaginary, "seq", split_axis=2, concat_axis=1, tiled=True),
    )
    real_part, imaginary = twist(
        gathered[0], gathered[1], block_angles(devices, portion, extent), -1.0
    )
    pieces = inverse_section(real_part, imaginary, 1, False)[0] * (1.0 / extent)
    blocks = lax.all_to_all(pieces, "seq", split_axis=1, concat_axis=2, tiled=True)
    return blocks[:, 0]


def body(projected, long_filter, short_kernel, skip_gain, cotangent):
    rows_here = projected.shape[1]
    extent = rows_here * lax.axis_size("seq")
    factor = 1.0 / math.sqrt(extent)
    kernel_span = short_kernel.shape[1]
    margin = kernel_span // 2
    padded = with_halo(projected, (("seq", 1),), margin)
    shorts = jnp.zeros(projected.shape, jnp.float32)
    for offset in range(kernel_span):
        shorts = shorts + short_kernel[:, offset][:, None, :] * padded[
            :, offset : offset + rows_here
        ].astype(jnp.float32)
    gated_signal = shorts[1] * shorts[2]
    transform, restore = (sequence_forward, sequence_inverse)
    upstream = cotangent.astype(jnp.float32)
    grad_response = upstream * shorts[0]
    spec_real, spec_imag = transform(jnp.stack([gated_signal, long_filter]), extent)
    gated_real, gated_imag = (spec_real[0], spec_imag[0])
    filter_real, filter_imag = (spec_real[1] * factor, spec_imag[1] * factor)
    product_real = filter_real * gated_real - filter_imag * gated_imag
    product_imag = filter_real * gated_imag + filter_imag * gated_real
    convolved = restore(product_real[None], product_imag[None], extent)[0]
    upstream_real, upstream_imag = transform(grad_response[None], extent)
    upstream_real, upstream_imag = (upstream_real[0], upstream_imag[0])
    back_real = jnp.stack(
        [
            filter_real * upstream_real + filter_imag * upstream_imag,
            gated_real * upstream_real + gated_imag * upstream_imag,
        ]
    )
    back_imag = jnp.stack(
        [
            filter_real * upstream_imag - filter_imag * upstream_real,
            gated_real * upstream_imag - gated_imag * upstream_real,
        ]
    )
    restored = restore(back_real, back_imag, extent)
    grad_gated = restored[0] + skip_gain * grad_response
    filter_grad = restored[1] * factor
    response = convolved + skip_gain * gated_signal
    layer_output = (response * shorts[0]).astype(jnp.bfloat16)
    grad_shorts = jnp.stack([upstream * response, grad_gated * shorts[2], grad_gated * shorts[1]])
    rimmed = with_halo(grad_shorts, (("seq", 1),), margin)
    stream_sum = jnp.zeros(grad_shorts.shape, jnp.float32)
    kernel_terms = []
    for offset in range(kernel_span):
        start_row = 2 * margin - offset
        stream_sum = (
            stream_sum
            + short_kernel[:, offset][:, None, :] * rimmed[:, start_row : start_row + rows_here]
        )
        kernel_terms.append(
            jnp.sum(
                grad_shorts * padded[:, offset : offset + rows_here].astype(jnp.float32), axis=1
            )
        )
    kernel_part = jnp.stack(kernel_terms, axis=1)
    skip_part = jnp.sum(grad_response * gated_signal, axis=0)
    kernel_total, skip_total = lax.psum((kernel_part, skip_part), "seq")
    return (
        layer_output,
        stream_sum.astype(jnp.bfloat16),
        filter_grad,
        kernel_total * factor,
        skip_total * factor,
    )


def solution(mesh):
    placed = (
        P(None, ("groups", "seq"), "chan"),
        P(("groups", "seq"), "chan"),
        P(None, None, "chan"),
        P("chan"),
        P(("groups", "seq"), "chan"),
    )
    devices = mesh.shape["seq"]

    def run(projected, *others):
        rows, channels = projected.shape[1:]
        if channels == HALF * devices and rows == LANES and devices & (devices - 1) == 0:
            return packed_body(devices, projected, *others)
        return body(projected, *others)

    return jax.shard_map(
        run,
        mesh=mesh,
        in_specs=placed,
        out_specs=(
            P(("groups", "seq"), "chan"),
            P(None, ("groups", "seq"), "chan"),
            P(("groups", "seq"), "chan"),
            P("groups", None, "chan"),
            P(("groups", "chan")),
        ),
        check_vma=False,
    )
```

```python
import functools
import math

import jax
import jax.numpy as jnp
import ml_dtypes
import numpy as np
from jax import lax
from jax.experimental import pallas as pl
from jax.experimental.pallas import tpu as pltpu
from jax.sharding import PartitionSpec as P

HIGHEST = lax.Precision.HIGHEST
LANES = 128
HALF = LANES // 2
RIM = 8
LIMIT = 20 * 1024 * 1024
BEND = 15.0
SPREAD = 251.0 * math.log(2.0) / math.log(1.0 + BEND)
LOWEST = -125.0 * math.log(2.0)
TINY = 1e-35


def turned(value, step, extent):
    real_part, imaginary = value
    step = step % extent
    if step == 0:
        return value
    if 2 * step == extent:
        return (-real_part, None if imaginary is None else -imaginary)
    if 4 * step == extent:
        return (None if imaginary is None else -imaginary, real_part)
    if 4 * step == 3 * extent:
        return (imaginary, -real_part)
    cosine = math.cos(2.0 * math.pi * step / extent)
    sine = math.sin(2.0 * math.pi * step / extent)
    if imaginary is None:
        return (real_part * cosine, real_part * sine)
    return (real_part * cosine - imaginary * sine, imaginary * cosine + real_part * sine)


def part_sum(left, right, sign):
    if right is None:
        return left
    if left is None:
        return right if sign > 0 else -right
    return left + right if sign > 0 else left - right


def real_spectrum(values):
    extent = len(values)
    if extent == 2:
        return [(values[0] + values[1], None), (values[0] - values[1], None)]
    even, odd = real_spectrum(values[0::2]), real_spectrum(values[1::2])
    half = extent // 2

    def entry(spectrum, index):
        index = index % half
        if 2 * index <= half:
            return spectrum[index]
        real_part, imaginary = spectrum[half - index]
        return (real_part, None if imaginary is None else -imaginary)

    found = []
    for index in range(half + 1):
        left, right = entry(even, index), turned(entry(odd, index), -index, extent)
        found.append((part_sum(left[0], right[0], 1), part_sum(left[1], right[1], 1)))
    return found


def real_values(spectrum):
    extent = 2 * (len(spectrum) - 1)
    if extent == 2:
        first, last = spectrum[0][0], spectrum[1][0]
        return [first + last, first - last]
    half = extent // 2
    even, odd = [], []
    for index in range(half // 2 + 1):
        real_part, imaginary = spectrum[index]
        if 2 * index == half:
            even.append((2.0 * real_part, None))
            odd.append((-2.0 * imaginary, None))
            continue
        other_real, other_imag = spectrum[half - index]
        even.append(
            (real_part + other_real, part_sum(imaginary, other_imag, -1))
        )
        odd.append(
            turned(
                (real_part - other_real, part_sum(imaginary, other_imag, 1)), index, extent
            )
        )
    found = [None] * extent
    found[0::2] = real_values(even)
    found[1::2] = real_values(odd)
    return found


def fine_tables(slabs, width):
    extent = slabs * width
    coarse = np.arange(slabs // 2 + 1)[:, None, None]
    fine = np.arange(width)[None, :, None]
    place = np.arange(width)[None, None, :]
    angles = ((coarse + slabs * fine) * place % extent) * (2.0 * np.pi / extent)
    cosine, sine = np.cos(angles), np.sin(angles)
    table = np.concatenate(
        [np.concatenate([cosine, sine], 2), np.concatenate([-sine, cosine], 2)], 1
    )
    inverse = np.swapaxes(table, 1, 2) / (extent * math.sqrt(extent))
    return table.astype(np.float32), inverse.astype(np.float32)


def low_lanes(shape):
    return lax.broadcasted_iota(jnp.int32, shape, len(shape) - 1) < HALF


def swap(value):
    return pltpu.roll(value, HALF, 1)


def wide(value):
    return value.astype(jnp.float32)


def join(first, second, parity):
    low = low_lanes(first.shape)
    if parity == 0:
        return jnp.where(low, first, swap(second))
    return jnp.where(low, swap(first), second)


def split(first, second):
    return join(first, second, 0), join(first, second, 1)


def bend_of(top):
    return jnp.where(top > TINY, BEND / jnp.maximum(top, TINY), 0.0)


def rounded_top(value):
    top = jnp.max(jnp.abs(value), axis=0, keepdims=True)
    return wide((top * (1.0 + 2.0**-7)).astype(jnp.bfloat16))


def sums_tops(tops, span, middle):
    low = low_lanes((1, LANES))
    last = jnp.where(low, tops[1], tops[2])
    return jnp.concatenate([tops[0]] * span + [tops[1]] * (middle - 1) + [last], axis=0)


def encode(value, bend):
    size = jnp.exp(SPREAD * jnp.log(1.0 + jnp.abs(value) * bend) + LOWEST)
    return jnp.where(value < 0.0, -size, size)


def decode(code, top):
    size = (jnp.exp((jnp.log(jnp.abs(code)) - LOWEST) * (1.0 / SPREAD)) - 1.0) * (top / BEND)
    return jnp.where(code < 0.0, -size, size)


def halves(value):
    coarse = value.astype(jnp.bfloat16)
    return coarse, (value - wide(coarse)).astype(jnp.bfloat16)


def apply_table(table, index, value):
    coarse, rest = halves(value)
    depth = coarse.shape[0]
    return jnp.dot(
        table[index],
        jnp.concatenate([coarse, coarse], axis=0),
        preferred_element_type=jnp.float32,
    ) + jnp.dot(table[index, :, :depth], rest, preferred_element_type=jnp.float32)


def layer_kernel(
    devices,
    projected_in,
    cotangent_in,
    filter_in,
    taps_in,
    gain_in,
    forward_in,
    inverse_in,
    recv_conv,
    recv_back,
    recv_sums,
    kept_out,
    taps_out,
    projected_ref,
    cotangent_ref,
    filter_ref,
    taps_ref,
    gain_ref,
    forward_ref,
    inverse_ref,
    send_first,
    recv_first,
    send_second,
    recv_second,
    send_filter,
    recv_filter,
    send_top,
    recv_top,
    send_rim,
    recv_rim,
    send_conv,
    send_back,
    send_sums,
    around,
    kept,
    first_rim,
    second_rim,
    first_short,
    signal,
    upstream,
    response,
    back,
    signal_spectra,
    product_spectra,
    load_sem,
    keep_sem,
    send_sem,
    recv_sem,
):
    hops = [(devices // 2 + (-1) ** i * ((i + 1) // 2)) for i in range(devices - 1)]
    arguments = (projected_in, cotangent_in, filter_in, taps_in, gain_in, forward_in, inverse_in)
    held = (
        projected_ref,
        cotangent_ref,
        filter_ref,
        taps_ref,
        gain_ref,
        forward_ref,
        inverse_ref,
    )
    loads = [
        pltpu.make_async_copy(source, target, load_sem.at[index])
        for index, (source, target) in enumerate(zip(arguments, held))
    ]
    for load in loads:
        load.start()
    rows, channels = cotangent_ref.shape
    tiles = channels // LANES
    span = taps_ref.shape[1]
    margin = span // 2
    width = rows // 2
    slabs = 2 * devices
    extent = rows * devices
    factor = 1.0 / math.sqrt(extent)
    me = lax.axis_index("seq")
    odd = lax.rem(me, 2) == 1

    def copy_to(kind, hop, source, target, peer):
        return pltpu.make_async_remote_copy(
            src_ref=source,
            dst_ref=target,
            send_sem=send_sem.at[kind, hop],
            recv_sem=recv_sem.at[kind, hop],
            device_id={"seq": peer},
            device_id_type=pl.DeviceIdType.MESH,
        )

    def peer_at(hop):
        return lax.rem(me + hop, devices)

    def source_at(hop):
        return lax.rem(me + devices - hop, devices)

    barrier = pltpu.get_barrier_semaphore()
    for hop in hops:
        pl.semaphore_signal(
            barrier, inc=1, device_id={"seq": peer_at(hop)}, device_id_type=pl.DeviceIdType.MESH
        )

    loads[0].wait()
    loads[1].wait()

    def lanes_of(peer):
        return pl.ds(pl.multiple_of((peer // 2) * LANES, LANES), LANES)

    def join_for(peer, first, second):
        flip = lax.rem(peer, 2) == 1
        return jnp.where(
            low_lanes(first.shape),
            jnp.where(flip, swap(first), first),
            jnp.where(flip, second, swap(second)),
        ).astype(jnp.bfloat16)

    def pack_first(peer, target):
        lanes = lanes_of(peer)
        target[...] = join_for(
            peer, wide(projected_ref[1, :, lanes]), wide(projected_ref[2, :, lanes])
        )

    def pack_second(peer, target):
        lanes = lanes_of(peer)
        target[...] = join_for(
            peer, wide(projected_ref[0, :, lanes]), wide(cotangent_ref[:, lanes])
        )

    for side, start in enumerate((0, rows - 2 * RIM)):
        part = slice(0, RIM) if side == 0 else slice(RIM, 2 * RIM)
        ends = [wide(projected_ref[s, start : start + 2 * RIM])[part] for s in range(3)]
        ends.append(wide(cotangent_ref[start : start + 2 * RIM])[part])
        for pair in range(2):
            send_rim[side, pair] = jnp.concatenate(ends[2 * pair : 2 * pair + 2], axis=0).astype(
                jnp.bfloat16
            )
    rim_copies = [
        copy_to(7, hop, send_rim.at[side], recv_rim.at[side], peer_at(hop))
        for side, hop in enumerate((devices - 1, 1))
    ]
    for place, hop in enumerate(hops):
        peer = peer_at(hop)
        pack_first(peer, send_first.at[peer])
        if place == 0:
            pl.semaphore_wait(barrier, devices - 1)
        copy_to(0, hop, send_first.at[peer], recv_first.at[me], peer).start()

    loads[2].wait()
    for tile in range(tiles):
        lanes = slice(tile * LANES, (tile + 1) * LANES)
        whole = filter_ref[:, lanes]
        top = jnp.max(jnp.abs(whole), axis=0, keepdims=True)
        coded = encode(whole, bend_of(top))
        for half in range(2):
            send_filter[2 * tile + half] = join(coded[:width], coded[width:], half).astype(
                jnp.bfloat16
            )
            send_top[2 * tile + half] = join(top, top, half)
    for hop in hops:
        peer = peer_at(hop)
        copy_to(2, hop, send_filter.at[peer], recv_filter.at[me], peer).start()
        copy_to(3, hop, send_top.at[peer], recv_top.at[me], peer).start()
    for hop in hops:
        peer = peer_at(hop)
        pack_second(peer, send_second.at[peer])
        copy_to(1, hop, send_second.at[peer], recv_second.at[me], peer).start()
    pack_first(me, recv_first.at[me])
    pack_second(me, recv_second.at[me])
    recv_filter[me] = send_filter[me]
    recv_top[me] = send_top[me]

    for load in loads[3:5]:
        load.wait()
    own = pl.ds(pl.multiple_of((me // 2) * LANES, LANES), LANES)

    def own_pair(first, second):
        return jnp.where(odd, join(first, second, 1), join(first, second, 0))

    gate_taps, left_taps, right_taps = [taps_ref[s, :, own] for s in range(3)]
    first_taps = own_pair(left_taps, right_taps)
    centre = wide(lax.broadcasted_iota(jnp.int32, (span, LANES), 0) == margin)
    second_taps = jnp.where(low_lanes((span, LANES)), own_pair(gate_taps, gate_taps), centre)
    own_gain = gain_ref[:, own]
    gain = own_pair(own_gain, own_gain)

    def wait_from(kind, source, target):
        for hop in hops:
            copy_to(
                kind, hop, source.at[peer_at(hop)], target.at[source_at(hop)], peer_at(hop)
            ).wait()

    def close_rim(rim):
        rim[0:RIM] = rim[extent : extent + RIM]
        rim[extent + RIM : extent + 2 * RIM] = rim[RIM : 2 * RIM]

    def open_rim(rim, received):
        for block in range(devices):
            rim[RIM + block * rows : RIM + (block + 1) * rows] = wide(received[block])
        close_rim(rim)

    def filtered(rim, taps, start):
        near = rim[pl.ds(start, width + 2 * RIM)]
        total = jnp.zeros((width, LANES), jnp.float32)
        for tap in range(span):
            low = RIM + tap - margin
            total = total + taps[tap : tap + 1] * near[low : low + width]
        return total

    wait_from(0, send_first, recv_first)
    open_rim(first_rim, recv_first)

    def shorten_first(slab, carry):
        start = pl.multiple_of(slab * width, width)
        total = filtered(first_rim, first_taps, start)
        first_short[pl.ds(start, width)] = total
        signal[pl.ds(start, width)] = total * swap(total)
        return carry

    lax.fori_loop(0, slabs, shorten_first, 0)
    for load in loads[5:]:
        load.wait()
    wait_from(2, send_filter, recv_filter)
    wait_from(3, send_top, recv_top)

    def put_spectrum(spectra, found, start, count):
        for index, (real_part, imaginary) in enumerate(found):
            if imaginary is None:
                imaginary = jnp.zeros_like(real_part)
            spectra[index, pl.ds(start, count)] = real_part
            spectra[index, pl.ds(width + start, count)] = imaginary

    def get_spectrum(spectra, start, count):
        found = []
        for index in range(slabs // 2 + 1):
            imaginary = None
            if 0 < index < slabs // 2:
                imaginary = spectra[index, pl.ds(width + start, count)]
            found.append((spectra[index, pl.ds(start, count)], imaginary))
        return found

    def first_spectrum(step, carry):
        start = pl.multiple_of(step * 16, 16)
        low = low_lanes((16, LANES))
        values = []
        for block in range(devices):
            found = decode(wide(recv_filter[block, pl.ds(start, 16)]), recv_top[block])
            for half in range(2):
                here = signal[pl.ds(block * rows + half * width + start, 16)]
                values.append(jnp.where(low, here, swap(found) if half == 0 else found))
        put_spectrum(signal_spectra, real_spectrum(values), start, 16)
        return carry

    lax.fori_loop(0, width // 16, first_spectrum, 0)

    for index in range(slabs // 2 + 1):
        found = apply_table(forward_ref, index, signal_spectra[index])
        signal_spectra[index] = found
        real_part, imaginary = found[:width], found[width:]
        other_real, other_imag = swap(real_part), swap(imaginary)
        product = jnp.concatenate(
            [
                real_part * other_real - imaginary * other_imag,
                real_part * other_imag + imaginary * other_real,
            ],
            axis=0,
        )
        product_spectra[index] = apply_table(inverse_ref, index, product)

    def first_back(step, top):
        start = pl.multiple_of(step * 8, 8)
        for slab, value in enumerate(real_values(get_spectrum(product_spectra, start, 8))):
            place = pl.ds(slab * width + start, 8)
            whole = value + gain * signal[place]
            response[place] = whole
            top = jnp.maximum(top, jnp.abs(whole))
        return top

    nothing = jnp.zeros((8, LANES), jnp.float32)
    top = lax.fori_loop(0, width // 8, first_back, nothing)
    response_top = rounded_top(top)
    response_bend = bend_of(response_top)

    def step_hop(step):
        return devices // 2 + (step + 1) // 2 * (1 - 2 * lax.rem(step, 2))

    def pack_conv(peer):
        start = pl.multiple_of(peer * rows, rows)
        folded = jnp.where(
            low_lanes((width, LANES)),
            response[pl.ds(start, width)],
            response[pl.ds(start + width, width)],
        )
        send_conv[peer] = encode(folded, response_bend).astype(jnp.bfloat16)

    def step_conv(step, carry):
        hop = step_hop(step)
        peer = peer_at(hop)
        pack_conv(peer)
        copy_to(4, hop, send_conv.at[peer], recv_conv.at[me], peer).start()
        return carry

    lax.fori_loop(0, devices - 1, step_conv, 0)
    pack_conv(me)
    for copy in rim_copies:
        copy.start()
    keeps = [
        pltpu.make_async_copy(source, target.at[me], keep_sem.at[index])
        for index, (source, target) in enumerate(
            (
                (send_conv.at[me], recv_conv),
                (send_back.at[me], recv_back),
                (send_sums, recv_sums),
            )
        )
    ]
    keeps[0].start()

    wait_from(1, send_second, recv_second)
    open_rim(second_rim, recv_second)

    def shorten_second(slab, carry):
        start = pl.multiple_of(slab * width, width)
        total = filtered(second_rim, second_taps, start)
        total = total * swap(total)
        upstream[pl.ds(start, width)] = total
        return carry + jnp.sum(
            (total * signal[pl.ds(start, width)]).reshape(-1, 8, LANES), axis=0
        )

    gain_sum = lax.fori_loop(0, slabs, shorten_second, nothing, unroll=2)

    def second_spectrum(step, carry):
        start = pl.multiple_of(step * 8, 8)
        values = [upstream[pl.ds(slab * width + start, 8)] for slab in range(slabs)]
        put_spectrum(product_spectra, real_spectrum(values), start, 8)
        return carry

    lax.fori_loop(0, width // 8, second_spectrum, 0, unroll=2)

    for index in range(slabs // 2 + 1):
        found = apply_table(forward_ref, index, product_spectra[index])
        real_part, imaginary = found[:width], found[width:]
        other_real = swap(signal_spectra[index, :width])
        other_imag = swap(signal_spectra[index, width:])
        product = jnp.concatenate(
            [
                real_part * other_real + imaginary * other_imag,
                imaginary * other_real - real_part * other_imag,
            ],
            axis=0,
        )
        product_spectra[index] = apply_table(inverse_ref, index, product)

    low_gain = jnp.where(low_lanes((1, LANES)), gain, 0.0)

    def second_back(step, top):
        start = pl.multiple_of(step * 8, 8)
        for slab, value in enumerate(real_values(get_spectrum(product_spectra, start, 8))):
            place = pl.ds(slab * width + start, 8)
            whole = value + low_gain * upstream[place]
            back[place] = whole
            top = jnp.maximum(top, jnp.abs(whole))
        return top

    top = lax.fori_loop(0, width // 8, second_back, nothing, unroll=2)
    back_top = rounded_top(top)
    back_bend = bend_of(back_top)
    rim_bend = jnp.where(low_lanes((1, LANES)), back_bend, response_bend)

    def pack_back(peer):
        start = pl.multiple_of(peer * rows, rows)
        send_back[peer, 0:rows] = encode(back[pl.ds(start, rows)], back_bend).astype(jnp.bfloat16)
        places = (
            lax.rem(start + extent - RIM, extent),
            lax.rem(start + rows, extent),
        )
        ends = []
        for place in places:
            here = pl.ds(pl.multiple_of(place, RIM), RIM)
            ends.append(jnp.where(low_lanes((RIM, LANES)), back[here], response[here]))
        send_back[peer, rows : rows + 2 * RIM] = encode(
            jnp.concatenate(ends, axis=0), rim_bend
        ).astype(jnp.bfloat16)

    def step_back(step, carry):
        hop = step_hop(step)
        peer = peer_at(hop)
        pack_back(peer)
        copy_to(5, hop, send_back.at[peer], recv_back.at[me], peer).start()
        return carry

    lax.fori_loop(0, devices - 1, step_back, 0)
    pack_back(me)
    keeps[1].start()

    def add_sums(slab, sums):
        sums = list(sums)
        start = pl.multiple_of(slab * width, width)
        here = pl.ds(start, width)
        low = low_lanes((width, LANES))
        grad = back[here]
        grad = jnp.where(low, grad, swap(grad)) * swap(first_short[here])
        near_first = first_rim[pl.ds(start, width + 2 * RIM)]
        near_second = second_rim[pl.ds(start, width + 2 * RIM)]
        other = response[here] * swap(near_second[RIM : RIM + width])
        for tap in range(span):
            inner = slice(RIM + tap - margin, RIM + tap - margin + width)
            for which, (grads, near) in enumerate(((grad, near_first), (other, near_second))):
                sums[which * span + tap] = sums[which * span + tap] + jnp.sum(
                    (grads * near[inner]).reshape(-1, 8, LANES), axis=0
                )
        return tuple(sums)

    sums = lax.fori_loop(0, slabs, add_sums, (nothing,) * (2 * span))
    sums = [factor * jnp.sum(value, axis=0, keepdims=True) for value in sums + (gain_sum,)]
    middle = (span + 1) // 2
    low = low_lanes((1, LANES))
    parts = sums[:span] + [join(sums[i], sums[i + middle], 0) for i in range(span, span + middle)]
    last = parts[-1]
    tops = [
        rounded_top(jnp.concatenate(parts[:span], axis=0)),
        rounded_top(jnp.concatenate(parts[span:-1] + [jnp.where(low, last, 0.0)], axis=0)),
        rounded_top(last),
    ]
    coded = encode(jnp.concatenate(parts, axis=0), bend_of(sums_tops(tops, span, middle)))
    send_sums[...] = jnp.concatenate([coded, *tops, response_top, back_top], axis=0).astype(
        jnp.bfloat16
    )
    for hop in hops:
        copy_to(6, hop, send_sums, recv_sums.at[me], peer_at(hop)).start()
    keeps[2].start()

    for copy in rim_copies:
        copy.wait()
    for stream in range(4):
        around[stream, 0:RIM] = jnp.zeros((RIM, channels), jnp.float32)
        around[stream, rows + 3 * RIM :] = jnp.zeros((RIM, channels), jnp.float32)
        half = slice((stream % 2) * RIM, (stream % 2 + 1) * RIM)
        before, after = wide(recv_rim[1, stream // 2])[half], wide(recv_rim[0, stream // 2])[half]
        around[stream, RIM : 2 * RIM] = before
        around[stream, rows + 2 * RIM : rows + 3 * RIM] = after
        source = cotangent_ref[...] if stream == 3 else projected_ref[stream]
        around[stream, 2 * RIM : 2 * RIM + rows] = wide(source)
    kept[3] = around[3, RIM : rows + 3 * RIM]

    def own_short(step, carry):
        stream, tile = step // tiles, lax.rem(step, tiles)
        lanes = pl.ds(pl.multiple_of(tile * LANES, LANES), LANES)
        taps = taps_ref[stream, :, lanes]
        for part in range(2):
            count = width + RIM
            total = jnp.zeros((count, LANES), jnp.float32)
            for tap in range(span):
                low = part * count + RIM + tap - margin
                total = total + taps[tap : tap + 1] * around[stream, low : low + count, lanes]
            kept[stream, part * count : (part + 1) * count, lanes] = total
        return carry

    lax.fori_loop(0, 3 * tiles, own_short, 0)
    keeping = pltpu.make_async_copy(kept, kept_out, keep_sem.at[3])
    keeping.start()
    passing = pltpu.make_async_copy(taps_ref, taps_out, keep_sem.at[4])
    passing.start()

    keeping.wait()
    passing.wait()
    for keep in keeps:
        keep.wait()
    wait_from(4, send_conv, recv_conv)
    wait_from(5, send_back, recv_back)
    for hop in hops:
        copy_to(6, hop, send_sums, recv_sums.at[source_at(hop)], peer_at(hop)).wait()


def unpack_kernel(*refs):
    held, results, refs = refs[:5], refs[5:10], refs[10:]
    output_ref, streams_ref, filter_grad_ref, taps_grad_ref, gain_grad_ref = refs[:5]
    recv_conv, recv_back, recv_sums, kept, taps_ref = held
    response, grad, grads, store_sem = refs[5:]
    tiles = recv_conv.shape[0] // 2
    rows = output_ref.shape[0]
    span = taps_grad_ref.shape[1]
    margin = span // 2
    middle = (span + 1) // 2
    stores = [
        pltpu.make_async_copy(refs[i], results[i], store_sem.at[i]) for i in (0, 2, 3, 4)
    ]
    streams = [
        pltpu.make_async_copy(streams_ref.at[i], results[1].at[i], store_sem.at[5 + i])
        for i in range(3)
    ]
    main = slice(RIM, RIM + rows)
    ends = (slice(0, RIM), slice(RIM + rows, rows + 2 * RIM))
    for tile in range(tiles):
        lanes = slice(tile * LANES, (tile + 1) * LANES)
        low = low_lanes((1, LANES))
        tops = [wide(recv_sums[2 * tile + half]) for half in range(2)]
        response_top, back_top = [
            [top[span + middle + i : span + middle + i + 1] for top in tops] for i in (3, 4)
        ]
        found = [decode(wide(recv_back[2 * tile + i, 0:rows]), back_top[i]) for i in range(2)]
        grad[main, lanes], filter_grad_ref[:, lanes] = split(*found)
        rims = [
            decode(
                wide(recv_back[2 * tile + i, rows : rows + 2 * RIM]),
                jnp.where(low, back_top[i], response_top[i]),
            )
            for i in range(2)
        ]
        for target, rim in zip((grad, response), split(*rims)):
            for index, place in enumerate(ends):
                target[place, lanes] = rim[index * RIM : (index + 1) * RIM]
    stores[1].start()
    for tile in range(tiles):
        lanes = slice(tile * LANES, (tile + 1) * LANES)
        tops = [wide(recv_sums[2 * tile + half]) for half in range(2)]
        count = span + middle
        low_part, high_part = split(
            *(
                decode(
                    top[:count],
                    sums_tops([top[count + i : count + i + 1] for i in range(3)], span, middle),
                )
                for top in tops
            )
        )
        taps_grad_ref[1, :, lanes] = low_part[0:span]
        taps_grad_ref[2, :, lanes] = high_part[0:span]
        taps_grad_ref[0, :middle, lanes] = low_part[span : span + middle]
        taps_grad_ref[0, middle:, lanes] = high_part[span : 2 * span - middle]
        gain_grad_ref[:, lanes] = high_part[2 * span - middle : 2 * span - middle + 1]
        pieces = split(
            *(
                decode(
                    wide(recv_conv[2 * tile + i]), tops[i][count + 3 : count + 4]
                )
                for i in range(2)
            )
        )
        whole = jnp.concatenate(pieces, axis=0)
        response[main, lanes] = whole
        output_ref[:, lanes] = (whole * kept[0, main, lanes]).astype(jnp.bfloat16)
    for index in (0, 2, 3):
        stores[index].start()
    for stream, (value, other) in enumerate(((response, 3), (grad, 2), (grad, 1))):
        for tile in range(tiles):
            lanes = slice(tile * LANES, (tile + 1) * LANES)
            grads[stream, tile] = value[:, lanes] * kept[other, :, lanes]
            taps = taps_ref[stream, :, lanes]
            total = jnp.zeros((rows, LANES), jnp.float32)
            for tap in range(span):
                first = RIM + margin - tap
                total = total + taps[tap : tap + 1] * grads[stream, tile, first : first + rows]
            streams_ref[stream, :, lanes] = total.astype(jnp.bfloat16)
        streams[stream].start()
    for store in stores + streams:
        store.wait()


def halved(table):
    coarse = table.astype(ml_dtypes.bfloat16)
    rest = (table - coarse.astype(np.float32)).astype(ml_dtypes.bfloat16)
    return np.concatenate([coarse, rest], axis=2)


def packed_body(devices, projected, long_filter, short_kernel, skip_gain, cotangent):
    rows, channels = long_filter.shape
    span = short_kernel.shape[1]
    extent = rows * devices
    slabs = 2 * devices
    width = rows // 2
    tables = [halved(table) for table in fine_tables(slabs, width)]
    sums_rows = span + (span + 1) // 2 + 5
    block = (devices, rows, LANES)
    half_block = (devices, width, LANES)
    longer = (devices, rows + 2 * RIM, LANES)
    narrow, full = jnp.bfloat16, jnp.float32
    arguments = (projected, cotangent, long_filter, short_kernel, skip_gain[None], *tables)
    in_hbm = pl.BlockSpec(memory_space=pltpu.HBM)
    anywhere = pl.BlockSpec(memory_space=pl.ANY)
    arguments = [pltpu.with_memory_space_constraint(value, pltpu.HBM) for value in arguments]
    packed_shapes = (
        jax.ShapeDtypeStruct(half_block, narrow),
        jax.ShapeDtypeStruct(longer, narrow),
        jax.ShapeDtypeStruct((devices, sums_rows, LANES), narrow),
        jax.ShapeDtypeStruct((4, rows + 2 * RIM, channels), full),
        jax.ShapeDtypeStruct(short_kernel.shape, full),
    )
    out_shapes = (
        jax.ShapeDtypeStruct((rows, channels), narrow),
        jax.ShapeDtypeStruct((3, rows, channels), narrow),
        jax.ShapeDtypeStruct((rows, channels), full),
        jax.ShapeDtypeStruct(short_kernel.shape, full),
        jax.ShapeDtypeStruct((1, channels), full),
    )
    packed = pl.pallas_call(
        functools.partial(layer_kernel, devices),
        out_shape=packed_shapes,
        in_specs=[in_hbm] * 7,
        out_specs=(anywhere,) * 5,
        scratch_shapes=[
            *(pltpu.VMEM(value.shape, value.dtype) for value in arguments),
            pltpu.VMEM(block, narrow),
            pltpu.VMEM(block, narrow),
            pltpu.VMEM(block, narrow),
            pltpu.VMEM(block, narrow),
            pltpu.VMEM(half_block, narrow),
            pltpu.VMEM(half_block, narrow),
            pltpu.VMEM((devices, 1, LANES), full),
            pltpu.VMEM((devices, 1, LANES), full),
            pltpu.VMEM((2, 2, 2 * RIM, channels), narrow),
            pltpu.VMEM((2, 2, 2 * RIM, channels), narrow),
            pltpu.VMEM(half_block, narrow),
            pltpu.VMEM(longer, narrow),
            pltpu.VMEM((sums_rows, LANES), narrow),
            pltpu.VMEM((4, rows + 4 * RIM, channels), full),
            pltpu.VMEM((4, rows + 2 * RIM, channels), full),
            pltpu.VMEM((extent + 2 * RIM, LANES), full),
            pltpu.VMEM((extent + 2 * RIM, LANES), full),
            *[pltpu.VMEM((extent, LANES), full)] * 5,
            *[pltpu.VMEM((slabs // 2 + 1, rows, LANES), full)] * 2,
            pltpu.SemaphoreType.DMA((len(arguments),)),
            pltpu.SemaphoreType.DMA((5,)),
            pltpu.SemaphoreType.DMA((8, devices)),
            pltpu.SemaphoreType.DMA((8, devices)),
        ],
        compiler_params=pltpu.CompilerParams(
            collective_id=0, has_side_effects=True, vmem_limit_bytes=LIMIT
        ),
    )(*arguments)
    found = pl.pallas_call(
        unpack_kernel,
        out_shape=out_shapes,
        in_specs=[pl.BlockSpec(memory_space=pltpu.VMEM)] * 5,
        out_specs=(in_hbm,) * 5,
        scratch_shapes=[
            *(pltpu.VMEM(value.shape, value.dtype) for value in out_shapes),
            *[pltpu.VMEM((rows + 2 * RIM, channels), full)] * 2,
            pltpu.VMEM((3, channels // LANES, rows + 2 * RIM, LANES), full),
            pltpu.SemaphoreType.DMA((8,)),
        ],
        compiler_params=pltpu.CompilerParams(vmem_limit_bytes=LIMIT),
    )(*packed)
    return (*found[:4], found[4][0])


def with_halo(block, sides, width):
    for axis, dim in sides:
        count = lax.axis_size(axis)
        forward = [(i, i + 1) for i in range(count - 1)]
        forward.append((count - 1, 0))
        backward = [(target, source) for source, target in forward]
        low = lax.ppermute(
            lax.slice_in_dim(block, block.shape[dim] - width, None, axis=dim), axis, forward
        )
        high = lax.ppermute(lax.slice_in_dim(block, 0, width, axis=dim), axis, backward)
        block = jnp.concatenate([low, block, high], axis=dim)
    return block


def dft_tables(extent):
    indices = jnp.arange(extent, dtype=jnp.int32)
    angles = (indices[:, None] * indices[None, :] % extent).astype(jnp.float32) * (
        2.0 * math.pi / extent
    )
    return (jnp.cos(angles), jnp.sin(angles))


def apply_along(matrix, signal, axis_dim):
    letters = "wxyz"
    target = letters[:axis_dim] + "k" + letters[axis_dim + 1 :]
    return jnp.einsum(
        "k" + letters[axis_dim] + "," + letters + "->" + target, matrix, signal, precision=HIGHEST
    )


def forward_section(real_part, imaginary, axis_dim):
    cosine, sine_table = dft_tables(real_part.shape[axis_dim])
    out_real = apply_along(cosine, real_part, axis_dim)
    out_imag = -apply_along(sine_table, real_part, axis_dim)
    if imaginary is not None:
        out_real = out_real + apply_along(sine_table, imaginary, axis_dim)
        out_imag = out_imag + apply_along(cosine, imaginary, axis_dim)
    return (out_real, out_imag)


def inverse_section(real_part, imaginary, axis_dim, keep_imag):
    cosine, sine_table = dft_tables(real_part.shape[axis_dim])
    out_real = apply_along(cosine, real_part, axis_dim) - apply_along(
        sine_table, imaginary, axis_dim
    )
    if keep_imag:
        return (
            out_real,
            apply_along(sine_table, real_part, axis_dim) + apply_along(cosine, imaginary, axis_dim),
        )
    return (out_real, None)


def twist(real_part, imaginary, angles, sign_factor):
    cosine = jnp.cos(angles)
    sine_table = jnp.sin(angles)
    return (
        real_part * cosine + sign_factor * imaginary * sine_table,
        imaginary * cosine - sign_factor * real_part * sine_table,
    )


def twiddle(low_index, high_index, extent):
    return (low_index * high_index % extent).astype(jnp.float32) * (2.0 * math.pi / extent)


def block_angles(devices, portion, extent):
    low_index = jnp.arange(devices, dtype=jnp.int32)[None, :, None, None]
    high_index = (lax.axis_index("seq") * portion + jnp.arange(portion, dtype=jnp.int32))[
        None, None, :, None
    ]
    return twiddle(low_index, high_index, extent)


def sequence_forward(signals, extent):
    devices = lax.axis_size("seq")
    portion = signals.shape[1] // devices
    columns = lax.all_to_all(signals[:, None], "seq", split_axis=2, concat_axis=1, tiled=True)
    real_part, imaginary = forward_section(columns, None, 1)
    real_part, imaginary = twist(real_part, imaginary, block_angles(devices, portion, extent), 1.0)
    spread = (
        lax.all_to_all(real_part, "seq", split_axis=1, concat_axis=2, tiled=True),
        lax.all_to_all(imaginary, "seq", split_axis=1, concat_axis=2, tiled=True),
    )
    return forward_section(spread[0], spread[1], 2)


def sequence_inverse(real_part, imaginary, extent):
    devices = lax.axis_size("seq")
    portion = real_part.shape[2] // devices
    real_part, imaginary = inverse_section(real_part, imaginary, 2, True)
    gathered = (
        lax.all_to_all(real_part, "seq", split_axis=2, concat_axis=1, tiled=True),
        lax.all_to_all(imaginary, "seq", split_axis=2, concat_axis=1, tiled=True),
    )
    real_part, imaginary = twist(
        gathered[0], gathered[1], block_angles(devices, portion, extent), -1.0
    )
    pieces = inverse_section(real_part, imaginary, 1, False)[0] * (1.0 / extent)
    blocks = lax.all_to_all(pieces, "seq", split_axis=1, concat_axis=2, tiled=True)
    return blocks[:, 0]


def body(projected, long_filter, short_kernel, skip_gain, cotangent):
    rows_here = projected.shape[1]
    extent = rows_here * lax.axis_size("seq")
    factor = 1.0 / math.sqrt(extent)
    kernel_span = short_kernel.shape[1]
    margin = kernel_span // 2
    padded = with_halo(projected, (("seq", 1),), margin)
    shorts = jnp.zeros(projected.shape, jnp.float32)
    for offset in range(kernel_span):
        shorts = shorts + short_kernel[:, offset][:, None, :] * padded[
            :, offset : offset + rows_here
        ].astype(jnp.float32)
    gated_signal = shorts[1] * shorts[2]
    transform, restore = (sequence_forward, sequence_inverse)
    upstream = cotangent.astype(jnp.float32)
    grad_response = upstream * shorts[0]
    spec_real, spec_imag = transform(jnp.stack([gated_signal, long_filter]), extent)
    gated_real, gated_imag = (spec_real[0], spec_imag[0])
    filter_real, filter_imag = (spec_real[1] * factor, spec_imag[1] * factor)
    product_real = filter_real * gated_real - filter_imag * gated_imag
    product_imag = filter_real * gated_imag + filter_imag * gated_real
    convolved = restore(product_real[None], product_imag[None], extent)[0]
    upstream_real, upstream_imag = transform(grad_response[None], extent)
    upstream_real, upstream_imag = (upstream_real[0], upstream_imag[0])
    back_real = jnp.stack(
        [
            filter_real * upstream_real + filter_imag * upstream_imag,
            gated_real * upstream_real + gated_imag * upstream_imag,
        ]
    )
    back_imag = jnp.stack(
        [
            filter_real * upstream_imag - filter_imag * upstream_real,
            gated_real * upstream_imag - gated_imag * upstream_real,
        ]
    )
    restored = restore(back_real, back_imag, extent)
    grad_gated = restored[0] + skip_gain * grad_response
    filter_grad = restored[1] * factor
    response = convolved + skip_gain * gated_signal
    layer_output = (response * shorts[0]).astype(jnp.bfloat16)
    grad_shorts = jnp.stack([upstream * response, grad_gated * shorts[2], grad_gated * shorts[1]])
    rimmed = with_halo(grad_shorts, (("seq", 1),), margin)
    stream_sum = jnp.zeros(grad_shorts.shape, jnp.float32)
    kernel_terms = []
    for offset in range(kernel_span):
        start_row = 2 * margin - offset
        stream_sum = (
            stream_sum
            + short_kernel[:, offset][:, None, :] * rimmed[:, start_row : start_row + rows_here]
        )
        kernel_terms.append(
            jnp.sum(
                grad_shorts * padded[:, offset : offset + rows_here].astype(jnp.float32), axis=1
            )
        )
    kernel_part = jnp.stack(kernel_terms, axis=1)
    skip_part = jnp.sum(grad_response * gated_signal, axis=0)
    kernel_total, skip_total = lax.psum((kernel_part, skip_part), "seq")
    return (
        layer_output,
        stream_sum.astype(jnp.bfloat16),
        filter_grad,
        kernel_total * factor,
        skip_total * factor,
    )


def solution(mesh):
    placed = (
        P(None, ("groups", "seq"), "chan"),
        P(("groups", "seq"), "chan"),
        P(None, None, "chan"),
        P("chan"),
        P(("groups", "seq"), "chan"),
    )
    devices = mesh.shape["seq"]

    def run(projected, *others):
        rows, channels = projected.shape[1:]
        if channels == HALF * devices and rows == LANES and devices & (devices - 1) == 0:
            return packed_body(devices, projected, *others)
        return body(projected, *others)

    return jax.shard_map(
        run,
        mesh=mesh,
        in_specs=placed,
        out_specs=(
            P(("groups", "seq"), "chan"),
            P(None, ("groups", "seq"), "chan"),
            P(("groups", "seq"), "chan"),
            P("groups", None, "chan"),
            P(("groups", "chan")),
        ),
        check_vma=False,
    )
```

```python
import functools
import math

import jax
import jax.numpy as jnp
import ml_dtypes
import numpy as np
from jax import lax
from jax.experimental import pallas as pl
from jax.experimental.pallas import tpu as pltpu
from jax.sharding import PartitionSpec as P

HIGHEST = lax.Precision.HIGHEST
LANES = 128
HALF = LANES // 2
RIM = 8
LIMIT = 20 * 1024 * 1024
BEND = 15.0
SPREAD = 251.0 * math.log(2.0) / math.log(1.0 + BEND)
LOWEST = -125.0 * math.log(2.0)
TINY = 1e-35


def turned(value, step, extent):
    real_part, imaginary = value
    step = step % extent
    if step == 0:
        return value
    if 2 * step == extent:
        return (-real_part, None if imaginary is None else -imaginary)
    if 4 * step == extent:
        return (None if imaginary is None else -imaginary, real_part)
    if 4 * step == 3 * extent:
        return (imaginary, -real_part)
    cosine = math.cos(2.0 * math.pi * step / extent)
    sine = math.sin(2.0 * math.pi * step / extent)
    if imaginary is None:
        return (real_part * cosine, real_part * sine)
    return (real_part * cosine - imaginary * sine, imaginary * cosine + real_part * sine)


def part_sum(left, right, sign):
    if right is None:
        return left
    if left is None:
        return right if sign > 0 else -right
    return left + right if sign > 0 else left - right


def real_spectrum(values):
    extent = len(values)
    if extent == 2:
        return [(values[0] + values[1], None), (values[0] - values[1], None)]
    even, odd = real_spectrum(values[0::2]), real_spectrum(values[1::2])
    half = extent // 2

    def entry(spectrum, index):
        index = index % half
        if 2 * index <= half:
            return spectrum[index]
        real_part, imaginary = spectrum[half - index]
        return (real_part, None if imaginary is None else -imaginary)

    found = []
    for index in range(half + 1):
        left, right = entry(even, index), turned(entry(odd, index), -index, extent)
        found.append((part_sum(left[0], right[0], 1), part_sum(left[1], right[1], 1)))
    return found


def real_values(spectrum):
    extent = 2 * (len(spectrum) - 1)
    if extent == 2:
        first, last = spectrum[0][0], spectrum[1][0]
        return [first + last, first - last]
    half = extent // 2
    even, odd = [], []
    for index in range(half // 2 + 1):
        real_part, imaginary = spectrum[index]
        if 2 * index == half:
            even.append((2.0 * real_part, None))
            odd.append((-2.0 * imaginary, None))
            continue
        other_real, other_imag = spectrum[half - index]
        even.append(
            (real_part + other_real, part_sum(imaginary, other_imag, -1))
        )
        odd.append(
            turned(
                (real_part - other_real, part_sum(imaginary, other_imag, 1)), index, extent
            )
        )
    found = [None] * extent
    found[0::2] = real_values(even)
    found[1::2] = real_values(odd)
    return found


def fine_tables(slabs, width):
    extent = slabs * width
    coarse = np.arange(slabs // 2 + 1)[:, None, None]
    fine = np.arange(width)[None, :, None]
    place = np.arange(width)[None, None, :]
    angles = ((coarse + slabs * fine) * place % extent) * (2.0 * np.pi / extent)
    cosine, sine = np.cos(angles), np.sin(angles)
    table = np.concatenate(
        [np.concatenate([cosine, sine], 2), np.concatenate([-sine, cosine], 2)], 1
    )
    inverse = np.swapaxes(table, 1, 2) / (extent * math.sqrt(extent))
    return table.astype(np.float32), inverse.astype(np.float32)


def low_lanes(shape):
    return lax.broadcasted_iota(jnp.int32, shape, len(shape) - 1) < HALF


def swap(value):
    return pltpu.roll(value, HALF, 1)


def wide(value):
    return value.astype(jnp.float32)


def join(first, second, parity):
    low = low_lanes(first.shape)
    if parity == 0:
        return jnp.where(low, first, swap(second))
    return jnp.where(low, swap(first), second)


def split(first, second):
    return join(first, second, 0), join(first, second, 1)


def bend_of(top):
    return jnp.where(top > TINY, BEND / jnp.maximum(top, TINY), 0.0)


def rounded_top(value):
    top = jnp.max(jnp.abs(value), axis=0, keepdims=True)
    return wide((top * (1.0 + 2.0**-7)).astype(jnp.bfloat16))


def sums_tops(tops, span, middle):
    low = low_lanes((1, LANES))
    last = jnp.where(low, tops[1], tops[2])
    return jnp.concatenate([tops[0]] * span + [tops[1]] * (middle - 1) + [last], axis=0)


def encode(value, bend):
    size = jnp.exp(SPREAD * jnp.log(1.0 + jnp.abs(value) * bend) + LOWEST)
    return jnp.where(value < 0.0, -size, size)


def decode(code, top):
    size = (jnp.exp((jnp.log(jnp.abs(code)) - LOWEST) * (1.0 / SPREAD)) - 1.0) * (top / BEND)
    return jnp.where(code < 0.0, -size, size)


def halves(value):
    coarse = value.astype(jnp.bfloat16)
    return coarse, (value - wide(coarse)).astype(jnp.bfloat16)


def apply_table(table, index, value):
    coarse, rest = halves(value)
    depth = coarse.shape[0]
    return jnp.dot(
        table[index],
        jnp.concatenate([coarse, coarse], axis=0),
        preferred_element_type=jnp.float32,
    ) + jnp.dot(table[index, :, :depth], rest, preferred_element_type=jnp.float32)


def layer_kernel(
    devices,
    projected_in,
    cotangent_in,
    filter_in,
    taps_in,
    gain_in,
    forward_in,
    inverse_in,
    recv_conv,
    recv_back,
    recv_sums,
    kept_out,
    taps_out,
    projected_ref,
    cotangent_ref,
    filter_ref,
    taps_ref,
    gain_ref,
    forward_ref,
    inverse_ref,
    send_first,
    recv_first,
    send_second,
    recv_second,
    send_filter,
    recv_filter,
    send_top,
    recv_top,
    send_rim,
    recv_rim,
    send_conv,
    send_back,
    send_sums,
    around,
    kept,
    first_rim,
    second_rim,
    first_short,
    signal,
    upstream,
    response,
    back,
    signal_spectra,
    product_spectra,
    load_sem,
    keep_sem,
    send_sem,
    recv_sem,
):
    hops = [(devices // 2 + (-1) ** i * ((i + 1) // 2)) for i in range(devices - 1)]
    arguments = (projected_in, cotangent_in, filter_in, taps_in, gain_in, forward_in, inverse_in)
    held = (
        projected_ref,
        cotangent_ref,
        filter_ref,
        taps_ref,
        gain_ref,
        forward_ref,
        inverse_ref,
    )
    loads = [
        pltpu.make_async_copy(source, target, load_sem.at[index])
        for index, (source, target) in enumerate(zip(arguments, held))
    ]
    for load in loads:
        load.start()
    rows, channels = cotangent_ref.shape
    tiles = channels // LANES
    span = taps_ref.shape[1]
    margin = span // 2
    width = rows // 2
    slabs = 2 * devices
    extent = rows * devices
    factor = 1.0 / math.sqrt(extent)
    me = lax.axis_index("seq")
    odd = lax.rem(me, 2) == 1

    def copy_to(kind, hop, source, target, peer):
        return pltpu.make_async_remote_copy(
            src_ref=source,
            dst_ref=target,
            send_sem=send_sem.at[kind, hop],
            recv_sem=recv_sem.at[kind, hop],
            device_id={"seq": peer},
            device_id_type=pl.DeviceIdType.MESH,
        )

    def peer_at(hop):
        return lax.rem(me + hop, devices)

    def source_at(hop):
        return lax.rem(me + devices - hop, devices)

    barrier = pltpu.get_barrier_semaphore()
    for hop in hops:
        pl.semaphore_signal(
            barrier, inc=1, device_id={"seq": peer_at(hop)}, device_id_type=pl.DeviceIdType.MESH
        )

    loads[0].wait()
    loads[1].wait()

    def lanes_of(peer):
        return pl.ds(pl.multiple_of((peer // 2) * LANES, LANES), LANES)

    def join_for(peer, first, second):
        flip = lax.rem(peer, 2) == 1
        return jnp.where(
            low_lanes(first.shape),
            jnp.where(flip, swap(first), first),
            jnp.where(flip, second, swap(second)),
        ).astype(jnp.bfloat16)

    def pack_first(peer, target):
        lanes = lanes_of(peer)
        target[...] = join_for(
            peer, wide(projected_ref[1, :, lanes]), wide(projected_ref[2, :, lanes])
        )

    def pack_second(peer, target):
        lanes = lanes_of(peer)
        target[...] = join_for(
            peer, wide(projected_ref[0, :, lanes]), wide(cotangent_ref[:, lanes])
        )

    for side, start in enumerate((0, rows - 2 * RIM)):
        part = slice(0, RIM) if side == 0 else slice(RIM, 2 * RIM)
        ends = [wide(projected_ref[s, start : start + 2 * RIM])[part] for s in range(3)]
        ends.append(wide(cotangent_ref[start : start + 2 * RIM])[part])
        for pair in range(2):
            send_rim[side, pair] = jnp.concatenate(ends[2 * pair : 2 * pair + 2], axis=0).astype(
                jnp.bfloat16
            )
    rim_copies = [
        copy_to(7, hop, send_rim.at[side], recv_rim.at[side], peer_at(hop))
        for side, hop in enumerate((devices - 1, 1))
    ]
    for place, hop in enumerate(hops):
        peer = peer_at(hop)
        pack_first(peer, send_first.at[peer])
        if place == 0:
            pl.semaphore_wait(barrier, devices - 1)
        copy_to(0, hop, send_first.at[peer], recv_first.at[me], peer).start()

    loads[2].wait()
    for tile in range(tiles):
        lanes = slice(tile * LANES, (tile + 1) * LANES)
        whole = filter_ref[:, lanes]
        top = jnp.max(jnp.abs(whole), axis=0, keepdims=True)
        coded = encode(whole, bend_of(top))
        for half in range(2):
            send_filter[2 * tile + half] = join(coded[:width], coded[width:], half).astype(
                jnp.bfloat16
            )
            send_top[2 * tile + half] = join(top, top, half)
    for hop in hops:
        peer = peer_at(hop)
        copy_to(2, hop, send_filter.at[peer], recv_filter.at[me], peer).start()
        copy_to(3, hop, send_top.at[peer], recv_top.at[me], peer).start()
    for hop in hops:
        peer = peer_at(hop)
        pack_second(peer, send_second.at[peer])
        copy_to(1, hop, send_second.at[peer], recv_second.at[me], peer).start()
    pack_first(me, recv_first.at[me])
    pack_second(me, recv_second.at[me])
    recv_filter[me] = send_filter[me]
    recv_top[me] = send_top[me]

    for load in loads[3:5]:
        load.wait()
    own = pl.ds(pl.multiple_of((me // 2) * LANES, LANES), LANES)

    def own_pair(first, second):
        return jnp.where(odd, join(first, second, 1), join(first, second, 0))

    gate_taps, left_taps, right_taps = [taps_ref[s, :, own] for s in range(3)]
    first_taps = own_pair(left_taps, right_taps)
    centre = wide(lax.broadcasted_iota(jnp.int32, (span, LANES), 0) == margin)
    second_taps = jnp.where(low_lanes((span, LANES)), own_pair(gate_taps, gate_taps), centre)
    own_gain = gain_ref[:, own]
    gain = own_pair(own_gain, own_gain)

    def wait_from(kind, source, target):
        for hop in hops:
            copy_to(
                kind, hop, source.at[peer_at(hop)], target.at[source_at(hop)], peer_at(hop)
            ).wait()

    def close_rim(rim):
        rim[0:RIM] = rim[extent : extent + RIM]
        rim[extent + RIM : extent + 2 * RIM] = rim[RIM : 2 * RIM]

    def open_rim(rim, received):
        for block in range(devices):
            rim[RIM + block * rows : RIM + (block + 1) * rows] = wide(received[block])
        close_rim(rim)

    def filtered(rim, taps, start):
        near = rim[pl.ds(start, width + 2 * RIM)]
        total = jnp.zeros((width, LANES), jnp.float32)
        for tap in range(span):
            low = RIM + tap - margin
            total = total + taps[tap : tap + 1] * near[low : low + width]
        return total

    wait_from(0, send_first, recv_first)
    open_rim(first_rim, recv_first)

    def shorten_first(slab, carry):
        start = pl.multiple_of(slab * width, width)
        total = filtered(first_rim, first_taps, start)
        first_short[pl.ds(start, width)] = total
        signal[pl.ds(start, width)] = total * swap(total)
        return carry

    lax.fori_loop(0, slabs, shorten_first, 0, unroll=2)
    for load in loads[5:]:
        load.wait()
    wait_from(2, send_filter, recv_filter)
    wait_from(3, send_top, recv_top)

    def put_spectrum(spectra, found, start, count):
        for index, (real_part, imaginary) in enumerate(found):
            if imaginary is None:
                imaginary = jnp.zeros_like(real_part)
            spectra[index, pl.ds(start, count)] = real_part
            spectra[index, pl.ds(width + start, count)] = imaginary

    def get_spectrum(spectra, start, count):
        found = []
        for index in range(slabs // 2 + 1):
            imaginary = None
            if 0 < index < slabs // 2:
                imaginary = spectra[index, pl.ds(width + start, count)]
            found.append((spectra[index, pl.ds(start, count)], imaginary))
        return found

    def first_spectrum(step, carry):
        start = pl.multiple_of(step * 16, 16)
        low = low_lanes((16, LANES))
        values = []
        for block in range(devices):
            found = decode(wide(recv_filter[block, pl.ds(start, 16)]), recv_top[block])
            for half in range(2):
                here = signal[pl.ds(block * rows + half * width + start, 16)]
                values.append(jnp.where(low, here, swap(found) if half == 0 else found))
        put_spectrum(signal_spectra, real_spectrum(values), start, 16)
        return carry

    lax.fori_loop(0, width // 16, first_spectrum, 0)

    for index in range(slabs // 2 + 1):
        found = apply_table(forward_ref, index, signal_spectra[index])
        signal_spectra[index] = found
        real_part, imaginary = found[:width], found[width:]
        other_real, other_imag = swap(real_part), swap(imaginary)
        product = jnp.concatenate(
            [
                real_part * other_real - imaginary * other_imag,
                real_part * other_imag + imaginary * other_real,
            ],
            axis=0,
        )
        product_spectra[index] = apply_table(inverse_ref, index, product)

    def first_back(step, top):
        start = pl.multiple_of(step * 8, 8)
        for slab, value in enumerate(real_values(get_spectrum(product_spectra, start, 8))):
            place = pl.ds(slab * width + start, 8)
            whole = value + gain * signal[place]
            response[place] = whole
            top = jnp.maximum(top, jnp.abs(whole))
        return top

    nothing = jnp.zeros((8, LANES), jnp.float32)
    top = lax.fori_loop(0, width // 8, first_back, nothing)
    response_top = rounded_top(top)
    response_bend = bend_of(response_top)

    def step_hop(step):
        return devices // 2 + (step + 1) // 2 * (1 - 2 * lax.rem(step, 2))

    def pack_conv(peer):
        start = pl.multiple_of(peer * rows, rows)
        folded = jnp.where(
            low_lanes((width, LANES)),
            response[pl.ds(start, width)],
            response[pl.ds(start + width, width)],
        )
        send_conv[peer] = encode(folded, response_bend).astype(jnp.bfloat16)

    def step_conv(step, carry):
        hop = step_hop(step)
        peer = peer_at(hop)
        pack_conv(peer)
        copy_to(4, hop, send_conv.at[peer], recv_conv.at[me], peer).start()
        return carry

    lax.fori_loop(0, devices - 1, step_conv, 0)
    pack_conv(me)
    for copy in rim_copies:
        copy.start()
    keeps = [
        pltpu.make_async_copy(source, target.at[me], keep_sem.at[index])
        for index, (source, target) in enumerate(
            (
                (send_conv.at[me], recv_conv),
                (send_back.at[me], recv_back),
                (send_sums, recv_sums),
            )
        )
    ]
    keeps[0].start()

    wait_from(1, send_second, recv_second)
    open_rim(second_rim, recv_second)

    def shorten_second(slab, carry):
        start = pl.multiple_of(slab * width, width)
        total = filtered(second_rim, second_taps, start)
        total = total * swap(total)
        upstream[pl.ds(start, width)] = total
        return carry + jnp.sum(
            (total * signal[pl.ds(start, width)]).reshape(-1, 8, LANES), axis=0
        )

    gain_sum = lax.fori_loop(0, slabs, shorten_second, nothing, unroll=2)

    def second_spectrum(step, carry):
        start = pl.multiple_of(step * 8, 8)
        values = [upstream[pl.ds(slab * width + start, 8)] for slab in range(slabs)]
        put_spectrum(product_spectra, real_spectrum(values), start, 8)
        return carry

    lax.fori_loop(0, width // 8, second_spectrum, 0, unroll=2)

    for index in range(slabs // 2 + 1):
        found = apply_table(forward_ref, index, product_spectra[index])
        real_part, imaginary = found[:width], found[width:]
        other_real = swap(signal_spectra[index, :width])
        other_imag = swap(signal_spectra[index, width:])
        product = jnp.concatenate(
            [
                real_part * other_real + imaginary * other_imag,
                imaginary * other_real - real_part * other_imag,
            ],
            axis=0,
        )
        product_spectra[index] = apply_table(inverse_ref, index, product)

    low_gain = jnp.where(low_lanes((1, LANES)), gain, 0.0)

    def second_back(step, top):
        start = pl.multiple_of(step * 8, 8)
        for slab, value in enumerate(real_values(get_spectrum(product_spectra, start, 8))):
            place = pl.ds(slab * width + start, 8)
            whole = value + low_gain * upstream[place]
            back[place] = whole
            top = jnp.maximum(top, jnp.abs(whole))
        return top

    top = lax.fori_loop(0, width // 8, second_back, nothing, unroll=2)
    back_top = rounded_top(top)
    back_bend = bend_of(back_top)
    rim_bend = jnp.where(low_lanes((1, LANES)), back_bend, response_bend)

    def pack_back(peer):
        start = pl.multiple_of(peer * rows, rows)
        send_back[peer, 0:rows] = encode(back[pl.ds(start, rows)], back_bend).astype(jnp.bfloat16)
        places = (
            lax.rem(start + extent - RIM, extent),
            lax.rem(start + rows, extent),
        )
        ends = []
        for place in places:
            here = pl.ds(pl.multiple_of(place, RIM), RIM)
            ends.append(jnp.where(low_lanes((RIM, LANES)), back[here], response[here]))
        send_back[peer, rows : rows + 2 * RIM] = encode(
            jnp.concatenate(ends, axis=0), rim_bend
        ).astype(jnp.bfloat16)

    def step_back(step, carry):
        hop = step_hop(step)
        peer = peer_at(hop)
        pack_back(peer)
        copy_to(5, hop, send_back.at[peer], recv_back.at[me], peer).start()
        return carry

    lax.fori_loop(0, devices - 1, step_back, 0)
    pack_back(me)
    keeps[1].start()

    def add_sums(slab, sums):
        sums = list(sums)
        start = pl.multiple_of(slab * width, width)
        here = pl.ds(start, width)
        low = low_lanes((width, LANES))
        grad = back[here]
        grad = jnp.where(low, grad, swap(grad)) * swap(first_short[here])
        near_first = first_rim[pl.ds(start, width + 2 * RIM)]
        near_second = second_rim[pl.ds(start, width + 2 * RIM)]
        other = response[here] * swap(near_second[RIM : RIM + width])
        for tap in range(span):
            inner = slice(RIM + tap - margin, RIM + tap - margin + width)
            for which, (grads, near) in enumerate(((grad, near_first), (other, near_second))):
                sums[which * span + tap] = sums[which * span + tap] + jnp.sum(
                    (grads * near[inner]).reshape(-1, 8, LANES), axis=0
                )
        return tuple(sums)

    sums = lax.fori_loop(0, slabs, add_sums, (nothing,) * (2 * span), unroll=2)
    sums = [factor * jnp.sum(value, axis=0, keepdims=True) for value in sums + (gain_sum,)]
    middle = (span + 1) // 2
    low = low_lanes((1, LANES))
    parts = sums[:span] + [join(sums[i], sums[i + middle], 0) for i in range(span, span + middle)]
    last = parts[-1]
    tops = [
        rounded_top(jnp.concatenate(parts[:span], axis=0)),
        rounded_top(jnp.concatenate(parts[span:-1] + [jnp.where(low, last, 0.0)], axis=0)),
        rounded_top(last),
    ]
    coded = encode(jnp.concatenate(parts, axis=0), bend_of(sums_tops(tops, span, middle)))
    send_sums[...] = jnp.concatenate([coded, *tops, response_top, back_top], axis=0).astype(
        jnp.bfloat16
    )
    for hop in hops:
        copy_to(6, hop, send_sums, recv_sums.at[me], peer_at(hop)).start()
    keeps[2].start()

    for copy in rim_copies:
        copy.wait()
    for stream in range(4):
        around[stream, 0:RIM] = jnp.zeros((RIM, channels), jnp.float32)
        around[stream, rows + 3 * RIM :] = jnp.zeros((RIM, channels), jnp.float32)
        half = slice((stream % 2) * RIM, (stream % 2 + 1) * RIM)
        before, after = wide(recv_rim[1, stream // 2])[half], wide(recv_rim[0, stream // 2])[half]
        around[stream, RIM : 2 * RIM] = before
        around[stream, rows + 2 * RIM : rows + 3 * RIM] = after
        source = cotangent_ref[...] if stream == 3 else projected_ref[stream]
        around[stream, 2 * RIM : 2 * RIM + rows] = wide(source)
    kept[3] = around[3, RIM : rows + 3 * RIM]

    def own_short(step, carry):
        stream, tile = step // tiles, lax.rem(step, tiles)
        lanes = pl.ds(pl.multiple_of(tile * LANES, LANES), LANES)
        taps = taps_ref[stream, :, lanes]
        for part in range(2):
            count = width + RIM
            total = jnp.zeros((count, LANES), jnp.float32)
            for tap in range(span):
                low = part * count + RIM + tap - margin
                total = total + taps[tap : tap + 1] * around[stream, low : low + count, lanes]
            kept[stream, part * count : (part + 1) * count, lanes] = total
        return carry

    lax.fori_loop(0, 3 * tiles, own_short, 0)
    keeping = pltpu.make_async_copy(kept, kept_out, keep_sem.at[3])
    keeping.start()
    passing = pltpu.make_async_copy(taps_ref, taps_out, keep_sem.at[4])
    passing.start()

    keeping.wait()
    passing.wait()
    for keep in keeps:
        keep.wait()
    wait_from(4, send_conv, recv_conv)
    wait_from(5, send_back, recv_back)
    for hop in hops:
        copy_to(6, hop, send_sums, recv_sums.at[source_at(hop)], peer_at(hop)).wait()


def unpack_kernel(*refs):
    held, results, refs = refs[:5], refs[5:10], refs[10:]
    output_ref, streams_ref, filter_grad_ref, taps_grad_ref, gain_grad_ref = refs[:5]
    recv_conv, recv_back, recv_sums, kept, taps_ref = held
    response, grad, grads, store_sem = refs[5:]
    tiles = recv_conv.shape[0] // 2
    rows = output_ref.shape[0]
    span = taps_grad_ref.shape[1]
    margin = span // 2
    middle = (span + 1) // 2
    stores = [
        pltpu.make_async_copy(refs[i], results[i], store_sem.at[i]) for i in (0, 2, 3, 4)
    ]
    streams = [
        pltpu.make_async_copy(streams_ref.at[i], results[1].at[i], store_sem.at[5 + i])
        for i in range(3)
    ]
    main = slice(RIM, RIM + rows)
    ends = (slice(0, RIM), slice(RIM + rows, rows + 2 * RIM))
    for tile in range(tiles):
        lanes = slice(tile * LANES, (tile + 1) * LANES)
        low = low_lanes((1, LANES))
        tops = [wide(recv_sums[2 * tile + half]) for half in range(2)]
        response_top, back_top = [
            [top[span + middle + i : span + middle + i + 1] for top in tops] for i in (3, 4)
        ]
        found = [decode(wide(recv_back[2 * tile + i, 0:rows]), back_top[i]) for i in range(2)]
        grad[main, lanes], filter_grad_ref[:, lanes] = split(*found)
        rims = [
            decode(
                wide(recv_back[2 * tile + i, rows : rows + 2 * RIM]),
                jnp.where(low, back_top[i], response_top[i]),
            )
            for i in range(2)
        ]
        for target, rim in zip((grad, response), split(*rims)):
            for index, place in enumerate(ends):
                target[place, lanes] = rim[index * RIM : (index + 1) * RIM]
    stores[1].start()
    for tile in range(tiles):
        lanes = slice(tile * LANES, (tile + 1) * LANES)
        tops = [wide(recv_sums[2 * tile + half]) for half in range(2)]
        count = span + middle
        low_part, high_part = split(
            *(
                decode(
                    top[:count],
                    sums_tops([top[count + i : count + i + 1] for i in range(3)], span, middle),
                )
                for top in tops
            )
        )
        taps_grad_ref[1, :, lanes] = low_part[0:span]
        taps_grad_ref[2, :, lanes] = high_part[0:span]
        taps_grad_ref[0, :middle, lanes] = low_part[span : span + middle]
        taps_grad_ref[0, middle:, lanes] = high_part[span : 2 * span - middle]
        gain_grad_ref[:, lanes] = high_part[2 * span - middle : 2 * span - middle + 1]
        pieces = split(
            *(
                decode(
                    wide(recv_conv[2 * tile + i]), tops[i][count + 3 : count + 4]
                )
                for i in range(2)
            )
        )
        whole = jnp.concatenate(pieces, axis=0)
        response[main, lanes] = whole
        output_ref[:, lanes] = (whole * kept[0, main, lanes]).astype(jnp.bfloat16)
    for index in (0, 2, 3):
        stores[index].start()
    for stream, (value, other) in enumerate(((response, 3), (grad, 2), (grad, 1))):
        for tile in range(tiles):
            lanes = slice(tile * LANES, (tile + 1) * LANES)
            grads[stream, tile] = value[:, lanes] * kept[other, :, lanes]
            taps = taps_ref[stream, :, lanes]
            total = jnp.zeros((rows, LANES), jnp.float32)
            for tap in range(span):
                first = RIM + margin - tap
                total = total + taps[tap : tap + 1] * grads[stream, tile, first : first + rows]
            streams_ref[stream, :, lanes] = total.astype(jnp.bfloat16)
        streams[stream].start()
    for store in stores + streams:
        store.wait()


def halved(table):
    coarse = table.astype(ml_dtypes.bfloat16)
    rest = (table - coarse.astype(np.float32)).astype(ml_dtypes.bfloat16)
    return np.concatenate([coarse, rest], axis=2)


def packed_body(devices, projected, long_filter, short_kernel, skip_gain, cotangent):
    rows, channels = long_filter.shape
    span = short_kernel.shape[1]
    extent = rows * devices
    slabs = 2 * devices
    width = rows // 2
    tables = [halved(table) for table in fine_tables(slabs, width)]
    sums_rows = span + (span + 1) // 2 + 5
    block = (devices, rows, LANES)
    half_block = (devices, width, LANES)
    longer = (devices, rows + 2 * RIM, LANES)
    narrow, full = jnp.bfloat16, jnp.float32
    arguments = (projected, cotangent, long_filter, short_kernel, skip_gain[None], *tables)
    in_hbm = pl.BlockSpec(memory_space=pltpu.HBM)
    anywhere = pl.BlockSpec(memory_space=pl.ANY)
    arguments = [pltpu.with_memory_space_constraint(value, pltpu.HBM) for value in arguments]
    packed_shapes = (
        jax.ShapeDtypeStruct(half_block, narrow),
        jax.ShapeDtypeStruct(longer, narrow),
        jax.ShapeDtypeStruct((devices, sums_rows, LANES), narrow),
        jax.ShapeDtypeStruct((4, rows + 2 * RIM, channels), full),
        jax.ShapeDtypeStruct(short_kernel.shape, full),
    )
    out_shapes = (
        jax.ShapeDtypeStruct((rows, channels), narrow),
        jax.ShapeDtypeStruct((3, rows, channels), narrow),
        jax.ShapeDtypeStruct((rows, channels), full),
        jax.ShapeDtypeStruct(short_kernel.shape, full),
        jax.ShapeDtypeStruct((1, channels), full),
    )
    packed = pl.pallas_call(
        functools.partial(layer_kernel, devices),
        out_shape=packed_shapes,
        in_specs=[in_hbm] * 7,
        out_specs=(anywhere,) * 5,
        scratch_shapes=[
            *(pltpu.VMEM(value.shape, value.dtype) for value in arguments),
            pltpu.VMEM(block, narrow),
            pltpu.VMEM(block, narrow),
            pltpu.VMEM(block, narrow),
            pltpu.VMEM(block, narrow),
            pltpu.VMEM(half_block, narrow),
            pltpu.VMEM(half_block, narrow),
            pltpu.VMEM((devices, 1, LANES), full),
            pltpu.VMEM((devices, 1, LANES), full),
            pltpu.VMEM((2, 2, 2 * RIM, channels), narrow),
            pltpu.VMEM((2, 2, 2 * RIM, channels), narrow),
            pltpu.VMEM(half_block, narrow),
            pltpu.VMEM(longer, narrow),
            pltpu.VMEM((sums_rows, LANES), narrow),
            pltpu.VMEM((4, rows + 4 * RIM, channels), full),
            pltpu.VMEM((4, rows + 2 * RIM, channels), full),
            pltpu.VMEM((extent + 2 * RIM, LANES), full),
            pltpu.VMEM((extent + 2 * RIM, LANES), full),
            *[pltpu.VMEM((extent, LANES), full)] * 5,
            *[pltpu.VMEM((slabs // 2 + 1, rows, LANES), full)] * 2,
            pltpu.SemaphoreType.DMA((len(arguments),)),
            pltpu.SemaphoreType.DMA((5,)),
            pltpu.SemaphoreType.DMA((8, devices)),
            pltpu.SemaphoreType.DMA((8, devices)),
        ],
        compiler_params=pltpu.CompilerParams(
            collective_id=0, has_side_effects=True, vmem_limit_bytes=LIMIT
        ),
    )(*arguments)
    found = pl.pallas_call(
        unpack_kernel,
        out_shape=out_shapes,
        in_specs=[pl.BlockSpec(memory_space=pltpu.VMEM)] * 5,
        out_specs=(in_hbm,) * 5,
        scratch_shapes=[
            *(pltpu.VMEM(value.shape, value.dtype) for value in out_shapes),
            *[pltpu.VMEM((rows + 2 * RIM, channels), full)] * 2,
            pltpu.VMEM((3, channels // LANES, rows + 2 * RIM, LANES), full),
            pltpu.SemaphoreType.DMA((8,)),
        ],
        compiler_params=pltpu.CompilerParams(vmem_limit_bytes=LIMIT),
    )(*packed)
    return (*found[:4], found[4][0])


def with_halo(block, sides, width):
    for axis, dim in sides:
        count = lax.axis_size(axis)
        forward = [(i, i + 1) for i in range(count - 1)]
        forward.append((count - 1, 0))
        backward = [(target, source) for source, target in forward]
        low = lax.ppermute(
            lax.slice_in_dim(block, block.shape[dim] - width, None, axis=dim), axis, forward
        )
        high = lax.ppermute(lax.slice_in_dim(block, 0, width, axis=dim), axis, backward)
        block = jnp.concatenate([low, block, high], axis=dim)
    return block


def dft_tables(extent):
    indices = jnp.arange(extent, dtype=jnp.int32)
    angles = (indices[:, None] * indices[None, :] % extent).astype(jnp.float32) * (
        2.0 * math.pi / extent
    )
    return (jnp.cos(angles), jnp.sin(angles))


def apply_along(matrix, signal, axis_dim):
    letters = "wxyz"
    target = letters[:axis_dim] + "k" + letters[axis_dim + 1 :]
    return jnp.einsum(
        "k" + letters[axis_dim] + "," + letters + "->" + target, matrix, signal, precision=HIGHEST
    )


def forward_section(real_part, imaginary, axis_dim):
    cosine, sine_table = dft_tables(real_part.shape[axis_dim])
    out_real = apply_along(cosine, real_part, axis_dim)
    out_imag = -apply_along(sine_table, real_part, axis_dim)
    if imaginary is not None:
        out_real = out_real + apply_along(sine_table, imaginary, axis_dim)
        out_imag = out_imag + apply_along(cosine, imaginary, axis_dim)
    return (out_real, out_imag)


def inverse_section(real_part, imaginary, axis_dim, keep_imag):
    cosine, sine_table = dft_tables(real_part.shape[axis_dim])
    out_real = apply_along(cosine, real_part, axis_dim) - apply_along(
        sine_table, imaginary, axis_dim
    )
    if keep_imag:
        return (
            out_real,
            apply_along(sine_table, real_part, axis_dim) + apply_along(cosine, imaginary, axis_dim),
        )
    return (out_real, None)


def twist(real_part, imaginary, angles, sign_factor):
    cosine = jnp.cos(angles)
    sine_table = jnp.sin(angles)
    return (
        real_part * cosine + sign_factor * imaginary * sine_table,
        imaginary * cosine - sign_factor * real_part * sine_table,
    )


def twiddle(low_index, high_index, extent):
    return (low_index * high_index % extent).astype(jnp.float32) * (2.0 * math.pi / extent)


def block_angles(devices, portion, extent):
    low_index = jnp.arange(devices, dtype=jnp.int32)[None, :, None, None]
    high_index = (lax.axis_index("seq") * portion + jnp.arange(portion, dtype=jnp.int32))[
        None, None, :, None
    ]
    return twiddle(low_index, high_index, extent)


def sequence_forward(signals, extent):
    devices = lax.axis_size("seq")
    portion = signals.shape[1] // devices
    columns = lax.all_to_all(signals[:, None], "seq", split_axis=2, concat_axis=1, tiled=True)
    real_part, imaginary = forward_section(columns, None, 1)
    real_part, imaginary = twist(real_part, imaginary, block_angles(devices, portion, extent), 1.0)
    spread = (
        lax.all_to_all(real_part, "seq", split_axis=1, concat_axis=2, tiled=True),
        lax.all_to_all(imaginary, "seq", split_axis=1, concat_axis=2, tiled=True),
    )
    return forward_section(spread[0], spread[1], 2)


def sequence_inverse(real_part, imaginary, extent):
    devices = lax.axis_size("seq")
    portion = real_part.shape[2] // devices
    real_part, imaginary = inverse_section(real_part, imaginary, 2, True)
    gathered = (
        lax.all_to_all(real_part, "seq", split_axis=2, concat_axis=1, tiled=True),
        lax.all_to_all(imaginary, "seq", split_axis=2, concat_axis=1, tiled=True),
    )
    real_part, imaginary = twist(
        gathered[0], gathered[1], block_angles(devices, portion, extent), -1.0
    )
    pieces = inverse_section(real_part, imaginary, 1, False)[0] * (1.0 / extent)
    blocks = lax.all_to_all(pieces, "seq", split_axis=1, concat_axis=2, tiled=True)
    return blocks[:, 0]


def body(projected, long_filter, short_kernel, skip_gain, cotangent):
    rows_here = projected.shape[1]
    extent = rows_here * lax.axis_size("seq")
    factor = 1.0 / math.sqrt(extent)
    kernel_span = short_kernel.shape[1]
    margin = kernel_span // 2
    padded = with_halo(projected, (("seq", 1),), margin)
    shorts = jnp.zeros(projected.shape, jnp.float32)
    for offset in range(kernel_span):
        shorts = shorts + short_kernel[:, offset][:, None, :] * padded[
            :, offset : offset + rows_here
        ].astype(jnp.float32)
    gated_signal = shorts[1] * shorts[2]
    transform, restore = (sequence_forward, sequence_inverse)
    upstream = cotangent.astype(jnp.float32)
    grad_response = upstream * shorts[0]
    spec_real, spec_imag = transform(jnp.stack([gated_signal, long_filter]), extent)
    gated_real, gated_imag = (spec_real[0], spec_imag[0])
    filter_real, filter_imag = (spec_real[1] * factor, spec_imag[1] * factor)
    product_real = filter_real * gated_real - filter_imag * gated_imag
    product_imag = filter_real * gated_imag + filter_imag * gated_real
    convolved = restore(product_real[None], product_imag[None], extent)[0]
    upstream_real, upstream_imag = transform(grad_response[None], extent)
    upstream_real, upstream_imag = (upstream_real[0], upstream_imag[0])
    back_real = jnp.stack(
        [
            filter_real * upstream_real + filter_imag * upstream_imag,
            gated_real * upstream_real + gated_imag * upstream_imag,
        ]
    )
    back_imag = jnp.stack(
        [
            filter_real * upstream_imag - filter_imag * upstream_real,
            gated_real * upstream_imag - gated_imag * upstream_real,
        ]
    )
    restored = restore(back_real, back_imag, extent)
    grad_gated = restored[0] + skip_gain * grad_response
    filter_grad = restored[1] * factor
    response = convolved + skip_gain * gated_signal
    layer_output = (response * shorts[0]).astype(jnp.bfloat16)
    grad_shorts = jnp.stack([upstream * response, grad_gated * shorts[2], grad_gated * shorts[1]])
    rimmed = with_halo(grad_shorts, (("seq", 1),), margin)
    stream_sum = jnp.zeros(grad_shorts.shape, jnp.float32)
    kernel_terms = []
    for offset in range(kernel_span):
        start_row = 2 * margin - offset
        stream_sum = (
            stream_sum
            + short_kernel[:, offset][:, None, :] * rimmed[:, start_row : start_row + rows_here]
        )
        kernel_terms.append(
            jnp.sum(
                grad_shorts * padded[:, offset : offset + rows_here].astype(jnp.float32), axis=1
            )
        )
    kernel_part = jnp.stack(kernel_terms, axis=1)
    skip_part = jnp.sum(grad_response * gated_signal, axis=0)
    kernel_total, skip_total = lax.psum((kernel_part, skip_part), "seq")
    return (
        layer_output,
        stream_sum.astype(jnp.bfloat16),
        filter_grad,
        kernel_total * factor,
        skip_total * factor,
    )


def solution(mesh):
    placed = (
        P(None, ("groups", "seq"), "chan"),
        P(("groups", "seq"), "chan"),
        P(None, None, "chan"),
        P("chan"),
        P(("groups", "seq"), "chan"),
    )
    devices = mesh.shape["seq"]

    def run(projected, *others):
        rows, channels = projected.shape[1:]
        if channels == HALF * devices and rows == LANES and devices & (devices - 1) == 0:
            return packed_body(devices, projected, *others)
        return body(projected, *others)

    return jax.shard_map(
        run,
        mesh=mesh,
        in_specs=placed,
        out_specs=(
            P(("groups", "seq"), "chan"),
            P(None, ("groups", "seq"), "chan"),
            P(("groups", "seq"), "chan"),
            P("groups", None, "chan"),
            P(("groups", "chan")),
        ),
        check_vma=False,
    )
```
